128 devices in a mesh: det: 8 (over y, core), tm: 16 (over z, x).
Axes of the slice: x: 4, y: 4, z: 4, core: 2. Of those that a mesh axis runs over, the one named last changes fastest.
Arguments:
- timestreams: float32 [256, 65536], P('det', 'tm')
- templates: float32 [256, 32], P('det')
- validity: int32 [256], P('det'), may hold values 0 or 1
- tile_index: int32 [256, 512], P('det', 'tm'), may hold values from 0 to 15, as said below
- row_offset: int32 [256, 512], P('det', 'tm'), may hold values from 0 to 63
- col_start: int32 [256, 512], P('det', 'tm'), may hold values from 0 to 127
Outputs:
- cleaned: float32 [256, 65536], P('det', 'tm')
- beamed: float32 [64, 2048], P('det', 'tm')
The draws below stay inside these ranges and needn't reach their ends.
Inputs may be any that keep to these rules, and one draw needn't show every extreme that they name: `tile_index`: any run may name any tile.
All inputs are finite; a program needn't handle non-finite values. No bound on the sum of `validity` on one device may be relied on, other than what follows from the above.
Results may differ from the reference program's by a relative error of at most 0.00011.
Values sent between devices are 32-bit elements; how exact they have to be, the bound alone decides.
No kernel may reach another device: no remote copies, remote signals or barrier semaphores. Data moves between devices by JAX's collectives and lax.ppermute only.
A program may use at most 64 MiB of HBM per device.

```python
import math
import jax
import jax.numpy as jnp
from jax import lax

SEG = 4096
NMODE = 32
FKEEP = 128
RUN = 128
TROWS = 64
TCOLS = 128
RADIUS = 3
NDET = 256
NSAMP = 65536
NRUN = 512
NTILE = 16


def template_table(key):
    return jax.random.normal(jax.random.fold_in(key, 101), (NDET, NMODE), jnp.float32) * NDET ** (-0.5)


def draw_templates(key, part):
    return template_table(key)


def draw_timestreams(key, part):
    table = template_table(key)
    freqs = jax.random.randint(jax.random.fold_in(key, 102), (NMODE, 3, 1), 1, FKEEP)
    phases = jax.random.uniform(jax.random.fold_in(key, 103), (NMODE, 3, 1), jnp.float32, -math.pi, math.pi)
    strength = 3.0 * jax.random.normal(jax.random.fold_in(key, 104), (NMODE, 3, 1), jnp.float32)
    sample_pos = (jnp.arange(NSAMP, dtype=jnp.int32) % SEG)[None, None, :]
    angle = 2.0 * math.pi * (freqs * sample_pos % SEG).astype(jnp.float32) / SEG + phases
    drifts = jnp.sum(strength * jnp.cos(angle), axis=1)
    common = jnp.dot(table, drifts, precision=lax.Precision.HIGHEST)
    noise = jax.random.normal(jax.random.fold_in(key, 106), (NDET, NSAMP), jnp.float32)
    return (noise + common).astype(jnp.float32)


def draw_tile_index(key, part):
    first = jax.random.randint(jax.random.fold_in(key, 201), (NDET, NRUN), 0, NTILE)
    second = jax.random.randint(jax.random.fold_in(key, 202), (NDET, NRUN), 0, NTILE)
    return jnp.minimum(first, second).astype(jnp.int32)


def plant(entries, key, smallest, top_value):
    spot = [jax.random.randint(jax.random.fold_in(key, axis), (), 0, length) for axis, length in enumerate(entries.shape)]
    widest = entries.shape.index(max(entries.shape))
    neighbour = spot[:widest] + [(spot[widest] + 1) % entries.shape[widest]] + spot[widest + 1:]
    return entries.at[tuple(spot)].set(smallest).at[tuple(neighbour)].set(top_value)


def setup_inputs(seed: int = 0) -> dict:
    key_of = jax.random.split(jax.random.key(seed), 7)
    timestreams = draw_timestreams(jax.random.fold_in(key_of[6], 71), 0)
    templates = draw_templates(jax.random.fold_in(key_of[6], 71), 0)
    validity = plant((jax.random.randint(key_of[2], (NDET,), 0, 8) < 7).astype(jnp.int32), jax.random.fold_in(key_of[2], 1), 0, 1)
    tile_index = draw_tile_index(jax.random.fold_in(key_of[6], 71), 0)
    row_offset = plant(jax.random.randint(key_of[4], (NDET, NRUN), 0, TROWS), jax.random.fold_in(key_of[4], 1), 0, TROWS - 1).astype(jnp.int32)
    col_start = plant(jax.random.randint(key_of[5], (NDET, NRUN), 0, TCOLS), jax.random.fold_in(key_of[5], 1), 0, TCOLS - 1).astype(jnp.int32)
    return {"timestreams": timestreams, "templates": templates, "validity": validity, "tile_index": tile_index, "row_offset": row_offset, "col_start": col_start}


def beam_taps():
    values = [math.exp(-(m * m) / 4.5) for m in range(-RADIUS, RADIUS + 1)]
    total = sum(values)
    return [v / total for v in values]

def reference(timestreams, templates, validity, tile_index, row_offset, col_start):
    hp = lax.Precision.HIGHEST
    weight = validity.astype(jnp.float32)
    mode_gram = jnp.dot(templates.T, templates * weight[:, None], precision=hp)
    mode_gram = mode_gram + 0.05 * jnp.eye(NMODE, dtype=jnp.float32)
    projected = jnp.dot(templates.T, timestreams * weight[:, None], precision=hp)
    factor = jnp.linalg.cholesky(mode_gram)
    amplitude = jax.scipy.linalg.cho_solve((factor, True), projected)
    blocks = amplitude.reshape(NMODE, NSAMP // SEG, SEG)
    spectra = jnp.fft.rfft(blocks, axis=-1)
    keep = (jnp.arange(SEG // 2 + 1) < FKEEP).astype(jnp.float32)
    lowpass = jnp.fft.irfft(spectra * keep, n=SEG, axis=-1).astype(jnp.float32).reshape(NMODE, NSAMP)
    cleaned = weight[:, None] * (timestreams - jnp.dot(templates, lowpass, precision=hp))
    offsets = jnp.arange(RUN, dtype=jnp.int32)
    column = tile_index[:, :, None] * TCOLS + (col_start[:, :, None] + offsets) % TCOLS
    flat_index = (row_offset[:, :, None] * (NTILE * TCOLS) + column).astype(jnp.int32)
    cells = TROWS * NTILE * TCOLS
    binsum = jax.ops.segment_sum(cleaned.reshape(-1), flat_index.reshape(-1), num_segments=cells)
    hit_values = jnp.broadcast_to(weight[:, None, None], flat_index.shape).reshape(-1)
    hits = jax.ops.segment_sum(hit_values, flat_index.reshape(-1), num_segments=cells)
    binned = (binsum / (hits + 1.0)).reshape(TROWS, NTILE * TCOLS)
    taps = beam_taps()
    padded = jnp.pad(binned, RADIUS)
    smoothed = jnp.zeros((TROWS, padded.shape[1]), jnp.float32)
    for shift_pos in range(2 * RADIUS + 1):
        smoothed = smoothed + taps[shift_pos] * padded[shift_pos:shift_pos + TROWS, :]
    beamed = jnp.zeros((TROWS, NTILE * TCOLS), jnp.float32)
    for shift_pos in range(2 * RADIUS + 1):
        beamed = beamed + taps[shift_pos] * smoothed[:, shift_pos:shift_pos + NTILE * TCOLS]
    return (cleaned, beamed)
```

```python
import math

import jax
import jax.numpy as jnp
import numpy as np
from jax import lax
from jax.experimental import pallas as pl
from jax.experimental.pallas import tpu as pltpu
from jax.sharding import Mesh
from jax.sharding import PartitionSpec as P
import ml_dtypes

SEG = 4096
NMODE = 32
FKEEP = 128
RUN = 128
TROWS = 64
TCOLS = 128
RADIUS = 3
DETS = 32
CHUNK = 256
NCHUNK = SEG // CHUNK
NRUNS = DETS * SEG // RUN
NT = 16
NY = 4
OWN = 8
BROWS = 16
NBLK = NY * NT
ZROWS = (TROWS // OWN + 1) * NT
BF = jnp.bfloat16
F32 = jnp.float32


def split_np(a):
    hi = a.astype(np.float32).astype(ml_dtypes.bfloat16)
    lo = (a - hi.astype(np.float64)).astype(np.float32).astype(ml_dtypes.bfloat16)
    return hi, lo


def tables():
    j = np.arange(CHUNK)[:, None]
    k = np.arange(FKEEP)[None, :]
    phi = 2.0 * np.pi * (j * k % SEG) / SEG
    basis = np.concatenate([np.cos(phi), np.sin(phi)], axis=1)
    c = np.arange(NCHUNK)[:, None]
    theta = 2.0 * np.pi * (c * CHUNK * k % SEG) / SEG
    twiddle = np.concatenate([np.cos(theta), np.sin(theta)], axis=1).astype(np.float32)
    scale = np.where(np.arange(FKEEP) == 0, 1.0 / SEG, 2.0 / SEG)
    synth = basis.T * np.concatenate([scale, scale])[:, None]
    return split_np(basis), split_np(synth), twiddle


def beam_taps():
    values = [math.exp(-(m * m) / 4.5) for m in range(-RADIUS, RADIUS + 1)]
    total = sum(values)
    return [v / total for v in values]


def split(a):
    hi = a.astype(BF)
    return hi, (a - hi.astype(F32)).astype(BF)


def mm(a, b):
    return jnp.dot(a, b, preferred_element_type=F32)


def mm0(a, b):
    return lax.dot_general(
        a, b, (((0,), (0,)), ((), ())), precision=lax.Precision.HIGHEST,
        preferred_element_type=F32,
    )


def column(row, n):
    full = jnp.broadcast_to(row, (n, row.shape[1]))
    same = lax.broadcasted_iota(jnp.int32, full.shape, 0) == lax.broadcasted_iota(
        jnp.int32, full.shape, 1
    )
    return jnp.sum(jnp.where(same, full, 0.0), axis=1, keepdims=True)


def analysis_kernel(x_ref, t_ref, v_ref, eh_ref, el_ref, tw_ref, out_ref):
    w = column(v_ref[...].astype(F32), DETS)
    x = jnp.concatenate(
        [x_ref[:, c * CHUNK : (c + 1) * CHUNK] for c in range(NCHUNK)], axis=0
    )
    hi, lo = split(x)
    y = mm(hi, eh_ref[...]) + mm(lo, eh_ref[...]) + mm(hi, el_ref[...])
    re = jnp.zeros((DETS, FKEEP), F32)
    im = jnp.zeros((DETS, FKEEP), F32)
    for c in range(NCHUNK):
        yc = y[c * DETS : (c + 1) * DETS, :FKEEP]
        ys = y[c * DETS : (c + 1) * DETS, FKEEP:]
        cos = tw_ref[c : c + 1, :FKEEP]
        sin = tw_ref[c : c + 1, FKEEP:]
        re = re + (cos * yc - sin * ys)
        im = im + (sin * yc + cos * ys)
    t = t_ref[...]
    wt = t * w
    out_ref[:, 0:FKEEP] = mm0(wt, re)
    out_ref[:, FKEEP : 2 * FKEEP] = mm0(wt, im)
    gram = mm0(wt, t)
    out_ref[:, 2 * FKEEP :] = jnp.concatenate(
        [gram, jnp.zeros((NMODE, FKEEP - NMODE), F32)], axis=1
    )


def edge_col(lane):
    slot = lane >> 3
    return jnp.where(slot < 3, TCOLS - RADIUS + slot, slot - 3)


def index_kernel(
    core_ref, line_ref, zid_ref, cs_ref, ro_ref, v_ref,
    send_ref, keep_ref, zhot_ref, idx_ref, edge_ref, mask_ref, zh_ref,
):
    line = line_ref[...]
    for which, ref in ((1, send_ref), (0, keep_ref)):
        core = core_ref[0] ^ which
        l = lax.broadcasted_iota(jnp.int32, (NBLK * BROWS, 128), 0)
        i = l & (BROWS - 1)
        b = l >> 4
        row = (b >> 4) * (2 * OWN) + core * OWN - RADIUS + i
        ok = (i < OWN + 2 * RADIUS) & (row >= 0) & (row < TROWS)
        ident = jnp.where(ok, (b & (NT - 1)) * TROWS + row, -1)
        for q in range(NRUNS // 128):
            hot = ident == line[:, q * 128 : (q + 1) * 128]
            ref[:, q * 128 : (q + 1) * 128] = jnp.where(hot, 1.0, 0.0).astype(BF)
    zl = lax.broadcasted_iota(jnp.int32, (ZROWS, NRUNS), 0)
    zhot = jnp.where(zl == zid_ref[...], 1.0, 0.0).astype(BF)
    zhot_ref[...] = zhot
    w = column(v_ref[...].astype(F32), DETS)
    lane = lax.broadcasted_iota(jnp.int32, (DETS, 128), 1)
    ecol = edge_col(lane)
    hparts = []
    for c in range(SEG // RUN):
        sl = slice(c * DETS, (c + 1) * DETS)
        cs = jnp.broadcast_to(cs_ref[:, c : c + 1], (DETS, 128))
        ro = jnp.broadcast_to(ro_ref[:, c : c + 1], (DETS, 128))
        idx_ref[sl, :] = (lane - cs) & (TCOLS - 1)
        edge_ref[sl, :] = (ecol - cs) & (TCOLS - 1)
        here = ((ro + RADIUS) & (OWN - 1)) == (lane & (OWN - 1))
        mask_ref[sl, :] = jnp.where(here & (lane < 48), 1.0, 0.0)
        hparts.append(jnp.where(here & (lane >= 48) & (lane < 56), w, 0.0).astype(BF))
    zh_ref[...] = mm(zhot, jnp.concatenate(hparts, axis=0))


def solve(gram, rhs):
    n = gram.shape[0]
    a = jnp.concatenate([gram, rhs], axis=1)
    rows = lax.broadcasted_iota(jnp.int32, a.shape, 0)
    for k in range(n):
        pivot = a[k : k + 1, :]
        pivot = pivot / a[k : k + 1, k : k + 1]
        a = jnp.where(rows == k, pivot, a - a[:, k : k + 1] * pivot)
    return a[:, n:]


def shifted_tiles(z, by):
    zero = jnp.zeros((z.shape[0], 1, 128), F32)
    if by < 0:
        return jnp.concatenate([zero, z[:, :-1]], axis=1)
    return jnp.concatenate([z[:, 1:], zero], axis=1)


def clean_kernel(
    core_ref, p_ref, q_ref, t_ref, v_ref, x_ref, sh_ref, sl_ref, tw_ref,
    idx_ref, edge_ref, mask_ref, zhot_ref, zh_ref, send_hot_ref,
    clean_ref, send_ref, vals_ref, rows_ref,
):
    w = column(v_ref[...].astype(F32), DETS)
    p = p_ref[...] + q_ref[...]
    eye = lax.broadcasted_iota(jnp.int32, (NMODE, NMODE), 0) == lax.broadcasted_iota(
        jnp.int32, (NMODE, NMODE), 1
    )
    gram = p[:, 2 * FKEEP : 2 * FKEEP + NMODE] + jnp.where(eye, 0.05, 0.0)
    coef = solve(gram, t_ref[...].T)
    a = mm0(coef, p[:, :FKEEP])
    b = mm0(coef, p[:, FKEEP : 2 * FKEEP])
    parts = []
    for c in range(NCHUNK):
        cos = tw_ref[c : c + 1, :FKEEP]
        sin = tw_ref[c : c + 1, FKEEP:]
        parts.append(jnp.concatenate([a * cos + b * sin, b * cos - a * sin], axis=1))
    hi, lo = split(jnp.concatenate(parts, axis=0))
    low = mm(hi, sh_ref[...]) + mm(lo, sh_ref[...]) + mm(hi, sl_ref[...])
    runs = []
    for c in range(NCHUNK):
        part = w * (x_ref[:, c * CHUNK : (c + 1) * CHUNK] - low[c * DETS : (c + 1) * DETS, :])
        clean_ref[:, c * CHUNK : (c + 1) * CHUNK] = part
        runs.append(part[:, :RUN])
        runs.append(part[:, RUN:])
    run = jnp.concatenate(runs, axis=0)
    vals = jnp.concatenate(
        split(jnp.take_along_axis(run, idx_ref[...], axis=1, mode="promise_in_bounds")), axis=1
    )
    vals_ref[...] = vals
    evals = jnp.take_along_axis(run, edge_ref[...], axis=1, mode="promise_in_bounds")
    evals = jnp.concatenate(split(evals * mask_ref[...]), axis=1)
    z = mm(zhot_ref[...], evals)
    z = (z[:, :128] + z[:, 128:] + zh_ref[...]).reshape(ZROWS // NT, NT, 128)
    left = shifted_tiles(z, -1)
    right = shifted_tiles(z, 1)
    lane = lax.broadcasted_iota(jnp.int32, z.shape, 2)
    left_hits = left
    right_hits = jnp.concatenate([jnp.zeros(z.shape[:2] + (8,), F32), right[:, :, :-8]], axis=2)
    near = jnp.where(
        lane < 24, left, jnp.where(lane < 48, right, jnp.where(lane < 56, left_hits, right_hits))
    )
    near = jnp.where(lane < 64, near, 0.0)
    mine = jnp.where((lane >= 48) & (lane < 56), z, 0.0)
    nd = TROWS // OWN

    def both(v):
        return v[:nd] + jnp.concatenate([jnp.zeros((nd, NT, 64), F32), v[1:, :, :64]], axis=2)

    rows14 = both(near)
    rows15 = both(mine)
    core = core_ref[0]

    def pick(v, which):
        return jnp.concatenate(
            [jnp.where(which == 1, v[2 * y + 1], v[2 * y]) for y in range(NY)], axis=0
        )

    rows_ref[0:NBLK, :] = pick(rows14, core)
    rows_ref[NBLK : 2 * NBLK, :] = pick(rows15, core)
    s = mm(send_hot_ref[...], vals)
    send_ref[...] = s[:, :128] + s[:, 128:]
    send_ref[pl.ds(14, NBLK, stride=BROWS), :] = pick(rows14, core ^ 1)
    send_ref[pl.ds(15, NBLK, stride=BROWS), :] = pick(rows15, core ^ 1)


def keep_kernel(hot_ref, vals_ref, rows_ref, keep_ref):
    s = mm(hot_ref[...], vals_ref[...])
    keep_ref[...] = s[:, :128] + s[:, 128:]
    keep_ref[pl.ds(14, NBLK, stride=BROWS), :] = rows_ref[0:NBLK, :]
    keep_ref[pl.ds(15, NBLK, stride=BROWS), :] = rows_ref[NBLK : 2 * NBLK, :]


def beam_kernel(blocks_ref, out_ref):
    total = blocks_ref[0:BROWS, :]
    for b in range(1, NBLK):
        total = total + blocks_ref[b * BROWS : (b + 1) * BROWS, :]
    near = jnp.broadcast_to(total[14:15, :], (BROWS, 128))
    mine = jnp.broadcast_to(total[15:16, :], (BROWS, 128))
    i = lax.broadcasted_iota(jnp.int32, (BROWS, 128), 0)
    lane = lax.broadcasted_iota(jnp.int32, (BROWS, 128), 1)
    spot = jnp.where(i < OWN, i, 64 + i - OWN)

    def take(src, slot):
        return jnp.sum(jnp.where(lane == spot + 8 * slot, src, 0.0), axis=1, keepdims=True)

    left_hits = take(near, 6) + 1.0
    right_hits = take(near, 7) + 1.0
    hits = take(mine, 6) + 1.0
    valid = i < OWN + 2 * RADIUS
    binned = jnp.where(valid, total / hits, 0.0)
    left = [take(near, m) / left_hits for m in range(RADIUS)]
    right = [take(near, RADIUS + m) / right_hits for m in range(RADIUS)]
    taps = beam_taps()
    smooth = taps[RADIUS] * binned
    for m in range(1, RADIUS + 1):
        moved = pltpu.roll(binned, m, 1)
        for q in range(m):
            moved = jnp.where(lane == q, left[RADIUS - m + q], moved)
        smooth = smooth + taps[RADIUS - m] * moved
        moved = pltpu.roll(binned, TCOLS - m, 1)
        for q in range(m):
            moved = jnp.where(lane == TCOLS - m + q, right[q], moved)
        smooth = smooth + taps[RADIUS + m] * moved
    out = taps[0] * smooth[0:OWN, :]
    for m in range(1, 2 * RADIUS + 1):
        out = out + taps[m] * smooth[m : m + OWN, :]
    out_ref[...] = out


VMEM = pl.BlockSpec(memory_space=pltpu.VMEM)
SMEM = pl.BlockSpec(memory_space=pltpu.SMEM)


def call(kernel, shapes, specs, name, flops, *args):
    nbytes = sum(math.prod(s.shape) * 4 for s in shapes) + sum(a.size * 4 for a in args)
    return pl.pallas_call(
        kernel,
        out_shape=shapes,
        in_specs=specs,
        out_specs=[VMEM] * len(shapes),
        name=name,
        compiler_params=pltpu.CompilerParams(vmem_limit_bytes=48 << 20),
        cost_estimate=pl.CostEstimate(flops=flops, bytes_accessed=nbytes, transcendentals=0),
    )(*args)


def sds(shape, dtype=F32):
    return jax.ShapeDtypeStruct(shape, dtype)


def body(timestreams, templates, validity, tile_index, row_offset, col_start):
    (eh, el), (sh, sl), tw = tables()
    eh, el, sh, sl, tw = (jnp.asarray(v) for v in (eh, el, sh, sl, tw))
    core = lax.axis_index("core").reshape(1)
    v_row = validity.reshape(1, DETS)
    (part,) = call(
        analysis_kernel, [sds((NMODE, 3 * FKEEP))], [VMEM] * 6, "analysis", 400_000_000,
        timestreams, templates, v_row, eh, el, tw,
    )
    part = part + lax.ppermute(part, "core", [(0, 1), (1, 0)])
    part = part + lax.ppermute(part, "y", [(k, k ^ 1) for k in range(NY)])
    other = lax.ppermute(part, "y", [(k, k ^ 2) for k in range(NY)])
    line = (tile_index * TROWS + row_offset).T.reshape(1, NRUNS)
    zid = (((row_offset + RADIUS) >> 3) * NT + tile_index).T.reshape(1, NRUNS)
    big = (NBLK * BROWS, NRUNS)
    send_hot, keep_hot, zhot, idx, edge, mask, zh = call(
        index_kernel,
        [
            sds(big, BF), sds(big, BF), sds((ZROWS, NRUNS), BF),
            sds((NRUNS, 128), jnp.int32), sds((NRUNS, 128), jnp.int32),
            sds((NRUNS, 128)), sds((ZROWS, 128)),
        ],
        [SMEM] + [VMEM] * 5, "index", 100_000_000,
        core, line, zid, col_start, row_offset, v_row,
    )
    cleaned, send, vals, rows = call(
        clean_kernel,
        [
            sds((DETS, SEG)), sds((NBLK * BROWS, 128)),
            sds((NRUNS, 256), BF), sds((2 * NBLK, 128)),
        ],
        [SMEM] + [VMEM] * 14, "clean", 1_000_000_000,
        core, part, other, templates, v_row, timestreams, sh, sl, tw,
        idx, edge, mask, zhot, zh, send_hot,
    )
    got = lax.ppermute(send, "core", [(0, 1), (1, 0)])
    (keep,) = call(
        keep_kernel, [sds((NBLK * BROWS, 128))], [VMEM] * 3, "keep", 500_000_000,
        keep_hot, vals, rows,
    )
    blocks = lax.all_to_all(keep + got, ("y", "z", "x"), 0, 0, tiled=True)
    (beamed,) = call(
        beam_kernel, [sds((OWN, TCOLS))], [VMEM], "beam", 1_000_000, blocks
    )
    return (cleaned, beamed)


def solution(mesh):
    fine = Mesh(mesh.devices.reshape(NY, 2, 4, 4), ("y", "core", "z", "x"))
    det, tm = ("y", "core"), ("z", "x")
    in_specs = (P(det, tm), P(det, None), P(det), P(det, tm), P(det, tm), P(det, tm))
    out_specs = (P(det, tm), P(det, tm))
    return jax.shard_map(body, mesh=fine, in_specs=in_specs, out_specs=out_specs, check_vma=False)
```

```python
import math

import jax
import jax.numpy as jnp
import numpy as np
from jax import lax
from jax.experimental import pallas as pl
from jax.experimental.pallas import tpu as pltpu
from jax.sharding import Mesh
from jax.sharding import PartitionSpec as P
import ml_dtypes

SEG = 4096
NMODE = 32
FKEEP = 128
RUN = 128
TROWS = 64
TCOLS = 128
RADIUS = 3
DETS = 32
CHUNK = 256
NCHUNK = SEG // CHUNK
NRUNS = DETS * SEG // RUN
NT = 16
NY = 4
OWN = 8
BROWS = 16
NBLK = NY * NT
ZROWS = (TROWS // OWN + 1) * NT
BF = jnp.bfloat16
F32 = jnp.float32


def split_np(a):
    hi = a.astype(np.float32).astype(ml_dtypes.bfloat16)
    lo = (a - hi.astype(np.float64)).astype(np.float32).astype(ml_dtypes.bfloat16)
    return hi, lo


def tables():
    j = np.arange(CHUNK)[:, None]
    k = np.arange(FKEEP)[None, :]
    phi = 2.0 * np.pi * (j * k % SEG) / SEG
    basis = np.concatenate([np.cos(phi), np.sin(phi)], axis=1)
    c = np.arange(NCHUNK)[:, None]
    theta = 2.0 * np.pi * (c * CHUNK * k % SEG) / SEG
    twiddle = np.concatenate([np.cos(theta), np.sin(theta)], axis=1).astype(np.float32)
    scale = np.where(np.arange(FKEEP) == 0, 1.0 / SEG, 2.0 / SEG)
    synth = basis.T * np.concatenate([scale, scale])[:, None]
    return np.concatenate(split_np(basis)), np.concatenate(split_np(synth)), twiddle


def beam_taps():
    values = [math.exp(-(m * m) / 4.5) for m in range(-RADIUS, RADIUS + 1)]
    total = sum(values)
    return [v / total for v in values]


def split(a):
    hi = a.astype(BF)
    return hi, (a - hi.astype(F32)).astype(BF)


def mm(a, b):
    return jnp.dot(a, b, preferred_element_type=F32)


def mm0(a, b):
    return lax.dot_general(
        a, b, (((0,), (0,)), ((), ())), precision=lax.Precision.HIGHEST,
        preferred_element_type=F32,
    )


def column(row, n):
    full = jnp.broadcast_to(row, (n, row.shape[1]))
    same = lax.broadcasted_iota(jnp.int32, full.shape, 0) == lax.broadcasted_iota(
        jnp.int32, full.shape, 1
    )
    return jnp.sum(jnp.where(same, full, 0.0), axis=1, keepdims=True)


def analysis_kernel(
    x_hbm, t_hbm, v_hbm, basis_hbm, synth_hbm, tw_hbm,
    out_ref, x_ref, synth_ref, tw_ref, tt_ref, w_ref,
    t_ref, v_ref, basis_ref, sems,
):
    copies = [
        pltpu.make_async_copy(src, dst, sems.at[n])
        for n, (src, dst) in enumerate(
            (
                (x_hbm, x_ref), (basis_hbm, basis_ref), (t_hbm, t_ref),
                (v_hbm, v_ref), (tw_hbm, tw_ref), (synth_hbm, synth_ref),
            )
        )
    ]
    for copy in copies:
        copy.start()
    copies[2].wait()
    copies[3].wait()
    w = column(v_ref[...].astype(F32), DETS)
    t = t_ref[...]
    wt = t * w
    w_ref[...] = jnp.broadcast_to(w, (DETS, 128))
    tt_ref[...] = t.T
    gram = mm0(wt, t)
    out_ref[:, 2 * FKEEP :] = jnp.concatenate(
        [gram, jnp.zeros((NMODE, FKEEP - NMODE), F32)], axis=1
    )
    copies[0].wait()
    copies[1].wait()
    x = jnp.concatenate(
        [x_ref[:, c * CHUNK : (c + 1) * CHUNK] for c in range(NCHUNK)], axis=0
    )
    hi, lo = split(x)
    eh = basis_ref[:CHUNK, :]
    y = mm(hi, eh) + mm(lo, eh) + mm(hi, basis_ref[CHUNK:, :])
    copies[4].wait()
    re = jnp.zeros((DETS, FKEEP), F32)
    im = jnp.zeros((DETS, FKEEP), F32)
    for c in range(NCHUNK):
        yc = y[c * DETS : (c + 1) * DETS, :FKEEP]
        ys = y[c * DETS : (c + 1) * DETS, FKEEP:]
        cos = tw_ref[c : c + 1, :FKEEP]
        sin = tw_ref[c : c + 1, FKEEP:]
        re = re + (cos * yc - sin * ys)
        im = im + (sin * yc + cos * ys)
    out_ref[:, 0:FKEEP] = mm0(wt, re)
    out_ref[:, FKEEP : 2 * FKEEP] = mm0(wt, im)
    copies[5].wait()


def edge_col(lane):
    slot = lane >> 3
    return jnp.where(slot < 3, TCOLS - RADIUS + slot, slot - 3)


def ids_of_blocks(core):
    l = lax.broadcasted_iota(jnp.int32, (NBLK * BROWS, 128), 0)
    i = l & (BROWS - 1)
    b = l >> 4
    row = (b >> 4) * (2 * OWN) + core * OWN - RADIUS + i
    ok = (i < OWN + 2 * RADIUS) & (row >= 0) & (row < TROWS)
    return jnp.where(ok, (b & (NT - 1)) * TROWS + row, -1)


def run_row(ids):
    flat = ids.astype(F32).T
    parts = [flat[c : c + 1, :] for c in range(SEG // RUN)]
    return jnp.concatenate(parts, axis=1).astype(jnp.int32)


def fill_hot(ref, ids, line):
    for q in range(NRUNS // 128):
        sl = slice(q * 128, (q + 1) * 128)
        ref[:, sl] = jnp.where(ids == line[:, sl], 1.0, 0.0).astype(BF)


def first_index_kernel(
    core_ref, ti_hbm, ro_hbm, cs_hbm,
    send_ref, line_ref, zid_ref, ro_ref, cs_ref, ti_ref, sems,
):
    copies = [
        pltpu.make_async_copy(src, dst, sems.at[n])
        for n, (src, dst) in enumerate(((ti_hbm, ti_ref), (ro_hbm, ro_ref), (cs_hbm, cs_ref)))
    ]
    for copy in copies:
        copy.start()
    ids = ids_of_blocks(core_ref[0] ^ 1)
    for copy in copies:
        copy.wait()
    ti = ti_ref[...]
    ro = ro_ref[...]
    line = run_row(ti * TROWS + ro)
    line_ref[...] = line
    zid_ref[...] = run_row(((ro + RADIUS) >> 3) * NT + ti)
    fill_hot(send_ref, ids, line)


def second_index_kernel(
    core_ref, line_ref, zid_ref, ro_ref, cs_ref, w_ref,
    keep_ref, zhot_ref, idx_ref, edge_ref, mask_ref, zh_ref,
):
    zl = lax.broadcasted_iota(jnp.int32, (ZROWS, NRUNS), 0)
    zhot = jnp.where(zl == zid_ref[...], 1.0, 0.0).astype(BF)
    zhot_ref[...] = zhot
    w = w_ref[...]
    lane = lax.broadcasted_iota(jnp.int32, (DETS, 128), 1)
    ecol = edge_col(lane)
    hparts = []
    for c in range(SEG // RUN):
        sl = slice(c * DETS, (c + 1) * DETS)
        cs = jnp.broadcast_to(cs_ref[:, c : c + 1], (DETS, 128))
        ro = jnp.broadcast_to(ro_ref[:, c : c + 1], (DETS, 128))
        idx_ref[sl, :] = (lane - cs) & (TCOLS - 1)
        edge_ref[sl, :] = (ecol - cs) & (TCOLS - 1)
        here = ((ro + RADIUS) & (OWN - 1)) == (lane & (OWN - 1))
        mask_ref[sl, :] = jnp.where(here & (lane < 48), 1.0, 0.0)
        hparts.append(jnp.where(here & (lane >= 48) & (lane < 56), w, 0.0).astype(BF))
    zh_ref[...] = mm(zhot, jnp.concatenate(hparts, axis=0))
    fill_hot(keep_ref, ids_of_blocks(core_ref[0]), line_ref[...])


def solve(gram, rhs):
    n = gram.shape[0]
    a = jnp.concatenate([gram, rhs], axis=1)
    rows = lax.broadcasted_iota(jnp.int32, a.shape, 0)
    for k in range(n):
        pivot = a[k : k + 1, :]
        pivot = pivot / a[k : k + 1, k : k + 1]
        a = jnp.where(rows == k, pivot, a - a[:, k : k + 1] * pivot)
    return a[:, n:]


def shifted_tiles(z, by):
    zero = jnp.zeros((z.shape[0], 1, 128), F32)
    if by < 0:
        return jnp.concatenate([zero, z[:, :-1]], axis=1)
    return jnp.concatenate([z[:, 1:], zero], axis=1)


def clean_kernel(
    core_ref, p_ref, q_ref, tt_ref, w_ref, x_ref, synth_ref, tw_ref,
    idx_ref, edge_ref, mask_ref, zhot_ref, zh_ref, send_hot_ref,
    clean_ref, send_ref, vals_ref, rows_ref,
):
    w = w_ref[...]
    w = jnp.concatenate([w, w], axis=1)
    p = p_ref[...] + q_ref[...]
    eye = lax.broadcasted_iota(jnp.int32, (NMODE, NMODE), 0) == lax.broadcasted_iota(
        jnp.int32, (NMODE, NMODE), 1
    )
    gram = p[:, 2 * FKEEP : 2 * FKEEP + NMODE] + jnp.where(eye, 0.05, 0.0)
    coef = solve(gram, tt_ref[...])
    a = mm0(coef, p[:, :FKEEP])
    b = mm0(coef, p[:, FKEEP : 2 * FKEEP])
    parts = []
    for c in range(NCHUNK):
        cos = tw_ref[c : c + 1, :FKEEP]
        sin = tw_ref[c : c + 1, FKEEP:]
        parts.append(jnp.concatenate([a * cos + b * sin, b * cos - a * sin], axis=1))
    hi, lo = split(jnp.concatenate(parts, axis=0))
    sh = synth_ref[:CHUNK, :]
    low = mm(hi, sh) + mm(lo, sh) + mm(hi, synth_ref[CHUNK:, :])
    runs = []
    for c in range(NCHUNK):
        part = w * (x_ref[:, c * CHUNK : (c + 1) * CHUNK] - low[c * DETS : (c + 1) * DETS, :])
        clean_ref[:, c * CHUNK : (c + 1) * CHUNK] = part
        runs.append(part[:, :RUN])
        runs.append(part[:, RUN:])
    run = jnp.concatenate(runs, axis=0)
    vals = jnp.concatenate(
        split(jnp.take_along_axis(run, idx_ref[...], axis=1, mode="promise_in_bounds")), axis=1
    )
    vals_ref[...] = vals
    evals = jnp.take_along_axis(run, edge_ref[...], axis=1, mode="promise_in_bounds")
    evals = jnp.concatenate(split(evals * mask_ref[...]), axis=1)
    z = mm(zhot_ref[...], evals)
    z = (z[:, :128] + z[:, 128:] + zh_ref[...]).reshape(ZROWS // NT, NT, 128)
    left = shifted_tiles(z, -1)
    right = shifted_tiles(z, 1)
    lane = lax.broadcasted_iota(jnp.int32, z.shape, 2)
    left_hits = left
    right_hits = jnp.concatenate([jnp.zeros(z.shape[:2] + (8,), F32), right[:, :, :-8]], axis=2)
    near = jnp.where(
        lane < 24, left, jnp.where(lane < 48, right, jnp.where(lane < 56, left_hits, right_hits))
    )
    near = jnp.where(lane < 64, near, 0.0)
    mine = jnp.where((lane >= 48) & (lane < 56), z, 0.0)
    nd = TROWS // OWN

    def both(v):
        return v[:nd] + jnp.concatenate([jnp.zeros((nd, NT, 64), F32), v[1:, :, :64]], axis=2)

    rows14 = both(near)
    rows15 = both(mine)
    core = core_ref[0]

    def pick(v, which):
        return jnp.concatenate(
            [jnp.where(which == 1, v[2 * y + 1], v[2 * y]) for y in range(NY)], axis=0
        )

    rows_ref[0:NBLK, :] = pick(rows14, core)
    rows_ref[NBLK : 2 * NBLK, :] = pick(rows15, core)
    s = mm(send_hot_ref[...], vals)
    send_ref[...] = s[:, :128] + s[:, 128:]
    send_ref[pl.ds(14, NBLK, stride=BROWS), :] = pick(rows14, core ^ 1)
    send_ref[pl.ds(15, NBLK, stride=BROWS), :] = pick(rows15, core ^ 1)


def keep_kernel(hot_ref, vals_ref, rows_ref, clean_ref, keep_ref, out_hbm, sem):
    copy = pltpu.make_async_copy(clean_ref, out_hbm, sem)
    copy.start()
    s = mm(hot_ref[...], vals_ref[...])
    keep_ref[...] = s[:, :128] + s[:, 128:]
    keep_ref[pl.ds(14, NBLK, stride=BROWS), :] = rows_ref[0:NBLK, :]
    keep_ref[pl.ds(15, NBLK, stride=BROWS), :] = rows_ref[NBLK : 2 * NBLK, :]
    copy.wait()


def beam_kernel(blocks_ref, out_ref):
    total = blocks_ref[0:BROWS, :]
    for b in range(1, NBLK):
        total = total + blocks_ref[b * BROWS : (b + 1) * BROWS, :]
    near = jnp.broadcast_to(total[14:15, :], (BROWS, 128))
    mine = jnp.broadcast_to(total[15:16, :], (BROWS, 128))
    i = lax.broadcasted_iota(jnp.int32, (BROWS, 128), 0)
    lane = lax.broadcasted_iota(jnp.int32, (BROWS, 128), 1)
    spot = jnp.where(i < OWN, i, 64 + i - OWN)

    def take(src, slot):
        return jnp.sum(jnp.where(lane == spot + 8 * slot, src, 0.0), axis=1, keepdims=True)

    left_hits = take(near, 6) + 1.0
    right_hits = take(near, 7) + 1.0
    hits = take(mine, 6) + 1.0
    valid = i < OWN + 2 * RADIUS
    binned = jnp.where(valid, total / hits, 0.0)
    left = [take(near, m) / left_hits for m in range(RADIUS)]
    right = [take(near, RADIUS + m) / right_hits for m in range(RADIUS)]
    taps = beam_taps()
    smooth = taps[RADIUS] * binned
    for m in range(1, RADIUS + 1):
        moved = pltpu.roll(binned, m, 1)
        for q in range(m):
            moved = jnp.where(lane == q, left[RADIUS - m + q], moved)
        smooth = smooth + taps[RADIUS - m] * moved
        moved = pltpu.roll(binned, TCOLS - m, 1)
        for q in range(m):
            moved = jnp.where(lane == TCOLS - m + q, right[q], moved)
        smooth = smooth + taps[RADIUS + m] * moved
    out = taps[0] * smooth[0:OWN, :]
    for m in range(1, 2 * RADIUS + 1):
        out = out + taps[m] * smooth[m : m + OWN, :]
    out_ref[...] = out


VMEM = pl.BlockSpec(memory_space=pltpu.VMEM)
SMEM = pl.BlockSpec(memory_space=pltpu.SMEM)
HBM = pl.BlockSpec(memory_space=pltpu.HBM)


def call(kernel, outs, specs, name, flops, *args, out_specs=None, scratch=()):
    args = [
        pltpu.with_memory_space_constraint(a, pltpu.HBM) if spec is HBM else a
        for a, spec in zip(args, specs)
    ]
    nbytes = sum(math.prod(s.shape) * 4 for s in outs) + sum(a.size * 4 for a in args)
    return pl.pallas_call(
        kernel,
        out_shape=outs,
        in_specs=specs,
        out_specs=out_specs or [VMEM] * len(outs),
        scratch_shapes=list(scratch),
        name=name,
        compiler_params=pltpu.CompilerParams(vmem_limit_bytes=40 << 20),
        cost_estimate=pl.CostEstimate(flops=flops, bytes_accessed=nbytes, transcendentals=0),
    )(*args)


def sds(shape, dtype=F32):
    return jax.ShapeDtypeStruct(shape, dtype)


I32 = jnp.int32


def body(timestreams, templates, validity, tile_index, row_offset, col_start):
    basis, synth, tw = tables()
    core = lax.axis_index("core").reshape(1)
    part, x, synth, tw, tt, w = call(
        analysis_kernel,
        [
            sds((NMODE, 3 * FKEEP)), sds((DETS, SEG)), sds((2 * CHUNK, 2 * FKEEP), BF),
            sds((NCHUNK, 2 * FKEEP)), sds((NMODE, DETS)), sds((DETS, 128)),
        ],
        [HBM] * 6, "analysis", 400_000_000,
        timestreams, templates, validity.reshape(1, DETS),
        jnp.asarray(basis), jnp.asarray(synth), jnp.asarray(tw),
        scratch=[
            pltpu.VMEM((DETS, NMODE), F32), pltpu.VMEM((1, DETS), I32),
            pltpu.VMEM((2 * CHUNK, 2 * FKEEP), BF), pltpu.SemaphoreType.DMA((6,)),
        ],
    )
    part = part + lax.ppermute(part, "core", [(0, 1), (1, 0)])
    tile_index, row_offset, col_start, part = lax.optimization_barrier(
        (tile_index, row_offset, col_start, part)
    )
    other = lax.ppermute(part, "y", [(k, k ^ 1) for k in range(NY)])
    big = (NBLK * BROWS, NRUNS)
    send_hot, line, zid, ro, cs = call(
        first_index_kernel,
        [
            sds(big, BF), sds((1, NRUNS), I32), sds((1, NRUNS), I32),
            sds((DETS, SEG // RUN), I32), sds((DETS, SEG // RUN), I32),
        ],
        [SMEM] + [HBM] * 3, "index1", 100_000_000,
        core, tile_index, row_offset, col_start,
        scratch=[pltpu.VMEM((DETS, SEG // RUN), I32), pltpu.SemaphoreType.DMA((3,))],
    )
    part = part + other
    part, line = lax.optimization_barrier((part, line))
    other = lax.ppermute(part, "y", [(k, k ^ 2) for k in range(NY)])
    keep_hot, zhot, idx, edge, mask, zh = call(
        second_index_kernel,
        [
            sds(big, BF), sds((ZROWS, NRUNS), BF),
            sds((NRUNS, 128), I32), sds((NRUNS, 128), I32),
            sds((NRUNS, 128)), sds((ZROWS, 128)),
        ],
        [SMEM] + [VMEM] * 5, "index2", 100_000_000,
        core, line, zid, ro, cs, w,
    )
    cleaned, send, vals, rows = call(
        clean_kernel,
        [
            sds((DETS, SEG)), sds((NBLK * BROWS, 128)),
            sds((NRUNS, 256), BF), sds((2 * NBLK, 128)),
        ],
        [SMEM] + [VMEM] * 13, "clean", 1_000_000_000,
        core, part, other, tt, w, x, synth, tw, idx, edge, mask, zhot, zh, send_hot,
    )
    got = lax.ppermute(send, "core", [(0, 1), (1, 0)])
    keep, cleaned = call(
        keep_kernel, [sds((NBLK * BROWS, 128)), sds((DETS, SEG))], [VMEM] * 4, "keep",
        500_000_000, keep_hot, vals, rows, cleaned,
        out_specs=[VMEM, HBM], scratch=[pltpu.SemaphoreType.DMA],
    )
    blocks = lax.all_to_all(keep + got, ("y", "z", "x"), 0, 0, tiled=True)
    (beamed,) = call(
        beam_kernel, [sds((OWN, TCOLS))], [VMEM], "beam", 1_000_000, blocks
    )
    return (cleaned, beamed)


def solution(mesh):
    fine = Mesh(mesh.devices.reshape(NY, 2, 4, 4), ("y", "core", "z", "x"))
    det, tm = ("y", "core"), ("z", "x")
    in_specs = (P(det, tm), P(det, None), P(det), P(det, tm), P(det, tm), P(det, tm))
    out_specs = (P(det, tm), P(det, tm))
    return jax.shard_map(body, mesh=fine, in_specs=in_specs, out_specs=out_specs, check_vma=False)
```

```python
import math

import jax
import jax.numpy as jnp
import numpy as np
from jax import lax
from jax.experimental import pallas as pl
from jax.experimental.pallas import tpu as pltpu
from jax.sharding import Mesh
from jax.sharding import PartitionSpec as P
import ml_dtypes

SEG = 4096
NMODE = 32
FKEEP = 128
RUN = 128
TROWS = 64
TCOLS = 128
RADIUS = 3
DETS = 32
CHUNK = 256
NCHUNK = SEG // CHUNK
NRUNS = DETS * SEG // RUN
NT = 16
NY = 4
OWN = 8
BROWS = 16
NBLK = NY * NT
ZROWS = (TROWS // OWN + 1) * NT
BF = jnp.bfloat16
F32 = jnp.float32


def split_np(a):
    hi = a.astype(np.float32).astype(ml_dtypes.bfloat16)
    lo = (a - hi.astype(np.float64)).astype(np.float32).astype(ml_dtypes.bfloat16)
    return hi, lo


def tables():
    j = np.arange(CHUNK)[:, None]
    k = np.arange(FKEEP)[None, :]
    phi = 2.0 * np.pi * (j * k % SEG) / SEG
    basis = np.concatenate([np.cos(phi), np.sin(phi)], axis=1)
    c = np.arange(NCHUNK)[:, None]
    theta = 2.0 * np.pi * (c * CHUNK * k % SEG) / SEG
    twiddle = np.concatenate([np.cos(theta), np.sin(theta)], axis=1).astype(np.float32)
    scale = np.where(np.arange(FKEEP) == 0, 1.0 / SEG, 2.0 / SEG)
    synth = basis.T * np.concatenate([scale, scale])[:, None]
    return np.concatenate(split_np(basis)), np.concatenate(split_np(synth)), twiddle


def beam_taps():
    values = [math.exp(-(m * m) / 4.5) for m in range(-RADIUS, RADIUS + 1)]
    total = sum(values)
    return [v / total for v in values]


def split(a):
    hi = a.astype(BF)
    return hi, (a - hi.astype(F32)).astype(BF)


def mm(a, b):
    return jnp.dot(a, b, preferred_element_type=F32)


def mm0(a, b):
    return lax.dot_general(
        a, b, (((0,), (0,)), ((), ())), precision=lax.Precision.HIGHEST,
        preferred_element_type=F32,
    )


def mm0_split(a, b):
    ah, al = split(a)
    bh, bl = split(b)
    return lax.dot_general(
        jnp.concatenate([ah, al, ah], axis=0), jnp.concatenate([bh, bh, bl], axis=0),
        (((0,), (0,)), ((), ())), preferred_element_type=F32,
    )


def column(row, n):
    full = jnp.broadcast_to(row, (n, row.shape[1]))
    same = lax.broadcasted_iota(jnp.int32, full.shape, 0) == lax.broadcasted_iota(
        jnp.int32, full.shape, 1
    )
    return jnp.sum(jnp.where(same, full, 0.0), axis=1, keepdims=True)


def analysis_kernel(
    x_hbm, t_hbm, v_hbm, basis_hbm, synth_hbm, tw_hbm,
    out_ref, x_ref, synth_ref, tw_ref, tt_ref, w_ref,
    t_ref, v_ref, basis_ref, sems,
):
    copies = [
        pltpu.make_async_copy(src, dst, sems.at[n])
        for n, (src, dst) in enumerate(
            (
                (x_hbm, x_ref), (basis_hbm, basis_ref), (t_hbm, t_ref),
                (v_hbm, v_ref), (tw_hbm, tw_ref), (synth_hbm, synth_ref),
            )
        )
    ]
    for copy in copies:
        copy.start()
    copies[2].wait()
    copies[3].wait()
    w = column(v_ref[...].astype(F32), DETS)
    t = t_ref[...]
    wt = t * w
    w_ref[...] = jnp.broadcast_to(w, (DETS, 128))
    tt_ref[...] = t.T
    gram = mm0(wt, t)
    out_ref[:, 2 * FKEEP :] = jnp.concatenate(
        [gram, jnp.zeros((NMODE, FKEEP - NMODE), F32)], axis=1
    )
    copies[0].wait()
    copies[1].wait()
    x = jnp.concatenate(
        [x_ref[:, c * CHUNK : (c + 1) * CHUNK] for c in range(NCHUNK)], axis=0
    )
    hi, lo = split(x)
    eh = basis_ref[:CHUNK, :]
    y = mm(hi, eh) + mm(lo, eh) + mm(hi, basis_ref[CHUNK:, :])
    copies[4].wait()
    re = jnp.zeros((DETS, FKEEP), F32)
    im = jnp.zeros((DETS, FKEEP), F32)
    for c in range(NCHUNK):
        yc = y[c * DETS : (c + 1) * DETS, :FKEEP]
        ys = y[c * DETS : (c + 1) * DETS, FKEEP:]
        cos = tw_ref[c : c + 1, :FKEEP]
        sin = tw_ref[c : c + 1, FKEEP:]
        re = re + (cos * yc - sin * ys)
        im = im + (sin * yc + cos * ys)
    out_ref[:, : 2 * FKEEP] = mm0_split(wt, jnp.concatenate([re, im], axis=1))
    copies[5].wait()


def edge_col(lane):
    slot = lane >> 3
    return jnp.where(slot < 3, TCOLS - RADIUS + slot, slot - 3)


def ids_of_blocks(core):
    l = lax.broadcasted_iota(jnp.int32, (NBLK * BROWS, 128), 0)
    i = l & (BROWS - 1)
    b = l >> 4
    row = (b >> 4) * (2 * OWN) + core * OWN - RADIUS + i
    ok = (i < OWN + 2 * RADIUS) & (row >= 0) & (row < TROWS)
    return jnp.where(ok, (b & (NT - 1)) * TROWS + row, -1)


def run_row(ids):
    flat = ids.astype(F32).T
    parts = [flat[c : c + 1, :] for c in range(SEG // RUN)]
    return jnp.concatenate(parts, axis=1).astype(jnp.int32)


def fill_hot(ref, ids, line):
    for q in range(NRUNS // 128):
        sl = slice(q * 128, (q + 1) * 128)
        ref[:, sl] = jnp.where(ids == line[:, sl], 1.0, 0.0).astype(BF)


def first_index_kernel(
    core_ref, ti_hbm, ro_hbm, cs_hbm,
    send_ref, line_ref, zid_ref, ro_ref, cs_ref, ti_ref, sems,
):
    copies = [
        pltpu.make_async_copy(src, dst, sems.at[n])
        for n, (src, dst) in enumerate(((ti_hbm, ti_ref), (ro_hbm, ro_ref), (cs_hbm, cs_ref)))
    ]
    for copy in copies:
        copy.start()
    ids = ids_of_blocks(core_ref[0] ^ 1)
    for copy in copies:
        copy.wait()
    ti = ti_ref[...]
    ro = ro_ref[...]
    line = run_row(ti * TROWS + ro)
    line_ref[...] = line
    zid_ref[...] = run_row(((ro + RADIUS) >> 3) * NT + ti)
    fill_hot(send_ref, ids, line)


def second_index_kernel(
    core_ref, line_ref, zid_ref, ro_ref, cs_ref, w_ref,
    keep_ref, zhot_ref, idx_ref, edge_ref, mask_ref, zh_ref,
):
    zl = lax.broadcasted_iota(jnp.int32, (ZROWS, NRUNS), 0)
    zhot = jnp.where(zl == zid_ref[...], 1.0, 0.0).astype(BF)
    zhot_ref[...] = zhot
    w = w_ref[...]
    lane = lax.broadcasted_iota(jnp.int32, (DETS, 128), 1)
    ecol = edge_col(lane)
    hparts = []
    for c in range(SEG // RUN):
        sl = slice(c * DETS, (c + 1) * DETS)
        cs = jnp.broadcast_to(cs_ref[:, c : c + 1], (DETS, 128))
        ro = jnp.broadcast_to(ro_ref[:, c : c + 1], (DETS, 128))
        idx_ref[sl, :] = (lane - cs) & (TCOLS - 1)
        edge_ref[sl, :] = (ecol - cs) & (TCOLS - 1)
        here = ((ro + RADIUS) & (OWN - 1)) == (lane & (OWN - 1))
        mask_ref[sl, :] = jnp.where(here & (lane < 48), 1.0, 0.0)
        hparts.append(jnp.where(here & (lane >= 48) & (lane < 56), w, 0.0).astype(BF))
    zh_ref[...] = mm(zhot, jnp.concatenate(hparts, axis=0))
    fill_hot(keep_ref, ids_of_blocks(core_ref[0]), line_ref[...])


def lanes_of(v, k):
    return jnp.broadcast_to(v[:, k : k + 1], (8, 128))


def row_of(v, r):
    return jnp.broadcast_to(v[r : r + 1, :], (8, 128))


def solve(gram, rhs):
    n = gram.shape[0]
    eye = lax.broadcasted_iota(jnp.int32, gram.shape, 0) == lax.broadcasted_iota(
        jnp.int32, gram.shape, 1
    )
    diag = jnp.where(eye, gram, 0.0)
    down = lax.rsqrt(jnp.sum(diag, axis=1, keepdims=True))
    along = lax.rsqrt(jnp.sum(diag, axis=0, keepdims=True))
    full = jnp.concatenate(
        [gram * down * along, rhs * down, jnp.zeros((n, 128 - 2 * n), F32)], axis=1
    )
    a = [full[8 * i : 8 * i + 8, :] for i in range(n // 8)]
    sub = lax.broadcasted_iota(jnp.int32, (8, 128), 0)
    for k in range(0, n, 4):
        here, r = k // 8, k % 8
        c = [[lanes_of(v, k + j) for v in a] for j in range(4)]
        p = [[row_of(c[j][here], r + i) for j in range(4)] for i in range(4)]
        rows = [row_of(a[here], r + i) for i in range(4)]
        i1 = 1.0 / (p[0][0] * p[1][1] - p[0][1] * p[0][1])
        e00, e01, e11 = p[1][1] * i1, -p[0][1] * i1, p[0][0] * i1
        w00 = e00 * p[0][2] + e01 * p[1][2]
        w01 = e00 * p[0][3] + e01 * p[1][3]
        w10 = e01 * p[0][2] + e11 * p[1][2]
        w11 = e01 * p[0][3] + e11 * p[1][3]
        s00 = p[2][2] - (p[0][2] * w00 + p[1][2] * w10)
        s01 = p[2][3] - (p[0][2] * w01 + p[1][2] * w11)
        s11 = p[3][3] - (p[0][3] * w01 + p[1][3] * w11)
        i2 = 1.0 / (s00 * s11 - s01 * s01)
        y0 = e00 * rows[0] + e01 * rows[1]
        y1 = e01 * rows[0] + e11 * rows[1]
        q2 = rows[2] - (p[0][2] * y0 + p[1][2] * y1)
        q3 = rows[3] - (p[0][3] * y0 + p[1][3] * y1)
        n2 = (s11 * q2 - s01 * q3) * i2
        n3 = (s00 * q3 - s01 * q2) * i2
        n0 = y0 - (w00 * n2 + w01 * n3)
        n1 = y1 - (w10 * n2 + w11 * n3)
        for i in range(n // 8):
            a[i] = a[i] - ((c[0][i] * n0 + c[1][i] * n1) + (c[2][i] * n2 + c[3][i] * n3))
        for j, new in enumerate((n0, n1, n2, n3)):
            a[here] = jnp.where(sub == r + j, new, a[here])
    return jnp.concatenate(a, axis=0)[:, n : 2 * n] * down


def shifted_tiles(z, by):
    zero = jnp.zeros((z.shape[0], 1, 128), F32)
    if by < 0:
        return jnp.concatenate([zero, z[:, :-1]], axis=1)
    return jnp.concatenate([z[:, 1:], zero], axis=1)


def clean_kernel(
    core_ref, p_ref, q_ref, tt_ref, w_ref, x_ref, synth_ref, tw_ref,
    idx_ref, edge_ref, mask_ref, zhot_ref, zh_ref, send_hot_ref,
    clean_ref, send_ref, vals_ref, rows_ref,
):
    w = w_ref[...]
    w = jnp.concatenate([w, w], axis=1)
    p = p_ref[...] + q_ref[...]
    eye = lax.broadcasted_iota(jnp.int32, (NMODE, NMODE), 0) == lax.broadcasted_iota(
        jnp.int32, (NMODE, NMODE), 1
    )
    gram = p[:, 2 * FKEEP : 2 * FKEEP + NMODE] + jnp.where(eye, 0.05, 0.0)
    coef = solve(gram, tt_ref[...])
    ab = mm0_split(coef, p[:, : 2 * FKEEP])
    a = ab[:, :FKEEP]
    b = ab[:, FKEEP:]
    parts = []
    for c in range(NCHUNK):
        cos = tw_ref[c : c + 1, :FKEEP]
        sin = tw_ref[c : c + 1, FKEEP:]
        parts.append(jnp.concatenate([a * cos + b * sin, b * cos - a * sin], axis=1))
    hi, lo = split(jnp.concatenate(parts, axis=0))
    sh = synth_ref[:CHUNK, :]
    low = mm(hi, sh) + mm(lo, sh) + mm(hi, synth_ref[CHUNK:, :])
    runs = []
    for c in range(NCHUNK):
        part = w * (x_ref[:, c * CHUNK : (c + 1) * CHUNK] - low[c * DETS : (c + 1) * DETS, :])
        clean_ref[:, c * CHUNK : (c + 1) * CHUNK] = part
        runs.append(part[:, :RUN])
        runs.append(part[:, RUN:])
    run = jnp.concatenate(runs, axis=0)
    vals = jnp.concatenate(
        split(jnp.take_along_axis(run, idx_ref[...], axis=1, mode="promise_in_bounds")), axis=1
    )
    vals_ref[...] = vals
    evals = jnp.take_along_axis(run, edge_ref[...], axis=1, mode="promise_in_bounds")
    evals = jnp.concatenate(split(evals * mask_ref[...]), axis=1)
    z = mm(zhot_ref[...], evals)
    z = (z[:, :128] + z[:, 128:] + zh_ref[...]).reshape(ZROWS // NT, NT, 128)
    left = shifted_tiles(z, -1)
    right = shifted_tiles(z, 1)
    lane = lax.broadcasted_iota(jnp.int32, z.shape, 2)
    left_hits = left
    right_hits = jnp.concatenate([jnp.zeros(z.shape[:2] + (8,), F32), right[:, :, :-8]], axis=2)
    near = jnp.where(
        lane < 24, left, jnp.where(lane < 48, right, jnp.where(lane < 56, left_hits, right_hits))
    )
    near = jnp.where(lane < 64, near, 0.0)
    mine = jnp.where((lane >= 48) & (lane < 56), z, 0.0)
    nd = TROWS // OWN

    def both(v):
        return v[:nd] + jnp.concatenate([jnp.zeros((nd, NT, 64), F32), v[1:, :, :64]], axis=2)

    rows14 = both(near)
    rows15 = both(mine)
    core = core_ref[0]

    def pick(v, which):
        return jnp.concatenate(
            [jnp.where(which == 1, v[2 * y + 1], v[2 * y]) for y in range(NY)], axis=0
        )

    rows_ref[0:NBLK, :] = pick(rows14, core)
    rows_ref[NBLK : 2 * NBLK, :] = pick(rows15, core)
    s = mm(send_hot_ref[...], vals)
    send_ref[...] = s[:, :128] + s[:, 128:]
    send_ref[pl.ds(14, NBLK, stride=BROWS), :] = pick(rows14, core ^ 1)
    send_ref[pl.ds(15, NBLK, stride=BROWS), :] = pick(rows15, core ^ 1)


def keep_kernel(hot_ref, vals_ref, rows_ref, clean_ref, keep_ref, out_hbm, sem):
    copy = pltpu.make_async_copy(clean_ref, out_hbm, sem)
    copy.start()
    s = mm(hot_ref[...], vals_ref[...])
    keep_ref[...] = s[:, :128] + s[:, 128:]
    keep_ref[pl.ds(14, NBLK, stride=BROWS), :] = rows_ref[0:NBLK, :]
    keep_ref[pl.ds(15, NBLK, stride=BROWS), :] = rows_ref[NBLK : 2 * NBLK, :]
    copy.wait()


def beam_kernel(blocks_ref, out_ref):
    sums = [blocks_ref[b * BROWS : (b + 1) * BROWS, :] for b in range(4)]
    for b in range(4, NBLK):
        sums[b % 4] = sums[b % 4] + blocks_ref[b * BROWS : (b + 1) * BROWS, :]
    total = (sums[0] + sums[1]) + (sums[2] + sums[3])
    near = jnp.broadcast_to(total[14:15, :], (BROWS, 128))
    mine = jnp.broadcast_to(total[15:16, :], (BROWS, 128))
    i = lax.broadcasted_iota(jnp.int32, (BROWS, 128), 0)
    lane = lax.broadcasted_iota(jnp.int32, (BROWS, 128), 1)
    spot = jnp.where(i < OWN, i, 64 + i - OWN)

    def take(src, slot):
        return jnp.sum(jnp.where(lane == spot + 8 * slot, src, 0.0), axis=1, keepdims=True)

    left_hits = take(near, 6) + 1.0
    right_hits = take(near, 7) + 1.0
    hits = take(mine, 6) + 1.0
    valid = i < OWN + 2 * RADIUS
    binned = jnp.where(valid, total / hits, 0.0)
    left = [take(near, m) / left_hits for m in range(RADIUS)]
    right = [take(near, RADIUS + m) / right_hits for m in range(RADIUS)]
    taps = beam_taps()
    smooth = taps[RADIUS] * binned
    for m in range(1, RADIUS + 1):
        moved = pltpu.roll(binned, m, 1)
        for q in range(m):
            moved = jnp.where(lane == q, left[RADIUS - m + q], moved)
        smooth = smooth + taps[RADIUS - m] * moved
        moved = pltpu.roll(binned, TCOLS - m, 1)
        for q in range(m):
            moved = jnp.where(lane == TCOLS - m + q, right[q], moved)
        smooth = smooth + taps[RADIUS + m] * moved
    out = taps[0] * smooth[0:OWN, :]
    for m in range(1, 2 * RADIUS + 1):
        out = out + taps[m] * smooth[m : m + OWN, :]
    out_ref[...] = out


VMEM = pl.BlockSpec(memory_space=pltpu.VMEM)
SMEM = pl.BlockSpec(memory_space=pltpu.SMEM)
HBM = pl.BlockSpec(memory_space=pltpu.HBM)


def call(kernel, outs, specs, name, flops, *args, out_specs=None, scratch=()):
    args = [
        pltpu.with_memory_space_constraint(a, pltpu.HBM) if spec is HBM else a
        for a, spec in zip(args, specs)
    ]
    nbytes = sum(math.prod(s.shape) * 4 for s in outs) + sum(a.size * 4 for a in args)
    return pl.pallas_call(
        kernel,
        out_shape=outs,
        in_specs=specs,
        out_specs=out_specs or [VMEM] * len(outs),
        scratch_shapes=list(scratch),
        name=name,
        compiler_params=pltpu.CompilerParams(vmem_limit_bytes=40 << 20),
        cost_estimate=pl.CostEstimate(flops=flops, bytes_accessed=nbytes, transcendentals=0),
    )(*args)


def sds(shape, dtype=F32):
    return jax.ShapeDtypeStruct(shape, dtype)


I32 = jnp.int32


def body(timestreams, templates, validity, tile_index, row_offset, col_start):
    basis, synth, tw = tables()
    core = lax.axis_index("core").reshape(1)
    part, x, synth, tw, tt, w = call(
        analysis_kernel,
        [
            sds((NMODE, 3 * FKEEP)), sds((DETS, SEG)), sds((2 * CHUNK, 2 * FKEEP), BF),
            sds((NCHUNK, 2 * FKEEP)), sds((NMODE, DETS)), sds((DETS, 128)),
        ],
        [HBM] * 6, "analysis", 400_000_000,
        timestreams, templates, validity.reshape(1, DETS),
        jnp.asarray(basis), jnp.asarray(synth), jnp.asarray(tw),
        scratch=[
            pltpu.VMEM((DETS, NMODE), F32), pltpu.VMEM((1, DETS), I32),
            pltpu.VMEM((2 * CHUNK, 2 * FKEEP), BF), pltpu.SemaphoreType.DMA((6,)),
        ],
    )
    part = part + lax.ppermute(part, "core", [(0, 1), (1, 0)])
    tile_index, row_offset, col_start, part = lax.optimization_barrier(
        (tile_index, row_offset, col_start, part)
    )
    other = lax.ppermute(part, "y", [(k, k ^ 1) for k in range(NY)])
    big = (NBLK * BROWS, NRUNS)
    send_hot, line, zid, ro, cs = call(
        first_index_kernel,
        [
            sds(big, BF), sds((1, NRUNS), I32), sds((1, NRUNS), I32),
            sds((DETS, SEG // RUN), I32), sds((DETS, SEG // RUN), I32),
        ],
        [SMEM] + [HBM] * 3, "index1", 100_000_000,
        core, tile_index, row_offset, col_start,
        scratch=[pltpu.VMEM((DETS, SEG // RUN), I32), pltpu.SemaphoreType.DMA((3,))],
    )
    part = part + other
    part, line = lax.optimization_barrier((part, line))
    other = lax.ppermute(part, "y", [(k, k ^ 3) for k in range(NY)])
    keep_hot, zhot, idx, edge, mask, zh = call(
        second_index_kernel,
        [
            sds(big, BF), sds((ZROWS, NRUNS), BF),
            sds((NRUNS, 128), I32), sds((NRUNS, 128), I32),
            sds((NRUNS, 128)), sds((ZROWS, 128)),
        ],
        [SMEM] + [VMEM] * 5, "index2", 100_000_000,
        core, line, zid, ro, cs, w,
    )
    cleaned, send, vals, rows = call(
        clean_kernel,
        [
            sds((DETS, SEG)), sds((NBLK * BROWS, 128)),
            sds((NRUNS, 256), BF), sds((2 * NBLK, 128)),
        ],
        [SMEM] + [VMEM] * 13, "clean", 1_000_000_000,
        core, part, other, tt, w, x, synth, tw, idx, edge, mask, zhot, zh, send_hot,
    )
    got = lax.ppermute(send, "core", [(0, 1), (1, 0)])
    keep, cleaned = call(
        keep_kernel, [sds((NBLK * BROWS, 128)), sds((DETS, SEG))], [VMEM] * 4, "keep",
        500_000_000, keep_hot, vals, rows, cleaned,
        out_specs=[VMEM, HBM], scratch=[pltpu.SemaphoreType.DMA],
    )
    blocks = lax.all_to_all(keep + got, ("y", "z", "x"), 0, 0, tiled=True)
    (beamed,) = call(
        beam_kernel, [sds((OWN, TCOLS))], [VMEM], "beam", 1_000_000, blocks
    )
    return (cleaned, beamed)


def solution(mesh):
    fine = Mesh(mesh.devices.reshape(NY, 2, 4, 4), ("y", "core", "z", "x"))
    det, tm = ("y", "core"), ("z", "x")
    in_specs = (P(det, tm), P(det, None), P(det), P(det, tm), P(det, tm), P(det, tm))
    out_specs = (P(det, tm), P(det, tm))
    return jax.shard_map(body, mesh=fine, in_specs=in_specs, out_specs=out_specs, check_vma=False)
```

```python
import math

import jax
import jax.numpy as jnp
import numpy as np
from jax import lax
from jax.experimental import pallas as pl
from jax.experimental.pallas import tpu as pltpu
from jax.sharding import Mesh
from jax.sharding import PartitionSpec as P
import ml_dtypes

SEG = 4096
NMODE = 32
FKEEP = 128
RUN = 128
TROWS = 64
TCOLS = 128
RADIUS = 3
DETS = 32
CHUNK = 256
NCHUNK = SEG // CHUNK
XPIECE = 1024
NRUNS = DETS * SEG // RUN
NT = 16
NY = 4
OWN = 8
BROWS = 16
NBLK = NY * NT
ZROWS = (TROWS // OWN + 1) * NT
BF = jnp.bfloat16
F32 = jnp.float32


def split_np(a):
    hi = a.astype(np.float32).astype(ml_dtypes.bfloat16)
    lo = (a - hi.astype(np.float64)).astype(np.float32).astype(ml_dtypes.bfloat16)
    return hi, lo


def tables():
    j = np.arange(CHUNK)[:, None]
    k = np.arange(FKEEP)[None, :]
    phi = 2.0 * np.pi * (j * k % SEG) / SEG
    basis = np.concatenate([np.cos(phi), np.sin(phi)], axis=1)
    c = np.arange(NCHUNK)[:, None]
    theta = 2.0 * np.pi * (c * CHUNK * k % SEG) / SEG
    twiddle = np.concatenate([np.cos(theta), np.sin(theta)], axis=1).astype(np.float32)
    scale = np.where(np.arange(FKEEP) == 0, 1.0 / SEG, 2.0 / SEG)
    synth = basis.T * np.concatenate([scale, scale])[:, None]
    return np.concatenate(split_np(basis)), np.concatenate(split_np(synth)), twiddle


def beam_taps():
    values = [math.exp(-(m * m) / 4.5) for m in range(-RADIUS, RADIUS + 1)]
    total = sum(values)
    return [v / total for v in values]


def split(a):
    hi = a.astype(BF)
    return hi, (a - hi.astype(F32)).astype(BF)


def mm(a, b):
    return jnp.dot(a, b, preferred_element_type=F32)


def mm0(a, b):
    return lax.dot_general(
        a, b, (((0,), (0,)), ((), ())), precision=lax.Precision.HIGHEST,
        preferred_element_type=F32,
    )


def mm0_split(a, b):
    ah, al = split(a)
    bh, bl = split(b)
    return lax.dot_general(
        jnp.concatenate([ah, al, ah], axis=0), jnp.concatenate([bh, bh, bl], axis=0),
        (((0,), (0,)), ((), ())), preferred_element_type=F32,
    )


def column(row, n):
    full = jnp.broadcast_to(row, (n, row.shape[1]))
    same = lax.broadcasted_iota(jnp.int32, full.shape, 0) == lax.broadcasted_iota(
        jnp.int32, full.shape, 1
    )
    return jnp.sum(jnp.where(same, full, 0.0), axis=1, keepdims=True)


def analysis_kernel(
    x_hbm, t_hbm, v_hbm, basis_hbm, synth_hbm, tw_hbm,
    out_ref, x_ref, synth_ref, tw_ref, tt_ref, w_ref,
    t_ref, v_ref, basis_ref, sems,
):
    pieces = [
        (x_hbm.at[:, pl.ds(n * XPIECE, XPIECE)], x_ref.at[:, pl.ds(n * XPIECE, XPIECE)])
        for n in range(SEG // XPIECE)
    ]
    copies = [
        pltpu.make_async_copy(src, dst, sems.at[n])
        for n, (src, dst) in enumerate(
            [
                (t_hbm, t_ref), (v_hbm, v_ref), (basis_hbm, basis_ref), *pieces,
                (tw_hbm, tw_ref), (synth_hbm, synth_ref),
            ]
        )
    ]
    for copy in copies:
        copy.start()
    copies[0].wait()
    copies[1].wait()
    w = column(v_ref[...].astype(F32), DETS)
    t = t_ref[...]
    wt = t * w
    w_ref[...] = jnp.broadcast_to(w, (DETS, 128))
    tt_ref[...] = t.T
    gram = mm0(wt, t)
    out_ref[:, 2 * FKEEP :] = jnp.concatenate(
        [gram, jnp.zeros((NMODE, FKEEP - NMODE), F32)], axis=1
    )
    copies[2].wait()
    eh = basis_ref[:CHUNK, :]
    el = basis_ref[CHUNK:, :]
    ys = []
    per = XPIECE // CHUNK
    for n in range(SEG // XPIECE):
        copies[3 + n].wait()
        x = jnp.concatenate(
            [x_ref[:, c * CHUNK : (c + 1) * CHUNK] for c in range(n * per, (n + 1) * per)], axis=0
        )
        hi, lo = split(x)
        ys.append(mm(hi, eh) + mm(lo, eh) + mm(hi, el))
    copies[-2].wait()
    re = jnp.zeros((DETS, FKEEP), F32)
    im = jnp.zeros((DETS, FKEEP), F32)
    for c in range(NCHUNK):
        sl = slice(c % per * DETS, (c % per + 1) * DETS)
        yc = ys[c // per][sl, :FKEEP]
        yi = ys[c // per][sl, FKEEP:]
        cos = tw_ref[c : c + 1, :FKEEP]
        sin = tw_ref[c : c + 1, FKEEP:]
        re = re + (cos * yc - sin * yi)
        im = im + (sin * yc + cos * yi)
    out_ref[:, : 2 * FKEEP] = mm0_split(wt, jnp.concatenate([re, im], axis=1))
    copies[-1].wait()


def edge_col(lane):
    slot = lane >> 3
    return jnp.where(slot < 3, TCOLS - RADIUS + slot, slot - 3)


def ids_of_blocks(core):
    l = lax.broadcasted_iota(jnp.int32, (NBLK * BROWS, 128), 0)
    i = l & (BROWS - 1)
    b = l >> 4
    row = (b >> 4) * (2 * OWN) + core * OWN - RADIUS + i
    ok = (i < OWN + 2 * RADIUS) & (row >= 0) & (row < TROWS)
    return jnp.where(ok, (b & (NT - 1)) * TROWS + row, -1)


def run_row(ids):
    flat = ids.astype(F32).T
    parts = [flat[c : c + 1, :] for c in range(SEG // RUN)]
    return jnp.concatenate(parts, axis=1).astype(jnp.int32)


def fill_hot(ref, ids, line):
    for q in range(NRUNS // 128):
        sl = slice(q * 128, (q + 1) * 128)
        ref[:, sl] = jnp.where(ids == line[:, sl], 1.0, 0.0).astype(BF)


def first_index_kernel(
    core_ref, ti_hbm, ro_hbm, cs_hbm,
    send_ref, line_ref, zid_ref, ro_ref, cs_ref, ti_ref, sems,
):
    copies = [
        pltpu.make_async_copy(src, dst, sems.at[n])
        for n, (src, dst) in enumerate(((ti_hbm, ti_ref), (ro_hbm, ro_ref), (cs_hbm, cs_ref)))
    ]
    for copy in copies:
        copy.start()
    ids = ids_of_blocks(core_ref[0] ^ 1)
    for copy in copies:
        copy.wait()
    ti = ti_ref[...]
    ro = ro_ref[...]
    line = run_row(ti * TROWS + ro)
    line_ref[...] = line
    zid_ref[...] = run_row(((ro + RADIUS) >> 3) * NT + ti)
    fill_hot(send_ref, ids, line)


def second_index_kernel(
    core_ref, line_ref, zid_ref, ro_ref, cs_ref, w_ref,
    keep_ref, zhot_ref, idx_ref, edge_ref, mask_ref, zh_ref,
):
    zl = lax.broadcasted_iota(jnp.int32, (ZROWS, NRUNS), 0)
    zhot = jnp.where(zl == zid_ref[...], 1.0, 0.0).astype(BF)
    zhot_ref[...] = zhot
    w = w_ref[...]
    lane = lax.broadcasted_iota(jnp.int32, (DETS, 128), 1)
    ecol = edge_col(lane)
    hparts = []
    for c in range(SEG // RUN):
        sl = slice(c * DETS, (c + 1) * DETS)
        cs = jnp.broadcast_to(cs_ref[:, c : c + 1], (DETS, 128))
        ro = jnp.broadcast_to(ro_ref[:, c : c + 1], (DETS, 128))
        idx_ref[sl, :] = (lane - cs) & (TCOLS - 1)
        edge_ref[sl, :] = (ecol - cs) & (TCOLS - 1)
        here = ((ro + RADIUS) & (OWN - 1)) == (lane & (OWN - 1))
        mask_ref[sl, :] = jnp.where(here & (lane < 48), 1.0, 0.0)
        hparts.append(jnp.where(here & (lane >= 48) & (lane < 56), w, 0.0).astype(BF))
    zh_ref[...] = mm(zhot, jnp.concatenate(hparts, axis=0))
    fill_hot(keep_ref, ids_of_blocks(core_ref[0]), line_ref[...])


def lanes_of(v, k):
    return jnp.broadcast_to(v[:, k : k + 1], (8, 128))


def row_of(v, r):
    return jnp.broadcast_to(v[r : r + 1, :], (8, 128))


def solve(gram, rhs):
    n = gram.shape[0]
    eye = lax.broadcasted_iota(jnp.int32, gram.shape, 0) == lax.broadcasted_iota(
        jnp.int32, gram.shape, 1
    )
    diag = jnp.where(eye, gram, 0.0)
    down = lax.rsqrt(jnp.sum(diag, axis=1, keepdims=True))
    along = lax.rsqrt(jnp.sum(diag, axis=0, keepdims=True))
    full = jnp.concatenate(
        [gram * down * along, rhs * down, jnp.zeros((n, 128 - 2 * n), F32)], axis=1
    )
    a = [full[8 * i : 8 * i + 8, :] for i in range(n // 8)]
    sub = lax.broadcasted_iota(jnp.int32, (8, 128), 0)
    for k in range(0, n, 4):
        here, r = k // 8, k % 8
        c = [[lanes_of(v, k + j) for v in a] for j in range(4)]
        p = [[row_of(c[j][here], r + i) for j in range(4)] for i in range(4)]
        rows = [row_of(a[here], r + i) for i in range(4)]
        i1 = 1.0 / (p[0][0] * p[1][1] - p[0][1] * p[0][1])
        e00, e01, e11 = p[1][1] * i1, -p[0][1] * i1, p[0][0] * i1
        w00 = e00 * p[0][2] + e01 * p[1][2]
        w01 = e00 * p[0][3] + e01 * p[1][3]
        w10 = e01 * p[0][2] + e11 * p[1][2]
        w11 = e01 * p[0][3] + e11 * p[1][3]
        s00 = p[2][2] - (p[0][2] * w00 + p[1][2] * w10)
        s01 = p[2][3] - (p[0][2] * w01 + p[1][2] * w11)
        s11 = p[3][3] - (p[0][3] * w01 + p[1][3] * w11)
        i2 = 1.0 / (s00 * s11 - s01 * s01)
        y0 = e00 * rows[0] + e01 * rows[1]
        y1 = e01 * rows[0] + e11 * rows[1]
        q2 = rows[2] - (p[0][2] * y0 + p[1][2] * y1)
        q3 = rows[3] - (p[0][3] * y0 + p[1][3] * y1)
        n2 = (s11 * q2 - s01 * q3) * i2
        n3 = (s00 * q3 - s01 * q2) * i2
        n0 = y0 - (w00 * n2 + w01 * n3)
        n1 = y1 - (w10 * n2 + w11 * n3)
        for i in range(n // 8):
            a[i] = a[i] - ((c[0][i] * n0 + c[1][i] * n1) + (c[2][i] * n2 + c[3][i] * n3))
        for j, new in enumerate((n0, n1, n2, n3)):
            a[here] = jnp.where(sub == r + j, new, a[here])
    return jnp.concatenate(a, axis=0)[:, n : 2 * n] * down


def shifted_tiles(z, by):
    zero = jnp.zeros((z.shape[0], 1, 128), F32)
    if by < 0:
        return jnp.concatenate([zero, z[:, :-1]], axis=1)
    return jnp.concatenate([z[:, 1:], zero], axis=1)


def clean_kernel(
    core_ref, p_ref, q_ref, r_ref, s_ref, tt_ref, w_ref, x_ref, synth_ref, tw_ref,
    idx_ref, edge_ref, mask_ref, zhot_ref, zh_ref, send_hot_ref,
    clean_ref, send_ref, vals_ref, rows_ref,
):
    w = w_ref[...]
    w = jnp.concatenate([w, w], axis=1)
    p = (p_ref[...] + q_ref[...]) + (r_ref[...] + s_ref[...])
    eye = lax.broadcasted_iota(jnp.int32, (NMODE, NMODE), 0) == lax.broadcasted_iota(
        jnp.int32, (NMODE, NMODE), 1
    )
    gram = p[:, 2 * FKEEP : 2 * FKEEP + NMODE] + jnp.where(eye, 0.05, 0.0)
    coef = solve(gram, tt_ref[...])
    ab = mm0_split(coef, p[:, : 2 * FKEEP])
    a = ab[:, :FKEEP]
    b = ab[:, FKEEP:]
    parts = []
    for c in range(NCHUNK):
        cos = tw_ref[c : c + 1, :FKEEP]
        sin = tw_ref[c : c + 1, FKEEP:]
        parts.append(jnp.concatenate([a * cos + b * sin, b * cos - a * sin], axis=1))
    hi, lo = split(jnp.concatenate(parts, axis=0))
    sh = synth_ref[:CHUNK, :]
    low = mm(hi, sh) + mm(lo, sh) + mm(hi, synth_ref[CHUNK:, :])
    runs = []
    for c in range(NCHUNK):
        part = w * (x_ref[:, c * CHUNK : (c + 1) * CHUNK] - low[c * DETS : (c + 1) * DETS, :])
        clean_ref[:, c * CHUNK : (c + 1) * CHUNK] = part
        runs.append(part[:, :RUN])
        runs.append(part[:, RUN:])
    run = jnp.concatenate(runs, axis=0)
    vals = jnp.concatenate(
        split(jnp.take_along_axis(run, idx_ref[...], axis=1, mode="promise_in_bounds")), axis=1
    )
    vals_ref[...] = vals
    evals = jnp.take_along_axis(run, edge_ref[...], axis=1, mode="promise_in_bounds")
    evals = jnp.concatenate(split(evals * mask_ref[...]), axis=1)
    z = mm(zhot_ref[...], evals)
    z = (z[:, :128] + z[:, 128:] + zh_ref[...]).reshape(ZROWS // NT, NT, 128)
    left = shifted_tiles(z, -1)
    right = shifted_tiles(z, 1)
    lane = lax.broadcasted_iota(jnp.int32, z.shape, 2)
    left_hits = left
    right_hits = jnp.concatenate([jnp.zeros(z.shape[:2] + (8,), F32), right[:, :, :-8]], axis=2)
    near = jnp.where(
        lane < 24, left, jnp.where(lane < 48, right, jnp.where(lane < 56, left_hits, right_hits))
    )
    near = jnp.where(lane < 64, near, 0.0)
    mine = jnp.where((lane >= 48) & (lane < 56), z, 0.0)
    nd = TROWS // OWN

    def both(v):
        return v[:nd] + jnp.concatenate([jnp.zeros((nd, NT, 64), F32), v[1:, :, :64]], axis=2)

    rows14 = both(near)
    rows15 = both(mine)
    core = core_ref[0]

    def pick(v, which):
        return jnp.concatenate(
            [jnp.where(which == 1, v[2 * y + 1], v[2 * y]) for y in range(NY)], axis=0
        )

    rows_ref[0:NBLK, :] = pick(rows14, core)
    rows_ref[NBLK : 2 * NBLK, :] = pick(rows15, core)
    s = mm(send_hot_ref[...], vals)
    send_ref[...] = s[:, :128] + s[:, 128:]
    send_ref[pl.ds(14, NBLK, stride=BROWS), :] = pick(rows14, core ^ 1)
    send_ref[pl.ds(15, NBLK, stride=BROWS), :] = pick(rows15, core ^ 1)


def keep_kernel(hot_ref, vals_ref, rows_ref, clean_ref, keep_ref, out_hbm, sem):
    copy = pltpu.make_async_copy(clean_ref, out_hbm, sem)
    copy.start()
    s = mm(hot_ref[...], vals_ref[...])
    keep_ref[...] = s[:, :128] + s[:, 128:]
    keep_ref[pl.ds(14, NBLK, stride=BROWS), :] = rows_ref[0:NBLK, :]
    keep_ref[pl.ds(15, NBLK, stride=BROWS), :] = rows_ref[NBLK : 2 * NBLK, :]
    copy.wait()


def beam_kernel(blocks_ref, out_ref):
    sums = [blocks_ref[b * BROWS : (b + 1) * BROWS, :] for b in range(4)]
    for b in range(4, NBLK):
        sums[b % 4] = sums[b % 4] + blocks_ref[b * BROWS : (b + 1) * BROWS, :]
    total = (sums[0] + sums[1]) + (sums[2] + sums[3])
    near = jnp.broadcast_to(total[14:15, :], (BROWS, 128))
    mine = jnp.broadcast_to(total[15:16, :], (BROWS, 128))
    i = lax.broadcasted_iota(jnp.int32, (BROWS, 128), 0)
    lane = lax.broadcasted_iota(jnp.int32, (BROWS, 128), 1)
    spot = jnp.where(i < OWN, i, 64 + i - OWN)

    def take(src, slot):
        return jnp.sum(jnp.where(lane == spot + 8 * slot, src, 0.0), axis=1, keepdims=True)

    left_hits = take(near, 6) + 1.0
    right_hits = take(near, 7) + 1.0
    hits = take(mine, 6) + 1.0
    valid = i < OWN + 2 * RADIUS
    binned = jnp.where(valid, total / hits, 0.0)
    left = [take(near, m) / left_hits for m in range(RADIUS)]
    right = [take(near, RADIUS + m) / right_hits for m in range(RADIUS)]
    taps = beam_taps()
    smooth = taps[RADIUS] * binned
    for m in range(1, RADIUS + 1):
        moved = pltpu.roll(binned, m, 1)
        for q in range(m):
            moved = jnp.where(lane == q, left[RADIUS - m + q], moved)
        smooth = smooth + taps[RADIUS - m] * moved
        moved = pltpu.roll(binned, TCOLS - m, 1)
        for q in range(m):
            moved = jnp.where(lane == TCOLS - m + q, right[q], moved)
        smooth = smooth + taps[RADIUS + m] * moved
    out = taps[0] * smooth[0:OWN, :]
    for m in range(1, 2 * RADIUS + 1):
        out = out + taps[m] * smooth[m : m + OWN, :]
    out_ref[...] = out


VMEM = pl.BlockSpec(memory_space=pltpu.VMEM)
SMEM = pl.BlockSpec(memory_space=pltpu.SMEM)
HBM = pl.BlockSpec(memory_space=pltpu.HBM)


def call(kernel, outs, specs, name, flops, *args, out_specs=None, scratch=()):
    args = [
        pltpu.with_memory_space_constraint(a, pltpu.HBM) if spec is HBM else a
        for a, spec in zip(args, specs)
    ]
    nbytes = sum(math.prod(s.shape) * 4 for s in outs) + sum(a.size * 4 for a in args)
    return pl.pallas_call(
        kernel,
        out_shape=outs,
        in_specs=specs,
        out_specs=out_specs or [VMEM] * len(outs),
        scratch_shapes=list(scratch),
        name=name,
        compiler_params=pltpu.CompilerParams(vmem_limit_bytes=40 << 20),
        cost_estimate=pl.CostEstimate(flops=flops, bytes_accessed=nbytes, transcendentals=0),
    )(*args)


def sds(shape, dtype=F32):
    return jax.ShapeDtypeStruct(shape, dtype)


I32 = jnp.int32


def body(timestreams, templates, validity, tile_index, row_offset, col_start):
    basis, synth, tw = tables()
    core = lax.axis_index("core").reshape(1)
    part, x, synth, tw, tt, w = call(
        analysis_kernel,
        [
            sds((NMODE, 3 * FKEEP)), sds((DETS, SEG)), sds((2 * CHUNK, 2 * FKEEP), BF),
            sds((NCHUNK, 2 * FKEEP)), sds((NMODE, DETS)), sds((DETS, 128)),
        ],
        [HBM] * 6, "analysis", 400_000_000,
        timestreams, templates, validity.reshape(1, DETS),
        jnp.asarray(basis), jnp.asarray(synth), jnp.asarray(tw),
        scratch=[
            pltpu.VMEM((DETS, NMODE), F32), pltpu.VMEM((1, DETS), I32),
            pltpu.VMEM((2 * CHUNK, 2 * FKEEP), BF), pltpu.SemaphoreType.DMA((5 + SEG // XPIECE,)),
        ],
    )
    part = part + lax.ppermute(part, "core", [(0, 1), (1, 0)])
    tile_index, row_offset, col_start, part = lax.optimization_barrier(
        (tile_index, row_offset, col_start, part)
    )
    others = [lax.ppermute(part, "y", [(k, k ^ m) for k in range(NY)]) for m in (2, 3, 1)]
    big = (NBLK * BROWS, NRUNS)
    send_hot, line, zid, ro, cs = call(
        first_index_kernel,
        [
            sds(big, BF), sds((1, NRUNS), I32), sds((1, NRUNS), I32),
            sds((DETS, SEG // RUN), I32), sds((DETS, SEG // RUN), I32),
        ],
        [SMEM] + [HBM] * 3, "index1", 100_000_000,
        core, tile_index, row_offset, col_start,
        scratch=[pltpu.VMEM((DETS, SEG // RUN), I32), pltpu.SemaphoreType.DMA((3,))],
    )
    keep_hot, zhot, idx, edge, mask, zh = call(
        second_index_kernel,
        [
            sds(big, BF), sds((ZROWS, NRUNS), BF),
            sds((NRUNS, 128), I32), sds((NRUNS, 128), I32),
            sds((NRUNS, 128)), sds((ZROWS, 128)),
        ],
        [SMEM] + [VMEM] * 5, "index2", 100_000_000,
        core, line, zid, ro, cs, w,
    )
    cleaned, send, vals, rows = call(
        clean_kernel,
        [
            sds((DETS, SEG)), sds((NBLK * BROWS, 128)),
            sds((NRUNS, 256), BF), sds((2 * NBLK, 128)),
        ],
        [SMEM] + [VMEM] * 15, "clean", 1_000_000_000,
        core, part, *others, tt, w, x, synth, tw, idx, edge, mask, zhot, zh, send_hot,
    )
    got = lax.ppermute(send, "core", [(0, 1), (1, 0)])
    keep, cleaned = call(
        keep_kernel, [sds((NBLK * BROWS, 128)), sds((DETS, SEG))], [VMEM] * 4, "keep",
        500_000_000, keep_hot, vals, rows, cleaned,
        out_specs=[VMEM, HBM], scratch=[pltpu.SemaphoreType.DMA],
    )
    blocks = lax.all_to_all(keep + got, ("y", "z", "x"), 0, 0, tiled=True)
    (beamed,) = call(
        beam_kernel, [sds((OWN, TCOLS))], [VMEM], "beam", 1_000_000, blocks
    )
    return (cleaned, beamed)


def solution(mesh):
    fine = Mesh(mesh.devices.reshape(NY, 2, 4, 4), ("y", "core", "z", "x"))
    det, tm = ("y", "core"), ("z", "x")
    in_specs = (P(det, tm), P(det, None), P(det), P(det, tm), P(det, tm), P(det, tm))
    out_specs = (P(det, tm), P(det, tm))
    return jax.shard_map(body, mesh=fine, in_specs=in_specs, out_specs=out_specs, check_vma=False)
```

```python
import math

import jax
import jax.numpy as jnp
import numpy as np
from jax import lax
from jax.experimental import pallas as pl
from jax.experimental.pallas import tpu as pltpu
from jax.sharding import Mesh
from jax.sharding import PartitionSpec as P
import ml_dtypes

SEG = 4096
NMODE = 32
FKEEP = 128
RUN = 128
TROWS = 64
TCOLS = 128
RADIUS = 3
DETS = 32
CHUNK = 256
NCHUNK = SEG // CHUNK
XPIECE = 4096
NRUNS = DETS * SEG // RUN
NT = 16
NY = 4
OWN = 8
BROWS = 16
NBLK = NY * NT
ZROWS = (TROWS // OWN + 1) * NT
BF = jnp.bfloat16
F32 = jnp.float32


def split_np(a):
    hi = a.astype(np.float32).astype(ml_dtypes.bfloat16)
    lo = (a - hi.astype(np.float64)).astype(np.float32).astype(ml_dtypes.bfloat16)
    return hi, lo


def tables():
    j = np.arange(CHUNK)[:, None]
    k = np.arange(FKEEP)[None, :]
    phi = 2.0 * np.pi * (j * k % SEG) / SEG
    basis = np.concatenate([np.cos(phi), np.sin(phi)], axis=1)
    c = np.arange(NCHUNK)[:, None]
    theta = 2.0 * np.pi * (c * CHUNK * k % SEG) / SEG
    twiddle = np.concatenate([np.cos(theta), np.sin(theta)], axis=1).astype(np.float32)
    scale = np.where(np.arange(FKEEP) == 0, 1.0 / SEG, 2.0 / SEG)
    synth = basis.T * np.concatenate([scale, scale])[:, None]
    return np.concatenate(split_np(basis)), np.concatenate(split_np(synth)), twiddle


def beam_taps():
    values = [math.exp(-(m * m) / 4.5) for m in range(-RADIUS, RADIUS + 1)]
    total = sum(values)
    return [v / total for v in values]


def split(a):
    hi = a.astype(BF)
    return hi, (a - hi.astype(F32)).astype(BF)


def mm(a, b):
    return jnp.dot(a, b, preferred_element_type=F32)


def mm0(a, b):
    return lax.dot_general(
        a, b, (((0,), (0,)), ((), ())), precision=lax.Precision.HIGHEST,
        preferred_element_type=F32,
    )


def mm0_split(a, b):
    ah, al = split(a)
    bh, bl = split(b)
    return lax.dot_general(
        jnp.concatenate([ah, al, ah], axis=0), jnp.concatenate([bh, bh, bl], axis=0),
        (((0,), (0,)), ((), ())), preferred_element_type=F32,
    )


def column(row, n):
    full = jnp.broadcast_to(row, (n, row.shape[1]))
    same = lax.broadcasted_iota(jnp.int32, full.shape, 0) == lax.broadcasted_iota(
        jnp.int32, full.shape, 1
    )
    return jnp.sum(jnp.where(same, full, 0.0), axis=1, keepdims=True)


def run_row(ids):
    flat = ids.astype(F32).T
    parts = [flat[c : c + 1, :] for c in range(SEG // RUN)]
    return jnp.concatenate(parts, axis=1).astype(jnp.int32)


def analysis_kernel(
    x_hbm, t_hbm, v_hbm, ti_hbm, ro_hbm, cs_hbm, basis_hbm, synth_hbm, tw_hbm,
    out_ref, x_ref, synth_ref, tw_ref, tt_ref, w_ref, ro_ref, cs_ref, line_ref, zid_ref,
    t_ref, v_ref, ti_ref, basis_ref, sems,
):
    pieces = [
        (x_hbm.at[:, pl.ds(n * XPIECE, XPIECE)], x_ref.at[:, pl.ds(n * XPIECE, XPIECE)])
        for n in range(SEG // XPIECE)
    ]
    copies = [
        pltpu.make_async_copy(src, dst, sems.at[n])
        for n, (src, dst) in enumerate(
            [
                (t_hbm, t_ref), (v_hbm, v_ref), (basis_hbm, basis_ref), *pieces,
                (ti_hbm, ti_ref), (ro_hbm, ro_ref), (cs_hbm, cs_ref),
                (tw_hbm, tw_ref), (synth_hbm, synth_ref),
            ]
        )
    ]
    for copy in copies:
        copy.start()
    copies[0].wait()
    copies[1].wait()
    w = column(v_ref[...].astype(F32), DETS)
    t = t_ref[...]
    wt = t * w
    w_ref[...] = jnp.broadcast_to(w, (DETS, 128))
    tt_ref[...] = t.T
    gram = mm0(wt, t)
    out_ref[:, 2 * FKEEP :] = jnp.concatenate(
        [gram, jnp.zeros((NMODE, FKEEP - NMODE), F32)], axis=1
    )
    for copy in copies[-5:-2]:
        copy.wait()
    ti = ti_ref[...]
    ro = ro_ref[...]
    line_ref[...] = run_row(ti * TROWS + ro)
    zid_ref[...] = run_row(((ro + RADIUS) >> 3) * NT + ti)
    copies[2].wait()
    eh = basis_ref[:CHUNK, :]
    el = basis_ref[CHUNK:, :]
    ys = []
    per = XPIECE // CHUNK
    for n in range(SEG // XPIECE):
        copies[3 + n].wait()
        x = jnp.concatenate(
            [x_ref[:, c * CHUNK : (c + 1) * CHUNK] for c in range(n * per, (n + 1) * per)], axis=0
        )
        hi, lo = split(x)
        ys.append(mm(hi, eh) + mm(lo, eh) + mm(hi, el))
    copies[-2].wait()
    re = jnp.zeros((DETS, FKEEP), F32)
    im = jnp.zeros((DETS, FKEEP), F32)
    for c in range(NCHUNK):
        sl = slice(c % per * DETS, (c % per + 1) * DETS)
        yc = ys[c // per][sl, :FKEEP]
        yi = ys[c // per][sl, FKEEP:]
        cos = tw_ref[c : c + 1, :FKEEP]
        sin = tw_ref[c : c + 1, FKEEP:]
        re = re + (cos * yc - sin * yi)
        im = im + (sin * yc + cos * yi)
    out_ref[:, : 2 * FKEEP] = mm0_split(wt, jnp.concatenate([re, im], axis=1))
    copies[-1].wait()


def edge_col(lane):
    slot = lane >> 3
    return jnp.where(slot < 3, TCOLS - RADIUS + slot, slot - 3)


def ids_of_blocks(core):
    l = lax.broadcasted_iota(jnp.int32, (NBLK * BROWS, 128), 0)
    i = l & (BROWS - 1)
    b = l >> 4
    row = (b >> 4) * (2 * OWN) + core * OWN - RADIUS + i
    ok = (i < OWN + 2 * RADIUS) & (row >= 0) & (row < TROWS)
    return jnp.where(ok, (b & (NT - 1)) * TROWS + row, -1)


def fill_hot(ref, ids, line):
    for q in range(NRUNS // 128):
        sl = slice(q * 128, (q + 1) * 128)
        ref[:, sl] = jnp.where(ids == line[:, sl], 1.0, 0.0).astype(BF)


def first_index_kernel(core_ref, line_ref, send_ref):
    fill_hot(send_ref, ids_of_blocks(core_ref[0] ^ 1), line_ref[...])


def second_index_kernel(
    core_ref, line_ref, zid_ref, ro_ref, cs_ref, w_ref,
    keep_ref, zhot_ref, idx_ref, edge_ref, mask_ref, zh_ref,
):
    zl = lax.broadcasted_iota(jnp.int32, (ZROWS, NRUNS), 0)
    zhot = jnp.where(zl == zid_ref[...], 1.0, 0.0).astype(BF)
    zhot_ref[...] = zhot
    w = w_ref[...]
    lane = lax.broadcasted_iota(jnp.int32, (DETS, 128), 1)
    ecol = edge_col(lane)
    hparts = []
    for c in range(SEG // RUN):
        sl = slice(c * DETS, (c + 1) * DETS)
        cs = jnp.broadcast_to(cs_ref[:, c : c + 1], (DETS, 128))
        ro = jnp.broadcast_to(ro_ref[:, c : c + 1], (DETS, 128))
        idx_ref[sl, :] = (lane - cs) & (TCOLS - 1)
        edge_ref[sl, :] = (ecol - cs) & (TCOLS - 1)
        here = ((ro + RADIUS) & (OWN - 1)) == (lane & (OWN - 1))
        mask_ref[sl, :] = jnp.where(here & (lane < 48), 1.0, 0.0)
        hparts.append(jnp.where(here & (lane >= 48) & (lane < 56), w, 0.0).astype(BF))
    zh_ref[...] = mm(zhot, jnp.concatenate(hparts, axis=0))
    fill_hot(keep_ref, ids_of_blocks(core_ref[0]), line_ref[...])


def lanes_of(v, k):
    return jnp.broadcast_to(v[:, k : k + 1], (8, 128))


def row_of(v, r):
    return jnp.broadcast_to(v[r : r + 1, :], (8, 128))


def solve(gram, rhs):
    n = gram.shape[0]
    eye = lax.broadcasted_iota(jnp.int32, gram.shape, 0) == lax.broadcasted_iota(
        jnp.int32, gram.shape, 1
    )
    diag = jnp.where(eye, gram, 0.0)
    down = lax.rsqrt(jnp.sum(diag, axis=1, keepdims=True))
    along = lax.rsqrt(jnp.sum(diag, axis=0, keepdims=True))
    full = jnp.concatenate(
        [gram * down * along, rhs * down, jnp.zeros((n, 128 - 2 * n), F32)], axis=1
    )
    a = [full[8 * i : 8 * i + 8, :] for i in range(n // 8)]
    sub = lax.broadcasted_iota(jnp.int32, (8, 128), 0)
    for k in range(0, n, 4):
        here, r = k // 8, k % 8
        c = [[lanes_of(v, k + j) for v in a] for j in range(4)]
        p = [[row_of(c[j][here], r + i) for j in range(4)] for i in range(4)]
        rows = [row_of(a[here], r + i) for i in range(4)]
        i1 = 1.0 / (p[0][0] * p[1][1] - p[0][1] * p[0][1])
        e00, e01, e11 = p[1][1] * i1, -p[0][1] * i1, p[0][0] * i1
        w00 = e00 * p[0][2] + e01 * p[1][2]
        w01 = e00 * p[0][3] + e01 * p[1][3]
        w10 = e01 * p[0][2] + e11 * p[1][2]
        w11 = e01 * p[0][3] + e11 * p[1][3]
        s00 = p[2][2] - (p[0][2] * w00 + p[1][2] * w10)
        s01 = p[2][3] - (p[0][2] * w01 + p[1][2] * w11)
        s11 = p[3][3] - (p[0][3] * w01 + p[1][3] * w11)
        i2 = 1.0 / (s00 * s11 - s01 * s01)
        y0 = e00 * rows[0] + e01 * rows[1]
        y1 = e01 * rows[0] + e11 * rows[1]
        q2 = rows[2] - (p[0][2] * y0 + p[1][2] * y1)
        q3 = rows[3] - (p[0][3] * y0 + p[1][3] * y1)
        n2 = (s11 * q2 - s01 * q3) * i2
        n3 = (s00 * q3 - s01 * q2) * i2
        n0 = y0 - (w00 * n2 + w01 * n3)
        n1 = y1 - (w10 * n2 + w11 * n3)
        for i in range(n // 8):
            a[i] = a[i] - ((c[0][i] * n0 + c[1][i] * n1) + (c[2][i] * n2 + c[3][i] * n3))
        for j, new in enumerate((n0, n1, n2, n3)):
            a[here] = jnp.where(sub == r + j, new, a[here])
    return jnp.concatenate(a, axis=0)[:, n : 2 * n] * down


def shifted_tiles(z, by):
    zero = jnp.zeros((z.shape[0], 1, 128), F32)
    if by < 0:
        return jnp.concatenate([zero, z[:, :-1]], axis=1)
    return jnp.concatenate([z[:, 1:], zero], axis=1)


def clean_kernel(
    core_ref, p_ref, q_ref, r_ref, s_ref, tt_ref, w_ref, x_ref, synth_ref, tw_ref,
    idx_ref, edge_ref, mask_ref, zhot_ref, zh_ref, send_hot_ref,
    clean_ref, send_ref, vals_ref, rows_ref,
):
    w = w_ref[...]
    w = jnp.concatenate([w, w], axis=1)
    p = (p_ref[...] + q_ref[...]) + (r_ref[...] + s_ref[...])
    eye = lax.broadcasted_iota(jnp.int32, (NMODE, NMODE), 0) == lax.broadcasted_iota(
        jnp.int32, (NMODE, NMODE), 1
    )
    gram = p[:, 2 * FKEEP : 2 * FKEEP + NMODE] + jnp.where(eye, 0.05, 0.0)
    coef = solve(gram, tt_ref[...])
    ab = mm0_split(coef, p[:, : 2 * FKEEP])
    a = ab[:, :FKEEP]
    b = ab[:, FKEEP:]
    parts = []
    for c in range(NCHUNK):
        cos = tw_ref[c : c + 1, :FKEEP]
        sin = tw_ref[c : c + 1, FKEEP:]
        parts.append(jnp.concatenate([a * cos + b * sin, b * cos - a * sin], axis=1))
    hi, lo = split(jnp.concatenate(parts, axis=0))
    sh = synth_ref[:CHUNK, :]
    low = mm(hi, sh) + mm(lo, sh) + mm(hi, synth_ref[CHUNK:, :])
    runs = []
    for c in range(NCHUNK):
        part = w * (x_ref[:, c * CHUNK : (c + 1) * CHUNK] - low[c * DETS : (c + 1) * DETS, :])
        clean_ref[:, c * CHUNK : (c + 1) * CHUNK] = part
        runs.append(part[:, :RUN])
        runs.append(part[:, RUN:])
    run = jnp.concatenate(runs, axis=0)
    vals = jnp.concatenate(
        split(jnp.take_along_axis(run, idx_ref[...], axis=1, mode="promise_in_bounds")), axis=1
    )
    vals_ref[...] = vals
    evals = jnp.take_along_axis(run, edge_ref[...], axis=1, mode="promise_in_bounds")
    evals = jnp.concatenate(split(evals * mask_ref[...]), axis=1)
    z = mm(zhot_ref[...], evals)
    z = (z[:, :128] + z[:, 128:] + zh_ref[...]).reshape(ZROWS // NT, NT, 128)
    left = shifted_tiles(z, -1)
    right = shifted_tiles(z, 1)
    lane = lax.broadcasted_iota(jnp.int32, z.shape, 2)
    left_hits = left
    right_hits = jnp.concatenate([jnp.zeros(z.shape[:2] + (8,), F32), right[:, :, :-8]], axis=2)
    near = jnp.where(
        lane < 24, left, jnp.where(lane < 48, right, jnp.where(lane < 56, left_hits, right_hits))
    )
    near = jnp.where(lane < 64, near, 0.0)
    mine = jnp.where((lane >= 48) & (lane < 56), z, 0.0)
    nd = TROWS // OWN

    def both(v):
        return v[:nd] + jnp.concatenate([jnp.zeros((nd, NT, 64), F32), v[1:, :, :64]], axis=2)

    rows14 = both(near)
    rows15 = both(mine)
    core = core_ref[0]

    def pick(v, which):
        return jnp.concatenate(
            [jnp.where(which == 1, v[2 * y + 1], v[2 * y]) for y in range(NY)], axis=0
        )

    rows_ref[0:NBLK, :] = pick(rows14, core)
    rows_ref[NBLK : 2 * NBLK, :] = pick(rows15, core)
    s = mm(send_hot_ref[...], vals)
    send_ref[...] = s[:, :128] + s[:, 128:]
    send_ref[pl.ds(14, NBLK, stride=BROWS), :] = pick(rows14, core ^ 1)
    send_ref[pl.ds(15, NBLK, stride=BROWS), :] = pick(rows15, core ^ 1)


def keep_kernel(hot_ref, vals_ref, rows_ref, clean_ref, keep_ref, out_hbm, sem):
    copy = pltpu.make_async_copy(clean_ref, out_hbm, sem)
    copy.start()
    s = mm(hot_ref[...], vals_ref[...])
    keep_ref[...] = s[:, :128] + s[:, 128:]
    keep_ref[pl.ds(14, NBLK, stride=BROWS), :] = rows_ref[0:NBLK, :]
    keep_ref[pl.ds(15, NBLK, stride=BROWS), :] = rows_ref[NBLK : 2 * NBLK, :]
    copy.wait()


def beam_kernel(blocks_ref, out_ref):
    sums = [blocks_ref[b * BROWS : (b + 1) * BROWS, :] for b in range(4)]
    for b in range(4, NBLK):
        sums[b % 4] = sums[b % 4] + blocks_ref[b * BROWS : (b + 1) * BROWS, :]
    total = (sums[0] + sums[1]) + (sums[2] + sums[3])
    near = jnp.broadcast_to(total[14:15, :], (BROWS, 128))
    mine = jnp.broadcast_to(total[15:16, :], (BROWS, 128))
    i = lax.broadcasted_iota(jnp.int32, (BROWS, 128), 0)
    lane = lax.broadcasted_iota(jnp.int32, (BROWS, 128), 1)
    spot = jnp.where(i < OWN, i, 64 + i - OWN)

    def take(src, slot):
        return jnp.sum(jnp.where(lane == spot + 8 * slot, src, 0.0), axis=1, keepdims=True)

    left_hits = take(near, 6) + 1.0
    right_hits = take(near, 7) + 1.0
    hits = take(mine, 6) + 1.0
    valid = i < OWN + 2 * RADIUS
    binned = jnp.where(valid, total / hits, 0.0)
    left = [take(near, m) / left_hits for m in range(RADIUS)]
    right = [take(near, RADIUS + m) / right_hits for m in range(RADIUS)]
    taps = beam_taps()
    smooth = taps[RADIUS] * binned
    for m in range(1, RADIUS + 1):
        moved = pltpu.roll(binned, m, 1)
        for q in range(m):
            moved = jnp.where(lane == q, left[RADIUS - m + q], moved)
        smooth = smooth + taps[RADIUS - m] * moved
        moved = pltpu.roll(binned, TCOLS - m, 1)
        for q in range(m):
            moved = jnp.where(lane == TCOLS - m + q, right[q], moved)
        smooth = smooth + taps[RADIUS + m] * moved
    out = taps[0] * smooth[0:OWN, :]
    for m in range(1, 2 * RADIUS + 1):
        out = out + taps[m] * smooth[m : m + OWN, :]
    out_ref[...] = out


VMEM = pl.BlockSpec(memory_space=pltpu.VMEM)
SMEM = pl.BlockSpec(memory_space=pltpu.SMEM)
HBM = pl.BlockSpec(memory_space=pltpu.HBM)


def call(kernel, outs, specs, name, flops, *args, out_specs=None, scratch=()):
    args = [
        pltpu.with_memory_space_constraint(a, pltpu.HBM) if spec is HBM else a
        for a, spec in zip(args, specs)
    ]
    nbytes = sum(math.prod(s.shape) * 4 for s in outs) + sum(a.size * 4 for a in args)
    return pl.pallas_call(
        kernel,
        out_shape=outs,
        in_specs=specs,
        out_specs=out_specs or [VMEM] * len(outs),
        scratch_shapes=list(scratch),
        name=name,
        compiler_params=pltpu.CompilerParams(vmem_limit_bytes=40 << 20),
        cost_estimate=pl.CostEstimate(flops=flops, bytes_accessed=nbytes, transcendentals=0),
    )(*args)


def sds(shape, dtype=F32):
    return jax.ShapeDtypeStruct(shape, dtype)


I32 = jnp.int32


def body(timestreams, templates, validity, tile_index, row_offset, col_start):
    basis, synth, tw = tables()
    core = lax.axis_index("core").reshape(1)
    small = (DETS, SEG // RUN)
    big = (NBLK * BROWS, NRUNS)
    part, x, synth, tw, tt, w, ro, cs, line, zid = call(
        analysis_kernel,
        [
            sds((NMODE, 3 * FKEEP)), sds((DETS, SEG)), sds((2 * CHUNK, 2 * FKEEP), BF),
            sds((NCHUNK, 2 * FKEEP)), sds((NMODE, DETS)), sds((DETS, 128)),
            sds(small, I32), sds(small, I32), sds((1, NRUNS), I32), sds((1, NRUNS), I32),
        ],
        [HBM] * 9, "analysis", 400_000_000,
        timestreams, templates, validity.reshape(1, DETS), tile_index, row_offset, col_start,
        jnp.asarray(basis), jnp.asarray(synth), jnp.asarray(tw),
        scratch=[
            pltpu.VMEM((DETS, NMODE), F32), pltpu.VMEM((1, DETS), I32), pltpu.VMEM(small, I32),
            pltpu.VMEM((2 * CHUNK, 2 * FKEEP), BF), pltpu.SemaphoreType.DMA((8 + SEG // XPIECE,)),
        ],
    )
    other = lax.ppermute(part, "core", [(0, 1), (1, 0)])
    (send_hot,) = call(
        first_index_kernel, [sds(big, BF)], [SMEM, VMEM], "index1", 100_000_000, core, line
    )
    part, send_hot, line = lax.optimization_barrier((part + other, send_hot, line))
    others = [lax.ppermute(part, "y", [(k, k ^ m) for k in range(NY)]) for m in (2, 3, 1)]
    keep_hot, zhot, idx, edge, mask, zh = call(
        second_index_kernel,
        [
            sds(big, BF), sds((ZROWS, NRUNS), BF),
            sds((NRUNS, 128), I32), sds((NRUNS, 128), I32),
            sds((NRUNS, 128)), sds((ZROWS, 128)),
        ],
        [SMEM] + [VMEM] * 5, "index2", 100_000_000,
        core, line, zid, ro, cs, w,
    )
    cleaned, send, vals, rows = call(
        clean_kernel,
        [
            sds((DETS, SEG)), sds((NBLK * BROWS, 128)),
            sds((NRUNS, 256), BF), sds((2 * NBLK, 128)),
        ],
        [SMEM] + [VMEM] * 15, "clean", 1_000_000_000,
        core, part, *others, tt, w, x, synth, tw, idx, edge, mask, zhot, zh, send_hot,
    )
    got = lax.ppermute(send, "core", [(0, 1), (1, 0)])
    keep, cleaned = call(
        keep_kernel, [sds((NBLK * BROWS, 128)), sds((DETS, SEG))], [VMEM] * 4, "keep",
        500_000_000, keep_hot, vals, rows, cleaned,
        out_specs=[VMEM, HBM], scratch=[pltpu.SemaphoreType.DMA],
    )
    blocks = lax.all_to_all(keep + got, ("y", "z", "x"), 0, 0, tiled=True)
    (beamed,) = call(
        beam_kernel, [sds((OWN, TCOLS))], [VMEM], "beam", 1_000_000, blocks
    )
    return (cleaned, beamed)


def solution(mesh):
    fine = Mesh(mesh.devices.reshape(NY, 2, 4, 4), ("y", "core", "z", "x"))
    det, tm = ("y", "core"), ("z", "x")
    in_specs = (P(det, tm), P(det, None), P(det), P(det, tm), P(det, tm), P(det, tm))
    out_specs = (P(det, tm), P(det, tm))
    return jax.shard_map(body, mesh=fine, in_specs=in_specs, out_specs=out_specs, check_vma=False)
```

```python
import math

import jax
import jax.numpy as jnp
import numpy as np
from jax import lax
from jax.experimental import pallas as pl
from jax.experimental.pallas import tpu as pltpu
from jax.sharding import Mesh
from jax.sharding import PartitionSpec as P
import ml_dtypes

SEG = 4096
NMODE = 32
FKEEP = 128
RUN = 128
TROWS = 64
TCOLS = 128
RADIUS = 3
DETS = 32
CHUNK = 256
NCHUNK = SEG // CHUNK
XPIECE = 4096
NRUNS = DETS * SEG // RUN
NT = 16
NY = 4
OWN = 8
BROWS = 16
NBLK = NY * NT
ZROWS = (TROWS // OWN + 1) * NT
BF = jnp.bfloat16
F32 = jnp.float32


def split_np(a):
    hi = a.astype(np.float32).astype(ml_dtypes.bfloat16)
    lo = (a - hi.astype(np.float64)).astype(np.float32).astype(ml_dtypes.bfloat16)
    return hi, lo


def tables():
    j = np.arange(CHUNK)[:, None]
    k = np.arange(FKEEP)[None, :]
    phi = 2.0 * np.pi * (j * k % SEG) / SEG
    basis = np.concatenate([np.cos(phi), np.sin(phi)], axis=1)
    c = np.arange(NCHUNK)[:, None]
    theta = 2.0 * np.pi * (c * CHUNK * k % SEG) / SEG
    twiddle = np.concatenate([np.cos(theta), np.sin(theta)], axis=1).astype(np.float32)
    scale = np.where(np.arange(FKEEP) == 0, 1.0 / SEG, 2.0 / SEG)
    synth = basis.T * np.concatenate([scale, scale])[:, None]
    return np.concatenate(split_np(basis)), np.concatenate(split_np(synth)), twiddle


def beam_taps():
    values = [math.exp(-(m * m) / 4.5) for m in range(-RADIUS, RADIUS + 1)]
    total = sum(values)
    return [v / total for v in values]


def split(a):
    hi = a.astype(BF)
    return hi, (a - hi.astype(F32)).astype(BF)


def mm(a, b):
    return jnp.dot(a, b, preferred_element_type=F32)


def mm0(a, b):
    return lax.dot_general(
        a, b, (((0,), (0,)), ((), ())), precision=lax.Precision.HIGHEST,
        preferred_element_type=F32,
    )


def mm0_split(a, b):
    ah, al = split(a)
    bh, bl = split(b)
    return lax.dot_general(
        jnp.concatenate([ah, al, ah], axis=0), jnp.concatenate([bh, bh, bl], axis=0),
        (((0,), (0,)), ((), ())), preferred_element_type=F32,
    )


def column(row, n):
    full = jnp.broadcast_to(row, (n, row.shape[1]))
    same = lax.broadcasted_iota(jnp.int32, full.shape, 0) == lax.broadcasted_iota(
        jnp.int32, full.shape, 1
    )
    return jnp.sum(jnp.where(same, full, 0.0), axis=1, keepdims=True)


def run_row(ids):
    flat = ids.astype(F32).T
    parts = [flat[c : c + 1, :] for c in range(SEG // RUN)]
    return jnp.concatenate(parts, axis=1).astype(jnp.int32)


def analysis_kernel(
    x_hbm, t_hbm, v_hbm, ti_hbm, ro_hbm, cs_hbm, basis_hbm, synth_hbm, tw_hbm,
    out_ref, x_ref, synth_ref, tw_ref, rhs_ref, w_ref, ro_ref, cs_ref, line_ref, zid_ref,
    t_ref, v_ref, ti_ref, basis_ref, sems,
):
    pieces = [
        (x_hbm.at[:, pl.ds(n * XPIECE, XPIECE)], x_ref.at[:, pl.ds(n * XPIECE, XPIECE)])
        for n in range(SEG // XPIECE)
    ]
    copies = [
        pltpu.make_async_copy(src, dst, sems.at[n])
        for n, (src, dst) in enumerate(
            [
                (t_hbm, t_ref), (v_hbm, v_ref), (basis_hbm, basis_ref), *pieces,
                (ti_hbm, ti_ref), (ro_hbm, ro_ref), (cs_hbm, cs_ref),
                (tw_hbm, tw_ref), (synth_hbm, synth_ref),
            ]
        )
    ]
    for copy in copies:
        copy.start()
    copies[0].wait()
    copies[1].wait()
    w = column(v_ref[...].astype(F32), DETS)
    t = t_ref[...]
    wt = t * w
    w_ref[...] = jnp.broadcast_to(w, (DETS, 128))
    zero = jnp.zeros((NMODE, 32), F32)
    rhs_ref[...] = jnp.concatenate([zero, t.T, zero, zero], axis=1)
    gram = mm0(wt, t)
    out_ref[2 * NMODE :, :] = jnp.concatenate(
        [gram[8 * i : 8 * i + 8, :] for i in range(NMODE // 8)], axis=1
    )
    for copy in copies[-5:-2]:
        copy.wait()
    ti = ti_ref[...]
    ro = ro_ref[...]
    line_ref[...] = run_row(ti * TROWS + ro)
    zid_ref[...] = run_row(((ro + RADIUS) >> 3) * NT + ti)
    copies[2].wait()
    eh = basis_ref[:CHUNK, :]
    el = basis_ref[CHUNK:, :]
    ys = []
    per = XPIECE // CHUNK
    for n in range(SEG // XPIECE):
        copies[3 + n].wait()
        x = jnp.concatenate(
            [x_ref[:, c * CHUNK : (c + 1) * CHUNK] for c in range(n * per, (n + 1) * per)], axis=0
        )
        hi, lo = split(x)
        ys.append(mm(hi, eh) + mm(lo, eh) + mm(hi, el))
    copies[-2].wait()
    re = jnp.zeros((DETS, FKEEP), F32)
    im = jnp.zeros((DETS, FKEEP), F32)
    for c in range(NCHUNK):
        sl = slice(c % per * DETS, (c % per + 1) * DETS)
        yc = ys[c // per][sl, :FKEEP]
        yi = ys[c // per][sl, FKEEP:]
        cos = tw_ref[c : c + 1, :FKEEP]
        sin = tw_ref[c : c + 1, FKEEP:]
        re = re + (cos * yc - sin * yi)
        im = im + (sin * yc + cos * yi)
    both = mm0_split(wt, jnp.concatenate([re, im], axis=1))
    out_ref[:NMODE, :] = both[:, :FKEEP]
    out_ref[NMODE : 2 * NMODE, :] = both[:, FKEEP:]
    copies[-1].wait()


def edge_col(lane):
    slot = lane >> 3
    return jnp.where(slot < 3, TCOLS - RADIUS + slot, slot - 3)


def ids_of_blocks(core):
    l = lax.broadcasted_iota(jnp.int32, (NBLK * BROWS, 128), 0)
    i = l & (BROWS - 1)
    b = l >> 4
    row = (b >> 4) * (2 * OWN) + core * OWN - RADIUS + i
    ok = (i < OWN + 2 * RADIUS) & (row >= 0) & (row < TROWS)
    return jnp.where(ok, (b & (NT - 1)) * TROWS + row, -1)


def fill_hot(ref, ids, line):
    for q in range(NRUNS // 128):
        sl = slice(q * 128, (q + 1) * 128)
        ref[:, sl] = jnp.where(ids == line[:, sl], 1.0, 0.0).astype(BF)


def first_index_kernel(core_ref, line_ref, send_ref):
    fill_hot(send_ref, ids_of_blocks(core_ref[0] ^ 1), line_ref[...])


def second_index_kernel(
    core_ref, line_ref, zid_ref, ro_ref, cs_ref, w_ref,
    keep_ref, zhot_ref, idx_ref, edge_ref, mask_ref, zh_ref,
):
    zl = lax.broadcasted_iota(jnp.int32, (ZROWS, NRUNS), 0)
    zhot = jnp.where(zl == zid_ref[...], 1.0, 0.0).astype(BF)
    zhot_ref[...] = zhot
    w = w_ref[...]
    lane = lax.broadcasted_iota(jnp.int32, (DETS, 128), 1)
    ecol = edge_col(lane)
    hparts = []
    for c in range(SEG // RUN):
        sl = slice(c * DETS, (c + 1) * DETS)
        cs = jnp.broadcast_to(cs_ref[:, c : c + 1], (DETS, 128))
        ro = jnp.broadcast_to(ro_ref[:, c : c + 1], (DETS, 128))
        idx_ref[sl, :] = (lane - cs) & (TCOLS - 1)
        edge_ref[sl, :] = (ecol - cs) & (TCOLS - 1)
        here = ((ro + RADIUS) & (OWN - 1)) == (lane & (OWN - 1))
        mask_ref[sl, :] = jnp.where(here & (lane < 48), 1.0, 0.0)
        hparts.append(jnp.where(here & (lane >= 48) & (lane < 56), w, 0.0).astype(BF))
    zh_ref[...] = mm(zhot, jnp.concatenate(hparts, axis=0))
    fill_hot(keep_ref, ids_of_blocks(core_ref[0]), line_ref[...])


def lanes_of(v, k):
    return jnp.broadcast_to(v[:, k : k + 1], (8, 128))


def solve(packed, rhs):
    n = NMODE
    groups = range(n // 8)
    full = jnp.concatenate(
        [packed] + [pltpu.roll(packed, 128 - n * i, 1) for i in groups[1:]], axis=0
    )
    row = lax.broadcasted_iota(jnp.int32, (n, 128), 0)
    lane = lax.broadcasted_iota(jnp.int32, (n, 128), 1)
    full = jnp.where(lane < n, full, rhs) + jnp.where(lane == row, 0.05, 0.0)
    diag = jnp.where(lane == row, full, 0.0)
    down = lax.rsqrt(jnp.sum(diag, axis=1, keepdims=True))
    along = jnp.sum(jnp.where(lane < n, diag, 1.0 / n), axis=0, keepdims=True)
    full = full * down * lax.rsqrt(along)
    a = [full[8 * i : 8 * i + 8, :] for i in groups]
    sub = lax.broadcasted_iota(jnp.int32, (8, 128), 0)
    for q in range(8):
        c = [[lanes_of(v, 8 * j + q) for v in a] for j in groups]
        p = [[c[j][i] for j in groups] for i in groups]
        i1 = 1.0 / (p[0][0] * p[1][1] - p[0][1] * p[0][1])
        e00, e01, e11 = p[1][1] * i1, -p[0][1] * i1, p[0][0] * i1
        w00 = e00 * p[0][2] + e01 * p[1][2]
        w01 = e00 * p[0][3] + e01 * p[1][3]
        w10 = e01 * p[0][2] + e11 * p[1][2]
        w11 = e01 * p[0][3] + e11 * p[1][3]
        s00 = p[2][2] - (p[0][2] * w00 + p[1][2] * w10)
        s01 = p[2][3] - (p[0][2] * w01 + p[1][2] * w11)
        s11 = p[3][3] - (p[0][3] * w01 + p[1][3] * w11)
        i2 = 1.0 / (s00 * s11 - s01 * s01)
        y0 = e00 * a[0] + e01 * a[1]
        y1 = e01 * a[0] + e11 * a[1]
        q2 = a[2] - (p[0][2] * y0 + p[1][2] * y1)
        q3 = a[3] - (p[0][3] * y0 + p[1][3] * y1)
        n2 = (s11 * q2 - s01 * q3) * i2
        n3 = (s00 * q3 - s01 * q2) * i2
        n0 = y0 - (w00 * n2 + w01 * n3)
        n1 = y1 - (w10 * n2 + w11 * n3)
        new = [jnp.broadcast_to(v[q : q + 1, :], (8, 128)) for v in (n0, n1, n2, n3)]
        a = [
            jnp.where(
                sub == q,
                new[i],
                a[i] - ((c[0][i] * new[0] + c[1][i] * new[1]) + (c[2][i] * new[2] + c[3][i] * new[3])),
            )
            for i in groups
        ]
    return jnp.concatenate(a, axis=0)[:, n : 2 * n] * down


def shifted_tiles(z, by):
    zero = jnp.zeros((z.shape[0], 1, 128), F32)
    if by < 0:
        return jnp.concatenate([zero, z[:, :-1]], axis=1)
    return jnp.concatenate([z[:, 1:], zero], axis=1)


def clean_kernel(
    core_ref, p_ref, q_ref, r_ref, s_ref, rhs_ref, w_ref, x_ref, synth_ref, tw_ref,
    idx_ref, edge_ref, mask_ref, zhot_ref, zh_ref, send_hot_ref,
    clean_ref, send_ref, vals_ref, rows_ref,
):
    w = w_ref[...]
    w = jnp.concatenate([w, w], axis=1)
    p = (p_ref[...] + q_ref[...]) + (r_ref[...] + s_ref[...])
    coef = solve(p[2 * NMODE :, :], rhs_ref[...])
    ab = mm0_split(coef, jnp.concatenate([p[:NMODE, :], p[NMODE : 2 * NMODE, :]], axis=1))
    a = ab[:, :FKEEP]
    b = ab[:, FKEEP:]
    parts = []
    for c in range(NCHUNK):
        cos = tw_ref[c : c + 1, :FKEEP]
        sin = tw_ref[c : c + 1, FKEEP:]
        parts.append(jnp.concatenate([a * cos + b * sin, b * cos - a * sin], axis=1))
    hi, lo = split(jnp.concatenate(parts, axis=0))
    sh = synth_ref[:CHUNK, :]
    low = mm(hi, sh) + mm(lo, sh) + mm(hi, synth_ref[CHUNK:, :])
    runs = []
    for c in range(NCHUNK):
        part = w * (x_ref[:, c * CHUNK : (c + 1) * CHUNK] - low[c * DETS : (c + 1) * DETS, :])
        clean_ref[:, c * CHUNK : (c + 1) * CHUNK] = part
        runs.append(part[:, :RUN])
        runs.append(part[:, RUN:])
    run = jnp.concatenate(runs, axis=0)
    vals = jnp.concatenate(
        split(jnp.take_along_axis(run, idx_ref[...], axis=1, mode="promise_in_bounds")), axis=1
    )
    vals_ref[...] = vals
    evals = jnp.take_along_axis(run, edge_ref[...], axis=1, mode="promise_in_bounds")
    evals = jnp.concatenate(split(evals * mask_ref[...]), axis=1)
    z = mm(zhot_ref[...], evals)
    z = (z[:, :128] + z[:, 128:] + zh_ref[...]).reshape(ZROWS // NT, NT, 128)
    left = shifted_tiles(z, -1)
    right = shifted_tiles(z, 1)
    lane = lax.broadcasted_iota(jnp.int32, z.shape, 2)
    left_hits = left
    right_hits = jnp.concatenate([jnp.zeros(z.shape[:2] + (8,), F32), right[:, :, :-8]], axis=2)
    near = jnp.where(
        lane < 24, left, jnp.where(lane < 48, right, jnp.where(lane < 56, left_hits, right_hits))
    )
    near = jnp.where(lane < 64, near, 0.0)
    mine = jnp.where((lane >= 48) & (lane < 56), z, 0.0)
    nd = TROWS // OWN

    def both(v):
        return v[:nd] + jnp.concatenate([jnp.zeros((nd, NT, 64), F32), v[1:, :, :64]], axis=2)

    rows14 = both(near)
    rows15 = both(mine)
    core = core_ref[0]

    def pick(v, which):
        return jnp.concatenate(
            [jnp.where(which == 1, v[2 * y + 1], v[2 * y]) for y in range(NY)], axis=0
        )

    rows_ref[0:NBLK, :] = pick(rows14, core)
    rows_ref[NBLK : 2 * NBLK, :] = pick(rows15, core)
    s = mm(send_hot_ref[...], vals)
    send_ref[...] = s[:, :128] + s[:, 128:]
    send_ref[pl.ds(14, NBLK, stride=BROWS), :] = pick(rows14, core ^ 1)
    send_ref[pl.ds(15, NBLK, stride=BROWS), :] = pick(rows15, core ^ 1)


def keep_kernel(hot_ref, vals_ref, rows_ref, clean_ref, keep_ref, out_hbm, sem):
    copy = pltpu.make_async_copy(clean_ref, out_hbm, sem)
    copy.start()
    s = mm(hot_ref[...], vals_ref[...])
    keep_ref[...] = s[:, :128] + s[:, 128:]
    keep_ref[pl.ds(14, NBLK, stride=BROWS), :] = rows_ref[0:NBLK, :]
    keep_ref[pl.ds(15, NBLK, stride=BROWS), :] = rows_ref[NBLK : 2 * NBLK, :]
    copy.wait()


def beam_kernel(blocks_ref, out_ref):
    sums = [blocks_ref[b * BROWS : (b + 1) * BROWS, :] for b in range(4)]
    for b in range(4, NBLK):
        sums[b % 4] = sums[b % 4] + blocks_ref[b * BROWS : (b + 1) * BROWS, :]
    total = (sums[0] + sums[1]) + (sums[2] + sums[3])
    near = jnp.broadcast_to(total[14:15, :], (BROWS, 128))
    mine = jnp.broadcast_to(total[15:16, :], (BROWS, 128))
    i = lax.broadcasted_iota(jnp.int32, (BROWS, 128), 0)
    lane = lax.broadcasted_iota(jnp.int32, (BROWS, 128), 1)
    spot = jnp.where(i < OWN, i, 64 + i - OWN)

    def take(src, slot):
        return jnp.sum(jnp.where(lane == spot + 8 * slot, src, 0.0), axis=1, keepdims=True)

    left_hits = take(near, 6) + 1.0
    right_hits = take(near, 7) + 1.0
    hits = take(mine, 6) + 1.0
    valid = i < OWN + 2 * RADIUS
    binned = jnp.where(valid, total / hits, 0.0)
    left = [take(near, m) / left_hits for m in range(RADIUS)]
    right = [take(near, RADIUS + m) / right_hits for m in range(RADIUS)]
    taps = beam_taps()
    smooth = taps[RADIUS] * binned
    for m in range(1, RADIUS + 1):
        moved = pltpu.roll(binned, m, 1)
        for q in range(m):
            moved = jnp.where(lane == q, left[RADIUS - m + q], moved)
        smooth = smooth + taps[RADIUS - m] * moved
        moved = pltpu.roll(binned, TCOLS - m, 1)
        for q in range(m):
            moved = jnp.where(lane == TCOLS - m + q, right[q], moved)
        smooth = smooth + taps[RADIUS + m] * moved
    out = taps[0] * smooth[0:OWN, :]
    for m in range(1, 2 * RADIUS + 1):
        out = out + taps[m] * smooth[m : m + OWN, :]
    out_ref[...] = out


VMEM = pl.BlockSpec(memory_space=pltpu.VMEM)
SMEM = pl.BlockSpec(memory_space=pltpu.SMEM)
HBM = pl.BlockSpec(memory_space=pltpu.HBM)


def call(kernel, outs, specs, name, flops, *args, out_specs=None, scratch=()):
    args = [
        pltpu.with_memory_space_constraint(a, pltpu.HBM) if spec is HBM else a
        for a, spec in zip(args, specs)
    ]
    nbytes = sum(math.prod(s.shape) * 4 for s in outs) + sum(a.size * 4 for a in args)
    return pl.pallas_call(
        kernel,
        out_shape=outs,
        in_specs=specs,
        out_specs=out_specs or [VMEM] * len(outs),
        scratch_shapes=list(scratch),
        name=name,
        compiler_params=pltpu.CompilerParams(vmem_limit_bytes=40 << 20),
        cost_estimate=pl.CostEstimate(flops=flops, bytes_accessed=nbytes, transcendentals=0),
    )(*args)


def sds(shape, dtype=F32):
    return jax.ShapeDtypeStruct(shape, dtype)


I32 = jnp.int32


def body(timestreams, templates, validity, tile_index, row_offset, col_start):
    basis, synth, tw = tables()
    core = lax.axis_index("core").reshape(1)
    small = (DETS, SEG // RUN)
    big = (NBLK * BROWS, NRUNS)
    part, x, synth, tw, rhs, w, ro, cs, line, zid = call(
        analysis_kernel,
        [
            sds((2 * NMODE + 8, FKEEP)), sds((DETS, SEG)), sds((2 * CHUNK, 2 * FKEEP), BF),
            sds((NCHUNK, 2 * FKEEP)), sds((NMODE, 128)), sds((DETS, 128)),
            sds(small, I32), sds(small, I32), sds((1, NRUNS), I32), sds((1, NRUNS), I32),
        ],
        [HBM] * 9, "analysis", 400_000_000,
        timestreams, templates, validity.reshape(1, DETS), tile_index, row_offset, col_start,
        jnp.asarray(basis), jnp.asarray(synth), jnp.asarray(tw),
        scratch=[
            pltpu.VMEM((DETS, NMODE), F32), pltpu.VMEM((1, DETS), I32), pltpu.VMEM(small, I32),
            pltpu.VMEM((2 * CHUNK, 2 * FKEEP), BF), pltpu.SemaphoreType.DMA((8 + SEG // XPIECE,)),
        ],
    )
    other = lax.ppermute(part, "core", [(0, 1), (1, 0)])
    (send_hot,) = call(
        first_index_kernel, [sds(big, BF)], [SMEM, VMEM], "index1", 100_000_000, core, line
    )
    part, send_hot, line = lax.optimization_barrier((part + other, send_hot, line))
    others = [lax.ppermute(part, "y", [(k, k ^ m) for k in range(NY)]) for m in (2, 3, 1)]
    keep_hot, zhot, idx, edge, mask, zh = call(
        second_index_kernel,
        [
            sds(big, BF), sds((ZROWS, NRUNS), BF),
            sds((NRUNS, 128), I32), sds((NRUNS, 128), I32),
            sds((NRUNS, 128)), sds((ZROWS, 128)),
        ],
        [SMEM] + [VMEM] * 5, "index2", 100_000_000,
        core, line, zid, ro, cs, w,
    )
    cleaned, send, vals, rows = call(
        clean_kernel,
        [
            sds((DETS, SEG)), sds((NBLK * BROWS, 128)),
            sds((NRUNS, 256), BF), sds((2 * NBLK, 128)),
        ],
        [SMEM] + [VMEM] * 15, "clean", 1_000_000_000,
        core, part, *others, rhs, w, x, synth, tw, idx, edge, mask, zhot, zh, send_hot,
    )
    got = lax.ppermute(send, "core", [(0, 1), (1, 0)])
    keep, cleaned = call(
        keep_kernel, [sds((NBLK * BROWS, 128)), sds((DETS, SEG))], [VMEM] * 4, "keep",
        500_000_000, keep_hot, vals, rows, cleaned,
        out_specs=[VMEM, HBM], scratch=[pltpu.SemaphoreType.DMA],
    )
    blocks = lax.all_to_all(keep + got, ("y", "z", "x"), 0, 0, tiled=True)
    (beamed,) = call(
        beam_kernel, [sds((OWN, TCOLS))], [VMEM], "beam", 1_000_000, blocks
    )
    return (cleaned, beamed)


def solution(mesh):
    fine = Mesh(mesh.devices.reshape(NY, 2, 4, 4), ("y", "core", "z", "x"))
    det, tm = ("y", "core"), ("z", "x")
    in_specs = (P(det, tm), P(det, None), P(det), P(det, tm), P(det, tm), P(det, tm))
    out_specs = (P(det, tm), P(det, tm))
    return jax.shard_map(body, mesh=fine, in_specs=in_specs, out_specs=out_specs, check_vma=False)
```

```python
import math

import jax
import jax.numpy as jnp
import numpy as np
from jax import lax
from jax.experimental import pallas as pl
from jax.experimental.pallas import tpu as pltpu
from jax.sharding import Mesh
from jax.sharding import PartitionSpec as P
import ml_dtypes

SEG = 4096
NMODE = 32
FKEEP = 128
RUN = 128
TROWS = 64
TCOLS = 128
RADIUS = 3
DETS = 32
CHUNK = 256
NCHUNK = SEG // CHUNK
XPIECE = 4096
NRUNS = DETS * SEG // RUN
NT = 16
NY = 4
OWN = 8
BROWS = 16
NBLK = NY * NT
ZROWS = (TROWS // OWN + 1) * NT
BF = jnp.bfloat16
F32 = jnp.float32


def split_np(a):
    hi = a.astype(np.float32).astype(ml_dtypes.bfloat16)
    lo = (a - hi.astype(np.float64)).astype(np.float32).astype(ml_dtypes.bfloat16)
    return hi, lo


def tables():
    j = np.arange(CHUNK)[:, None]
    k = np.arange(FKEEP)[None, :]
    phi = 2.0 * np.pi * (j * k % SEG) / SEG
    basis = np.concatenate([np.cos(phi), np.sin(phi)], axis=1)
    c = np.arange(NCHUNK)[:, None]
    theta = 2.0 * np.pi * (c * CHUNK * k % SEG) / SEG
    twiddle = np.concatenate([np.cos(theta), np.sin(theta)], axis=1).astype(np.float32)
    scale = np.where(np.arange(FKEEP) == 0, 1.0 / SEG, 2.0 / SEG)
    synth = basis.T * np.concatenate([scale, scale])[:, None]
    return np.concatenate(split_np(basis)), np.concatenate(split_np(synth)), twiddle


def beam_taps():
    values = [math.exp(-(m * m) / 4.5) for m in range(-RADIUS, RADIUS + 1)]
    total = sum(values)
    return [v / total for v in values]


def split(a):
    hi = a.astype(BF)
    return hi, (a - hi.astype(F32)).astype(BF)


def mm(a, b):
    return jnp.dot(a, b, preferred_element_type=F32)


def mm0(a, b):
    return lax.dot_general(
        a, b, (((0,), (0,)), ((), ())), precision=lax.Precision.HIGHEST,
        preferred_element_type=F32,
    )


def mm0_split(a, b):
    ah, al = split(a)
    bh, bl = split(b)
    return lax.dot_general(
        jnp.concatenate([ah, al, ah], axis=0), jnp.concatenate([bh, bh, bl], axis=0),
        (((0,), (0,)), ((), ())), preferred_element_type=F32,
    )


def column(row, n):
    full = jnp.broadcast_to(row, (n, row.shape[1]))
    same = lax.broadcasted_iota(jnp.int32, full.shape, 0) == lax.broadcasted_iota(
        jnp.int32, full.shape, 1
    )
    return jnp.sum(jnp.where(same, full, 0.0), axis=1, keepdims=True)


def run_row(ids):
    flat = ids.astype(F32).T
    parts = [flat[c : c + 1, :] for c in range(SEG // RUN)]
    return jnp.concatenate(parts, axis=1).astype(jnp.int32)


def analysis_kernel(
    x_hbm, t_hbm, v_hbm, ti_hbm, ro_hbm, cs_hbm, basis_hbm, synth_hbm, tw_hbm,
    out_ref, x_ref, synth_ref, tw_ref, pack_ref, line_ref,
    t_ref, v_ref, ti_ref, ro_ref, cs_ref, basis_ref, sems,
):
    pieces = [
        (x_hbm.at[:, pl.ds(n * XPIECE, XPIECE)], x_ref.at[:, pl.ds(n * XPIECE, XPIECE)])
        for n in range(SEG // XPIECE)
    ]
    copies = [
        pltpu.make_async_copy(src, dst, sems.at[n])
        for n, (src, dst) in enumerate(
            [
                (t_hbm, t_ref), (v_hbm, v_ref), (basis_hbm, basis_ref), *pieces,
                (ti_hbm, ti_ref), (ro_hbm, ro_ref), (cs_hbm, cs_ref),
                (tw_hbm, tw_ref), (synth_hbm, synth_ref),
            ]
        )
    ]
    for copy in copies:
        copy.start()
    copies[0].wait()
    copies[1].wait()
    w = column(v_ref[...].astype(F32), DETS)
    t = t_ref[...]
    wt = t * w
    gram = mm0(wt, t)
    out_ref[2 * NMODE :, :] = jnp.concatenate(
        [gram[8 * i : 8 * i + 8, :] for i in range(NMODE // 8)], axis=1
    )
    for copy in copies[-5:-2]:
        copy.wait()
    line = ti_ref[...] * TROWS + ro_ref[...]
    line_ref[...] = run_row(line)
    pack_ref[...] = jnp.concatenate(
        [t, line.astype(F32), cs_ref[...].astype(F32), jnp.broadcast_to(w, (DETS, 32))], axis=1
    )
    copies[2].wait()
    eh = basis_ref[:CHUNK, :]
    el = basis_ref[CHUNK:, :]
    ys = []
    per = XPIECE // CHUNK
    for n in range(SEG // XPIECE):
        copies[3 + n].wait()
        x = jnp.concatenate(
            [x_ref[:, c * CHUNK : (c + 1) * CHUNK] for c in range(n * per, (n + 1) * per)], axis=0
        )
        hi, lo = split(x)
        ys.append(mm(hi, eh) + mm(lo, eh) + mm(hi, el))
    copies[-2].wait()
    re = jnp.zeros((DETS, FKEEP), F32)
    im = jnp.zeros((DETS, FKEEP), F32)
    for c in range(NCHUNK):
        sl = slice(c % per * DETS, (c % per + 1) * DETS)
        yc = ys[c // per][sl, :FKEEP]
        yi = ys[c // per][sl, FKEEP:]
        cos = tw_ref[c : c + 1, :FKEEP]
        sin = tw_ref[c : c + 1, FKEEP:]
        re = re + (cos * yc - sin * yi)
        im = im + (sin * yc + cos * yi)
    both = mm0_split(wt, jnp.concatenate([re, im], axis=1))
    out_ref[:NMODE, :] = both[:, :FKEEP]
    out_ref[NMODE : 2 * NMODE, :] = both[:, FKEEP:]
    copies[-1].wait()


def edge_col(lane):
    slot = lane >> 3
    return jnp.where(slot < 3, TCOLS - RADIUS + slot, slot - 3)


def ids_of_blocks(core):
    l = lax.broadcasted_iota(jnp.int32, (NBLK * BROWS, 128), 0)
    i = l & (BROWS - 1)
    b = l >> 4
    row = (b >> 4) * (2 * OWN) + core * OWN - RADIUS + i
    ok = (i < OWN + 2 * RADIUS) & (row >= 0) & (row < TROWS)
    return jnp.where(ok, (b & (NT - 1)) * TROWS + row, -1)


def fill_hot(ref, ids, line):
    for q in range(NRUNS // 128):
        sl = slice(q * 128, (q + 1) * 128)
        ref[:, sl] = jnp.where(ids == line[:, sl], 1.0, 0.0).astype(BF)


def first_index_kernel(core_ref, line_ref, hot_ref):
    fill_hot(hot_ref, ids_of_blocks(core_ref[0]), line_ref[...])


def second_index_kernel(
    core_ref, line_ref, pack_ref, other_ref,
    hot_ref, zhot_ref, idx_ref, edge_ref, mask_ref, zh_ref, rhs_ref, w_ref,
):
    packs = (pack_ref[...], other_ref[...])
    lines = [pack[:, 32:64].astype(jnp.int32) for pack in packs]
    rows = (line_ref[...], run_row(lines[1]))
    fill_hot(hot_ref, ids_of_blocks(core_ref[0]), rows[1])
    line = jnp.concatenate(rows, axis=1)
    zid = (((line & (TROWS - 1)) + RADIUS) >> 3) * NT + (line >> 6)
    zl = lax.broadcasted_iota(jnp.int32, (ZROWS, 2 * NRUNS), 0)
    zhot = jnp.where(zl == zid, 1.0, 0.0).astype(BF)
    zhot_ref[...] = zhot
    lane = lax.broadcasted_iota(jnp.int32, (DETS, 128), 1)
    ecol = edge_col(lane)
    hparts = []
    for n, pack in enumerate(packs):
        w = jnp.broadcast_to(pack[:, 96:97], (DETS, 128))
        w_ref[n * DETS : (n + 1) * DETS, :] = w
        ro3 = (lines[n] & (TROWS - 1)) + RADIUS
        css = pack[:, 64:96].astype(jnp.int32)
        for c in range(SEG // RUN):
            sl = slice(n * NRUNS + c * DETS, n * NRUNS + (c + 1) * DETS)
            cs = jnp.broadcast_to(css[:, c : c + 1], (DETS, 128))
            idx_ref[sl, :] = (lane - cs) & (TCOLS - 1)
            edge_ref[sl, :] = (ecol - cs) & (TCOLS - 1)
            here = ((jnp.broadcast_to(ro3[:, c : c + 1], (DETS, 128)) ^ lane) & (OWN - 1)) == 0
            mask_ref[sl, :] = jnp.where(here & (lane < 48), 1.0, 0.0)
            hparts.append(jnp.where(here & (lane >= 48) & (lane < 56), w, 0.0).astype(BF))
    zh_ref[...] = mm(zhot, jnp.concatenate(hparts, axis=0))
    zero = jnp.zeros((NMODE, 32), F32)
    rhs_ref[...] = jnp.concatenate(
        [zero, packs[0][:, :NMODE].T, packs[1][:, :NMODE].T, zero], axis=1
    )


def lanes_of(v, k):
    return jnp.broadcast_to(v[:, k : k + 1], (8, 128))


def solve(packed, rhs):
    n = NMODE
    groups = range(n // 8)
    full = jnp.concatenate(
        [packed] + [pltpu.roll(packed, 128 - n * i, 1) for i in groups[1:]], axis=0
    )
    row = lax.broadcasted_iota(jnp.int32, (n, 128), 0)
    lane = lax.broadcasted_iota(jnp.int32, (n, 128), 1)
    full = jnp.where(lane < n, full, rhs) + jnp.where(lane == row, 0.05, 0.0)
    diag = jnp.where(lane == row, full, 0.0)
    down = lax.rsqrt(jnp.sum(diag, axis=1, keepdims=True))
    along = jnp.sum(jnp.where(lane < n, diag, 1.0 / n), axis=0, keepdims=True)
    full = full * down * lax.rsqrt(along)
    a = [full[8 * i : 8 * i + 8, :] for i in groups]
    sub = lax.broadcasted_iota(jnp.int32, (8, 128), 0)
    for q in range(8):
        c = [[lanes_of(v, 8 * j + q) for v in a] for j in groups]
        p = [[c[j][i] for j in groups] for i in groups]
        i1 = 1.0 / (p[0][0] * p[1][1] - p[0][1] * p[0][1])
        e00, e01, e11 = p[1][1] * i1, -p[0][1] * i1, p[0][0] * i1
        w00 = e00 * p[0][2] + e01 * p[1][2]
        w01 = e00 * p[0][3] + e01 * p[1][3]
        w10 = e01 * p[0][2] + e11 * p[1][2]
        w11 = e01 * p[0][3] + e11 * p[1][3]
        s00 = p[2][2] - (p[0][2] * w00 + p[1][2] * w10)
        s01 = p[2][3] - (p[0][2] * w01 + p[1][2] * w11)
        s11 = p[3][3] - (p[0][3] * w01 + p[1][3] * w11)
        i2 = 1.0 / (s00 * s11 - s01 * s01)
        y0 = e00 * a[0] + e01 * a[1]
        y1 = e01 * a[0] + e11 * a[1]
        q2 = a[2] - (p[0][2] * y0 + p[1][2] * y1)
        q3 = a[3] - (p[0][3] * y0 + p[1][3] * y1)
        n2 = (s11 * q2 - s01 * q3) * i2
        n3 = (s00 * q3 - s01 * q2) * i2
        n0 = y0 - (w00 * n2 + w01 * n3)
        n1 = y1 - (w10 * n2 + w11 * n3)
        new = [jnp.broadcast_to(v[q : q + 1, :], (8, 128)) for v in (n0, n1, n2, n3)]
        a = [
            jnp.where(
                sub == q,
                new[i],
                a[i] - ((c[0][i] * new[0] + c[1][i] * new[1]) + (c[2][i] * new[2] + c[3][i] * new[3])),
            )
            for i in groups
        ]
    return jnp.concatenate(a, axis=0)[:, n : 3 * n] * down


def shifted_tiles(z, by):
    zero = jnp.zeros((z.shape[0], 1, 128), F32)
    if by < 0:
        return jnp.concatenate([zero, z[:, :-1]], axis=1)
    return jnp.concatenate([z[:, 1:], zero], axis=1)


def clean_kernel(
    core_ref, p_ref, q_ref, r_ref, s_ref, rhs_ref, w_ref, x_ref, other_ref, synth_ref, tw_ref,
    idx_ref, edge_ref, mask_ref, zhot_ref, zh_ref, hot_ref, other_hot_ref,
    blocks_ref, out_hbm, clean_ref, sem,
):
    p = (p_ref[...] + q_ref[...]) + (r_ref[...] + s_ref[...])
    coef = solve(p[2 * NMODE :, :], rhs_ref[...])
    ab = mm0_split(coef, jnp.concatenate([p[:NMODE, :], p[NMODE : 2 * NMODE, :]], axis=1))
    a = ab[:, :FKEEP]
    b = ab[:, FKEEP:]
    parts = []
    for c in range(NCHUNK):
        cos = tw_ref[c : c + 1, :FKEEP]
        sin = tw_ref[c : c + 1, FKEEP:]
        parts.append(jnp.concatenate([a * cos + b * sin, b * cos - a * sin], axis=1))
    hi, lo = split(jnp.concatenate(parts, axis=0))
    sh = synth_ref[:CHUNK, :]
    low = mm(hi, sh) + mm(lo, sh) + mm(hi, synth_ref[CHUNK:, :])
    runs = []
    for n, source in enumerate((x_ref, other_ref)):
        w = w_ref[n * DETS : (n + 1) * DETS, :]
        w = jnp.concatenate([w, w], axis=1)
        for c in range(NCHUNK):
            at = 2 * DETS * c + DETS * n
            part = w * (source[:, c * CHUNK : (c + 1) * CHUNK] - low[at : at + DETS, :])
            if n == 0:
                clean_ref[:, c * CHUNK : (c + 1) * CHUNK] = part
            runs.append(part[:, :RUN])
            runs.append(part[:, RUN:])
    copy = pltpu.make_async_copy(clean_ref, out_hbm, sem)
    copy.start()
    run = jnp.concatenate(runs, axis=0)
    vals = jnp.concatenate(
        split(jnp.take_along_axis(run, idx_ref[...], axis=1, mode="promise_in_bounds")), axis=1
    )
    evals = jnp.take_along_axis(run, edge_ref[...], axis=1, mode="promise_in_bounds")
    evals = jnp.concatenate(split(evals * mask_ref[...]), axis=1)
    s = mm(hot_ref[...], vals[:NRUNS]) + mm(other_hot_ref[...], vals[NRUNS:])
    blocks_ref[...] = s[:, :128] + s[:, 128:]
    z = mm(zhot_ref[...], evals)
    z = (z[:, :128] + z[:, 128:] + zh_ref[...]).reshape(ZROWS // NT, NT, 128)
    left = shifted_tiles(z, -1)
    right = shifted_tiles(z, 1)
    lane = lax.broadcasted_iota(jnp.int32, z.shape, 2)
    left_hits = left
    right_hits = jnp.concatenate([jnp.zeros(z.shape[:2] + (8,), F32), right[:, :, :-8]], axis=2)
    near = jnp.where(
        lane < 24, left, jnp.where(lane < 48, right, jnp.where(lane < 56, left_hits, right_hits))
    )
    near = jnp.where(lane < 64, near, 0.0)
    mine = jnp.where((lane >= 48) & (lane < 56), z, 0.0)
    nd = TROWS // OWN

    def both(v):
        return v[:nd] + jnp.concatenate([jnp.zeros((nd, NT, 64), F32), v[1:, :, :64]], axis=2)

    core = core_ref[0]
    for row, values in ((14, both(near)), (15, both(mine))):
        picked = [
            jnp.where(core == 1, values[2 * y + 1], values[2 * y]) for y in range(NY)
        ]
        blocks_ref[pl.ds(row, NBLK, stride=BROWS), :] = jnp.concatenate(picked, axis=0)
    copy.wait()


def beam_kernel(blocks_ref, out_ref):
    sums = [blocks_ref[b * BROWS : (b + 1) * BROWS, :] for b in range(4)]
    for b in range(4, NBLK):
        sums[b % 4] = sums[b % 4] + blocks_ref[b * BROWS : (b + 1) * BROWS, :]
    total = (sums[0] + sums[1]) + (sums[2] + sums[3])
    near = jnp.broadcast_to(total[14:15, :], (BROWS, 128))
    mine = jnp.broadcast_to(total[15:16, :], (BROWS, 128))
    i = lax.broadcasted_iota(jnp.int32, (BROWS, 128), 0)
    lane = lax.broadcasted_iota(jnp.int32, (BROWS, 128), 1)
    spot = jnp.where(i < OWN, i, 64 + i - OWN)

    def take(src, slot):
        return jnp.sum(jnp.where(lane == spot + 8 * slot, src, 0.0), axis=1, keepdims=True)

    left_hits = take(near, 6) + 1.0
    right_hits = take(near, 7) + 1.0
    hits = take(mine, 6) + 1.0
    valid = i < OWN + 2 * RADIUS
    binned = jnp.where(valid, total / hits, 0.0)
    left = [take(near, m) / left_hits for m in range(RADIUS)]
    right = [take(near, RADIUS + m) / right_hits for m in range(RADIUS)]
    taps = beam_taps()
    smooth = taps[RADIUS] * binned
    for m in range(1, RADIUS + 1):
        moved = pltpu.roll(binned, m, 1)
        for q in range(m):
            moved = jnp.where(lane == q, left[RADIUS - m + q], moved)
        smooth = smooth + taps[RADIUS - m] * moved
        moved = pltpu.roll(binned, TCOLS - m, 1)
        for q in range(m):
            moved = jnp.where(lane == TCOLS - m + q, right[q], moved)
        smooth = smooth + taps[RADIUS + m] * moved
    out = taps[0] * smooth[0:OWN, :]
    for m in range(1, 2 * RADIUS + 1):
        out = out + taps[m] * smooth[m : m + OWN, :]
    out_ref[...] = out


VMEM = pl.BlockSpec(memory_space=pltpu.VMEM)
SMEM = pl.BlockSpec(memory_space=pltpu.SMEM)
HBM = pl.BlockSpec(memory_space=pltpu.HBM)


def call(kernel, outs, specs, name, flops, *args, out_specs=None, scratch=()):
    args = [
        pltpu.with_memory_space_constraint(a, pltpu.HBM) if spec is HBM else a
        for a, spec in zip(args, specs)
    ]
    nbytes = sum(math.prod(s.shape) * 4 for s in outs) + sum(a.size * 4 for a in args)
    return pl.pallas_call(
        kernel,
        out_shape=outs,
        in_specs=specs,
        out_specs=out_specs or [VMEM] * len(outs),
        scratch_shapes=list(scratch),
        name=name,
        compiler_params=pltpu.CompilerParams(vmem_limit_bytes=40 << 20),
        cost_estimate=pl.CostEstimate(flops=flops, bytes_accessed=nbytes, transcendentals=0),
    )(*args)


def sds(shape, dtype=F32):
    return jax.ShapeDtypeStruct(shape, dtype)


I32 = jnp.int32


def body(timestreams, templates, validity, tile_index, row_offset, col_start):
    basis, synth, tw = tables()
    core = lax.axis_index("core").reshape(1)
    small = (DETS, SEG // RUN)
    big = (NBLK * BROWS, NRUNS)
    swap = [(0, 1), (1, 0)]
    mate_x = lax.ppermute(timestreams, "core", swap)
    part, x, synth, tw, pack, line = call(
        analysis_kernel,
        [
            sds((2 * NMODE + 8, FKEEP)), sds((DETS, SEG)), sds((2 * CHUNK, 2 * FKEEP), BF),
            sds((NCHUNK, 2 * FKEEP)), sds((DETS, 128)), sds((1, NRUNS), I32),
        ],
        [HBM] * 9, "analysis", 400_000_000,
        timestreams, templates, validity.reshape(1, DETS), tile_index, row_offset, col_start,
        jnp.asarray(basis), jnp.asarray(synth), jnp.asarray(tw),
        scratch=[
            pltpu.VMEM((DETS, NMODE), F32), pltpu.VMEM((1, DETS), I32), pltpu.VMEM(small, I32),
            pltpu.VMEM(small, I32), pltpu.VMEM(small, I32),
            pltpu.VMEM((2 * CHUNK, 2 * FKEEP), BF), pltpu.SemaphoreType.DMA((8 + SEG // XPIECE,)),
        ],
    )
    mate = lax.ppermute(part, "core", swap)
    (hot,) = call(
        first_index_kernel, [sds(big, BF)], [SMEM, VMEM], "index1", 100_000_000, core, line
    )
    mate_pack = lax.ppermute(pack, "core", swap)
    part, hot, line, mate_pack = lax.optimization_barrier((part + mate, hot, line, mate_pack))
    others = [lax.ppermute(part, "y", [(k, k ^ m) for k in range(NY)]) for m in (2, 3, 1)]
    twice = (2 * NRUNS, 128)
    mate_hot, zhot, idx, edge, mask, zh, rhs, w = call(
        second_index_kernel,
        [
            sds(big, BF), sds((ZROWS, 2 * NRUNS), BF), sds(twice, I32), sds(twice, I32),
            sds(twice), sds((ZROWS, 128)), sds((NMODE, 128)), sds((2 * DETS, 128)),
        ],
        [SMEM] + [VMEM] * 3, "index2", 100_000_000,
        core, line, pack, mate_pack,
    )
    blocks, cleaned = call(
        clean_kernel,
        [sds((NBLK * BROWS, 128)), sds((DETS, SEG))],
        [SMEM] + [VMEM] * 17, "clean", 2_000_000_000,
        core, part, *others, rhs, w, x, mate_x, synth, tw, idx, edge, mask, zhot, zh, hot, mate_hot,
        out_specs=[VMEM, HBM],
        scratch=[pltpu.VMEM((DETS, SEG), F32), pltpu.SemaphoreType.DMA],
    )
    blocks = lax.all_to_all(blocks, ("y", "z", "x"), 0, 0, tiled=True)
    (beamed,) = call(
        beam_kernel, [sds((OWN, TCOLS))], [VMEM], "beam", 1_000_000, blocks
    )
    return (cleaned, beamed)


def solution(mesh):
    fine = Mesh(mesh.devices.reshape(NY, 2, 4, 4), ("y", "core", "z", "x"))
    det, tm = ("y", "core"), ("z", "x")
    in_specs = (P(det, tm), P(det, None), P(det), P(det, tm), P(det, tm), P(det, tm))
    out_specs = (P(det, tm), P(det, tm))
    return jax.shard_map(body, mesh=fine, in_specs=in_specs, out_specs=out_specs, check_vma=False)
```

```python
import math

import jax
import jax.numpy as jnp
import numpy as np
from jax import lax
from jax.experimental import pallas as pl
from jax.experimental.pallas import tpu as pltpu
from jax.sharding import Mesh
from jax.sharding import PartitionSpec as P
import ml_dtypes

SEG = 4096
NMODE = 32
FKEEP = 128
RUN = 128
TROWS = 64
TCOLS = 128
RADIUS = 3
DETS = 32
CHUNK = 256
NCHUNK = SEG // CHUNK
XPIECE = 4096
NRUNS = DETS * SEG // RUN
NT = 16
NY = 4
OWN = 8
BROWS = 16
NBLK = NY * NT
ZROWS = (TROWS // OWN + 1) * NT
BF = jnp.bfloat16
F32 = jnp.float32


def split_np(a):
    hi = a.astype(np.float32).astype(ml_dtypes.bfloat16)
    lo = (a - hi.astype(np.float64)).astype(np.float32).astype(ml_dtypes.bfloat16)
    return hi, lo


def tables():
    j = np.arange(CHUNK)[:, None]
    k = np.arange(FKEEP)[None, :]
    phi = 2.0 * np.pi * (j * k % SEG) / SEG
    basis = np.concatenate([np.cos(phi), np.sin(phi)], axis=1)
    c = np.arange(NCHUNK)[:, None]
    theta = 2.0 * np.pi * (c * CHUNK * k % SEG) / SEG
    twiddle = np.concatenate([np.cos(theta), np.sin(theta)], axis=1).astype(np.float32)
    scale = np.where(np.arange(FKEEP) == 0, 1.0 / SEG, 2.0 / SEG)
    synth = basis.T * np.concatenate([scale, scale])[:, None]
    return np.concatenate(split_np(basis)), np.concatenate(split_np(synth)), twiddle


def beam_taps():
    values = [math.exp(-(m * m) / 4.5) for m in range(-RADIUS, RADIUS + 1)]
    total = sum(values)
    return [v / total for v in values]


def split(a):
    hi = a.astype(BF)
    return hi, (a - hi.astype(F32)).astype(BF)


def mm(a, b):
    return jnp.dot(a, b, preferred_element_type=F32)


def mm0(a, b):
    return lax.dot_general(
        a, b, (((0,), (0,)), ((), ())), precision=lax.Precision.HIGHEST,
        preferred_element_type=F32,
    )


def mm0_split(a, b):
    ah, al = split(a)
    bh, bl = split(b)
    return lax.dot_general(
        jnp.concatenate([ah, al, ah], axis=0), jnp.concatenate([bh, bh, bl], axis=0),
        (((0,), (0,)), ((), ())), preferred_element_type=F32,
    )


def column(row, n):
    full = jnp.broadcast_to(row, (n, row.shape[1]))
    same = lax.broadcasted_iota(jnp.int32, full.shape, 0) == lax.broadcasted_iota(
        jnp.int32, full.shape, 1
    )
    return jnp.sum(jnp.where(same, full, 0.0), axis=1, keepdims=True)


def run_row(ids):
    flat = ids.T
    parts = [flat[c : c + 1, :] for c in range(SEG // RUN)]
    return jnp.concatenate(parts, axis=1).astype(jnp.int32)


def analysis_kernel(
    x_hbm, t_hbm, v_hbm, ti_hbm, ro_hbm, cs_hbm, basis_hbm, synth_hbm, tw_hbm,
    out_ref, x_ref, synth_ref, tw_ref, pack_ref,
    t_ref, v_ref, ti_ref, ro_ref, cs_ref, basis_ref, sems,
):
    pieces = [
        (x_hbm.at[:, pl.ds(n * XPIECE, XPIECE)], x_ref.at[:, pl.ds(n * XPIECE, XPIECE)])
        for n in range(SEG // XPIECE)
    ]
    copies = [
        pltpu.make_async_copy(src, dst, sems.at[n])
        for n, (src, dst) in enumerate(
            [
                (t_hbm, t_ref), (v_hbm, v_ref), (basis_hbm, basis_ref), *pieces,
                (ti_hbm, ti_ref), (ro_hbm, ro_ref), (cs_hbm, cs_ref),
                (tw_hbm, tw_ref), (synth_hbm, synth_ref),
            ]
        )
    ]
    for copy in copies:
        copy.start()
    copies[0].wait()
    copies[1].wait()
    w = column(v_ref[...].astype(F32), DETS)
    t = t_ref[...]
    wt = t * w
    gram = mm0(wt, t)
    out_ref[2 * NMODE :, :] = jnp.concatenate(
        [gram[8 * i : 8 * i + 8, :] for i in range(NMODE // 8)], axis=1
    )
    for copy in copies[-5:-2]:
        copy.wait()
    line = ti_ref[...] * TROWS + ro_ref[...]
    pack_ref[...] = jnp.concatenate(
        [t, line.astype(F32), cs_ref[...].astype(F32), jnp.broadcast_to(w, (DETS, 32))], axis=1
    )
    copies[2].wait()
    eh = basis_ref[:CHUNK, :]
    el = basis_ref[CHUNK:, :]
    ys = []
    per = XPIECE // CHUNK
    for n in range(SEG // XPIECE):
        copies[3 + n].wait()
        x = jnp.concatenate(
            [x_ref[:, c * CHUNK : (c + 1) * CHUNK] for c in range(n * per, (n + 1) * per)], axis=0
        )
        hi, lo = split(x)
        ys.append(mm(hi, eh) + mm(lo, eh) + mm(hi, el))
    copies[-2].wait()
    re = jnp.zeros((DETS, FKEEP), F32)
    im = jnp.zeros((DETS, FKEEP), F32)
    for c in range(NCHUNK):
        sl = slice(c % per * DETS, (c % per + 1) * DETS)
        yc = ys[c // per][sl, :FKEEP]
        yi = ys[c // per][sl, FKEEP:]
        cos = tw_ref[c : c + 1, :FKEEP]
        sin = tw_ref[c : c + 1, FKEEP:]
        re = re + (cos * yc - sin * yi)
        im = im + (sin * yc + cos * yi)
    both = mm0_split(wt, jnp.concatenate([re, im], axis=1))
    out_ref[:NMODE, :] = both[:, :FKEEP]
    out_ref[NMODE : 2 * NMODE, :] = both[:, FKEEP:]
    copies[-1].wait()


def edge_col(lane):
    slot = lane >> 3
    return jnp.where(slot < 3, TCOLS - RADIUS + slot, slot - 3)


def ids_of_blocks(core):
    l = lax.broadcasted_iota(jnp.int32, (NBLK * BROWS, 128), 0)
    i = l & (BROWS - 1)
    b = l >> 4
    row = (b >> 4) * (2 * OWN) + core * OWN - RADIUS + i
    ok = (i < OWN + 2 * RADIUS) & (row >= 0) & (row < TROWS)
    return jnp.where(ok, (b & (NT - 1)) * TROWS + row, -1)


def fill_hot(ref, ids, line):
    for q in range(NRUNS // 128):
        sl = slice(q * 128, (q + 1) * 128)
        ref[:, sl] = jnp.where(ids == line[:, sl], 1.0, 0.0).astype(BF)


def first_index_kernel(core_ref, pack_ref, hot_ref, line_ref):
    line = run_row(pack_ref[:, 32:64])
    line_ref[...] = line
    fill_hot(hot_ref, ids_of_blocks(core_ref[0]), line)


def second_index_kernel(
    core_ref, line_ref, pack_ref, other_ref,
    hot_ref, zhot_ref, idx_ref, edge_ref, mask_ref, zh_ref, rhs_ref, w_ref,
):
    packs = (pack_ref[...], other_ref[...])
    lines = [pack[:, 32:64].astype(jnp.int32) for pack in packs]
    rows = (line_ref[...], run_row(packs[1][:, 32:64]))
    fill_hot(hot_ref, ids_of_blocks(core_ref[0]), rows[1])
    line = jnp.concatenate(rows, axis=1)
    zid = (((line & (TROWS - 1)) + RADIUS) >> 3) * NT + (line >> 6)
    zl = lax.broadcasted_iota(jnp.int32, (ZROWS, 2 * NRUNS), 0)
    zhot = jnp.where(zl == zid, 1.0, 0.0).astype(BF)
    zhot_ref[...] = zhot
    lane = lax.broadcasted_iota(jnp.int32, (DETS, 128), 1)
    ecol = edge_col(lane)
    hparts = []
    for n, pack in enumerate(packs):
        w = jnp.broadcast_to(pack[:, 96:97], (DETS, 128))
        w_ref[n * DETS : (n + 1) * DETS, :] = w
        ro3 = (lines[n] & (TROWS - 1)) + RADIUS
        css = pack[:, 64:96].astype(jnp.int32)
        for c in range(SEG // RUN):
            sl = slice(n * NRUNS + c * DETS, n * NRUNS + (c + 1) * DETS)
            cs = jnp.broadcast_to(css[:, c : c + 1], (DETS, 128))
            idx_ref[sl, :] = (lane - cs) & (TCOLS - 1)
            edge_ref[sl, :] = (ecol - cs) & (TCOLS - 1)
            here = ((jnp.broadcast_to(ro3[:, c : c + 1], (DETS, 128)) ^ lane) & (OWN - 1)) == 0
            mask_ref[sl, :] = jnp.where(here & (lane < 48), 1.0, 0.0)
            hparts.append(jnp.where(here & (lane >= 48) & (lane < 56), w, 0.0).astype(BF))
    zh_ref[...] = mm(zhot, jnp.concatenate(hparts, axis=0))
    zero = jnp.zeros((NMODE, 32), F32)
    rhs_ref[...] = jnp.concatenate(
        [zero, packs[0][:, :NMODE].T, packs[1][:, :NMODE].T, zero], axis=1
    )


def lanes_of(v, k):
    return jnp.broadcast_to(v[:, k : k + 1], (8, 128))


def solve(packed, rhs):
    n = NMODE
    groups = range(n // 8)
    full = jnp.concatenate(
        [packed] + [pltpu.roll(packed, 128 - n * i, 1) for i in groups[1:]], axis=0
    )
    row = lax.broadcasted_iota(jnp.int32, (n, 128), 0)
    lane = lax.broadcasted_iota(jnp.int32, (n, 128), 1)
    full = jnp.where(lane < n, full, rhs) + jnp.where(lane == row, 0.05, 0.0)
    diag = jnp.where(lane == row, full, 0.0)
    down = lax.rsqrt(jnp.sum(diag, axis=1, keepdims=True))
    along = jnp.sum(jnp.where(lane < n, diag, 1.0 / n), axis=0, keepdims=True)
    full = full * down * lax.rsqrt(along)
    a = [full[8 * i : 8 * i + 8, :] for i in groups]
    sub = lax.broadcasted_iota(jnp.int32, (8, 128), 0)
    for q in range(8):
        c = [[lanes_of(v, 8 * j + q) for v in a] for j in groups]
        p = [[c[j][i] for j in groups] for i in groups]
        i1 = 1.0 / (p[0][0] * p[1][1] - p[0][1] * p[0][1])
        e00, e01, e11 = p[1][1] * i1, -p[0][1] * i1, p[0][0] * i1
        w00 = e00 * p[0][2] + e01 * p[1][2]
        w01 = e00 * p[0][3] + e01 * p[1][3]
        w10 = e01 * p[0][2] + e11 * p[1][2]
        w11 = e01 * p[0][3] + e11 * p[1][3]
        s00 = p[2][2] - (p[0][2] * w00 + p[1][2] * w10)
        s01 = p[2][3] - (p[0][2] * w01 + p[1][2] * w11)
        s11 = p[3][3] - (p[0][3] * w01 + p[1][3] * w11)
        i2 = 1.0 / (s00 * s11 - s01 * s01)
        y0 = e00 * a[0] + e01 * a[1]
        y1 = e01 * a[0] + e11 * a[1]
        q2 = a[2] - (p[0][2] * y0 + p[1][2] * y1)
        q3 = a[3] - (p[0][3] * y0 + p[1][3] * y1)
        n2 = (s11 * q2 - s01 * q3) * i2
        n3 = (s00 * q3 - s01 * q2) * i2
        n0 = y0 - (w00 * n2 + w01 * n3)
        n1 = y1 - (w10 * n2 + w11 * n3)
        new = [jnp.broadcast_to(v[q : q + 1, :], (8, 128)) for v in (n0, n1, n2, n3)]
        a = [
            jnp.where(
                sub == q,
                new[i],
                a[i] - ((c[0][i] * new[0] + c[1][i] * new[1]) + (c[2][i] * new[2] + c[3][i] * new[3])),
            )
            for i in groups
        ]
    return jnp.concatenate(a, axis=0)[:, n : 3 * n] * down


def shifted_tiles(z, by):
    zero = jnp.zeros((z.shape[0], 1, 128), F32)
    if by < 0:
        return jnp.concatenate([zero, z[:, :-1]], axis=1)
    return jnp.concatenate([z[:, 1:], zero], axis=1)


def clean_kernel(
    core_ref, p_ref, q_ref, r_ref, s_ref, rhs_ref, w_ref, x_ref, other_ref, synth_ref, tw_ref,
    idx_ref, edge_ref, mask_ref, zhot_ref, zh_ref, hot_ref, other_hot_ref,
    blocks_ref, out_hbm, clean_ref, sem,
):
    p = (p_ref[...] + q_ref[...]) + (r_ref[...] + s_ref[...])
    coef = solve(p[2 * NMODE :, :], rhs_ref[...])
    ab = mm0_split(coef, jnp.concatenate([p[:NMODE, :], p[NMODE : 2 * NMODE, :]], axis=1))
    a = ab[:, :FKEEP]
    b = ab[:, FKEEP:]
    parts = []
    for c in range(NCHUNK):
        cos = tw_ref[c : c + 1, :FKEEP]
        sin = tw_ref[c : c + 1, FKEEP:]
        parts.append(jnp.concatenate([a * cos + b * sin, b * cos - a * sin], axis=1))
    hi, lo = split(jnp.concatenate(parts, axis=0))
    sh = synth_ref[:CHUNK, :]
    low = mm(hi, sh) + mm(lo, sh) + mm(hi, synth_ref[CHUNK:, :])
    runs = []
    for n, source in enumerate((x_ref, other_ref)):
        w = w_ref[n * DETS : (n + 1) * DETS, :]
        w = jnp.concatenate([w, w], axis=1)
        for c in range(NCHUNK):
            at = 2 * DETS * c + DETS * n
            part = w * (source[:, c * CHUNK : (c + 1) * CHUNK] - low[at : at + DETS, :])
            if n == 0:
                clean_ref[:, c * CHUNK : (c + 1) * CHUNK] = part
            runs.append(part[:, :RUN])
            runs.append(part[:, RUN:])
    copy = pltpu.make_async_copy(clean_ref, out_hbm, sem)
    copy.start()
    run = jnp.concatenate(runs, axis=0)
    vals = jnp.concatenate(
        split(jnp.take_along_axis(run, idx_ref[...], axis=1, mode="promise_in_bounds")), axis=1
    )
    evals = jnp.take_along_axis(run, edge_ref[...], axis=1, mode="promise_in_bounds")
    evals = jnp.concatenate(split(evals * mask_ref[...]), axis=1)
    s = mm(hot_ref[...], vals[:NRUNS]) + mm(other_hot_ref[...], vals[NRUNS:])
    blocks_ref[...] = s[:, :128] + s[:, 128:]
    z = mm(zhot_ref[...], evals)
    z = (z[:, :128] + z[:, 128:] + zh_ref[...]).reshape(ZROWS // NT, NT, 128)
    left = shifted_tiles(z, -1)
    right = shifted_tiles(z, 1)
    lane = lax.broadcasted_iota(jnp.int32, z.shape, 2)
    left_hits = left
    right_hits = jnp.concatenate([jnp.zeros(z.shape[:2] + (8,), F32), right[:, :, :-8]], axis=2)
    near = jnp.where(
        lane < 24, left, jnp.where(lane < 48, right, jnp.where(lane < 56, left_hits, right_hits))
    )
    near = jnp.where(lane < 64, near, 0.0)
    mine = jnp.where((lane >= 48) & (lane < 56), z, 0.0)
    nd = TROWS // OWN

    def both(v):
        return v[:nd] + jnp.concatenate([jnp.zeros((nd, NT, 64), F32), v[1:, :, :64]], axis=2)

    core = core_ref[0]
    for row, values in ((14, both(near)), (15, both(mine))):
        picked = [
            jnp.where(core == 1, values[2 * y + 1], values[2 * y]) for y in range(NY)
        ]
        blocks_ref[pl.ds(row, NBLK, stride=BROWS), :] = jnp.concatenate(picked, axis=0)
    copy.wait()


def beam_kernel(blocks_ref, out_ref):
    sums = [blocks_ref[b * BROWS : (b + 1) * BROWS, :] for b in range(4)]
    for b in range(4, NBLK):
        sums[b % 4] = sums[b % 4] + blocks_ref[b * BROWS : (b + 1) * BROWS, :]
    total = (sums[0] + sums[1]) + (sums[2] + sums[3])
    near = jnp.broadcast_to(total[14:15, :], (BROWS, 128))
    mine = jnp.broadcast_to(total[15:16, :], (BROWS, 128))
    i = lax.broadcasted_iota(jnp.int32, (BROWS, 128), 0)
    lane = lax.broadcasted_iota(jnp.int32, (BROWS, 128), 1)
    spot = jnp.where(i < OWN, i, 64 + i - OWN)

    def take(src, slot):
        return jnp.sum(jnp.where(lane == spot + 8 * slot, src, 0.0), axis=1, keepdims=True)

    left_hits = take(near, 6) + 1.0
    right_hits = take(near, 7) + 1.0
    hits = take(mine, 6) + 1.0
    valid = i < OWN + 2 * RADIUS
    binned = jnp.where(valid, total / hits, 0.0)
    left = [take(near, m) / left_hits for m in range(RADIUS)]
    right = [take(near, RADIUS + m) / right_hits for m in range(RADIUS)]
    taps = beam_taps()
    smooth = taps[RADIUS] * binned
    for m in range(1, RADIUS + 1):
        moved = pltpu.roll(binned, m, 1)
        for q in range(m):
            moved = jnp.where(lane == q, left[RADIUS - m + q], moved)
        smooth = smooth + taps[RADIUS - m] * moved
        moved = pltpu.roll(binned, TCOLS - m, 1)
        for q in range(m):
            moved = jnp.where(lane == TCOLS - m + q, right[q], moved)
        smooth = smooth + taps[RADIUS + m] * moved
    out = taps[0] * smooth[0:OWN, :]
    for m in range(1, 2 * RADIUS + 1):
        out = out + taps[m] * smooth[m : m + OWN, :]
    out_ref[...] = out


VMEM = pl.BlockSpec(memory_space=pltpu.VMEM)
SMEM = pl.BlockSpec(memory_space=pltpu.SMEM)
HBM = pl.BlockSpec(memory_space=pltpu.HBM)


def call(kernel, outs, specs, name, flops, *args, out_specs=None, scratch=()):
    args = [
        pltpu.with_memory_space_constraint(a, pltpu.HBM) if spec is HBM else a
        for a, spec in zip(args, specs)
    ]
    nbytes = sum(math.prod(s.shape) * 4 for s in outs) + sum(a.size * 4 for a in args)
    return pl.pallas_call(
        kernel,
        out_shape=outs,
        in_specs=specs,
        out_specs=out_specs or [VMEM] * len(outs),
        scratch_shapes=list(scratch),
        name=name,
        compiler_params=pltpu.CompilerParams(vmem_limit_bytes=40 << 20),
        cost_estimate=pl.CostEstimate(flops=flops, bytes_accessed=nbytes, transcendentals=0),
    )(*args)


def sds(shape, dtype=F32):
    return jax.ShapeDtypeStruct(shape, dtype)


I32 = jnp.int32


def body(timestreams, templates, validity, tile_index, row_offset, col_start):
    basis, synth, tw = tables()
    core = lax.axis_index("core").reshape(1)
    small = (DETS, SEG // RUN)
    big = (NBLK * BROWS, NRUNS)
    swap = [(0, 1), (1, 0)]
    mate_x = lax.ppermute(timestreams, "core", swap)
    part, x, synth, tw, pack = call(
        analysis_kernel,
        [
            sds((2 * NMODE + 8, FKEEP)), sds((DETS, SEG)), sds((2 * CHUNK, 2 * FKEEP), BF),
            sds((NCHUNK, 2 * FKEEP)), sds((DETS, 128)),
        ],
        [HBM] * 9, "analysis", 400_000_000,
        timestreams, templates, validity.reshape(1, DETS), tile_index, row_offset, col_start,
        jnp.asarray(basis), jnp.asarray(synth), jnp.asarray(tw),
        scratch=[
            pltpu.VMEM((DETS, NMODE), F32), pltpu.VMEM((1, DETS), I32), pltpu.VMEM(small, I32),
            pltpu.VMEM(small, I32), pltpu.VMEM(small, I32),
            pltpu.VMEM((2 * CHUNK, 2 * FKEEP), BF), pltpu.SemaphoreType.DMA((8 + SEG // XPIECE,)),
        ],
    )
    mate = lax.ppermute(part, "core", swap)
    hot, line = call(
        first_index_kernel, [sds(big, BF), sds((1, NRUNS), I32)], [SMEM, VMEM], "index1",
        100_000_000, core, pack,
    )
    mate_pack = lax.ppermute(pack, "core", swap)
    part, hot, line, mate_pack = lax.optimization_barrier((part + mate, hot, line, mate_pack))
    others = [
        lax.ppermute(part, "y", [(k, (k + m) % NY) for k in range(NY)]) for m in (1, 3, 2)
    ]
    twice = (2 * NRUNS, 128)
    mate_hot, zhot, idx, edge, mask, zh, rhs, w = call(
        second_index_kernel,
        [
            sds(big, BF), sds((ZROWS, 2 * NRUNS), BF), sds(twice, I32), sds(twice, I32),
            sds(twice), sds((ZROWS, 128)), sds((NMODE, 128)), sds((2 * DETS, 128)),
        ],
        [SMEM] + [VMEM] * 3, "index2", 100_000_000,
        core, line, pack, mate_pack,
    )
    blocks, cleaned = call(
        clean_kernel,
        [sds((NBLK * BROWS, 128)), sds((DETS, SEG))],
        [SMEM] + [VMEM] * 17, "clean", 2_000_000_000,
        core, part, *others, rhs, w, x, mate_x, synth, tw, idx, edge, mask, zhot, zh, hot, mate_hot,
        out_specs=[VMEM, HBM],
        scratch=[pltpu.VMEM((DETS, SEG), F32), pltpu.SemaphoreType.DMA],
    )
    blocks = lax.all_to_all(blocks, ("y", "z", "x"), 0, 0, tiled=True)
    (beamed,) = call(
        beam_kernel, [sds((OWN, TCOLS))], [VMEM], "beam", 1_000_000, blocks
    )
    return (cleaned, beamed)


def solution(mesh):
    fine = Mesh(mesh.devices.reshape(NY, 2, 4, 4), ("y", "core", "z", "x"))
    det, tm = ("y", "core"), ("z", "x")
    in_specs = (P(det, tm), P(det, None), P(det), P(det, tm), P(det, tm), P(det, tm))
    out_specs = (P(det, tm), P(det, tm))
    return jax.shard_map(body, mesh=fine, in_specs=in_specs, out_specs=out_specs, check_vma=False)
```

```python
import math

import jax
import jax.numpy as jnp
import numpy as np
from jax import lax
from jax.experimental import pallas as pl
from jax.experimental.pallas import tpu as pltpu
from jax.sharding import Mesh
from jax.sharding import PartitionSpec as P
import ml_dtypes

SEG = 4096
NMODE = 32
FKEEP = 128
RUN = 128
TROWS = 64
TCOLS = 128
RADIUS = 3
DETS = 32
CHUNK = 256
NCHUNK = SEG // CHUNK
WIDE = 1024
NRUNS = DETS * SEG // RUN
NT = 16
NY = 4
OWN = 8
BROWS = 16
NBLK = NY * NT
ZROWS = (TROWS // OWN + 1) * NT
BF = jnp.bfloat16
F32 = jnp.float32
I32 = jnp.int32
PART = 2 * NMODE + 8


def split_np(a):
    hi = a.astype(np.float32).astype(ml_dtypes.bfloat16)
    lo = (a - hi.astype(np.float64)).astype(np.float32).astype(ml_dtypes.bfloat16)
    return hi, lo


def tables():
    j = np.arange(CHUNK)[:, None]
    k = np.arange(FKEEP)[None, :]
    phi = 2.0 * np.pi * (j * k % SEG) / SEG
    basis = np.concatenate([np.cos(phi), np.sin(phi)], axis=1)
    c = np.arange(NCHUNK)[:, None]
    theta = 2.0 * np.pi * (c * CHUNK * k % SEG) / SEG
    twiddle = np.concatenate([np.cos(theta), np.sin(theta)], axis=1).astype(np.float32)
    scale = np.where(np.arange(FKEEP) == 0, 1.0 / SEG, 2.0 / SEG)
    phi = 2.0 * np.pi * (np.arange(WIDE)[:, None] * k % SEG) / SEG
    synth = np.concatenate([np.cos(phi), np.sin(phi)], axis=1).T
    synth = synth * np.concatenate([scale, scale])[:, None]
    return np.concatenate(split_np(basis)), np.concatenate(split_np(synth)), twiddle


def beam_taps():
    values = [math.exp(-(m * m) / 4.5) for m in range(-RADIUS, RADIUS + 1)]
    total = sum(values)
    return [v / total for v in values]


def split(a):
    hi = a.astype(BF)
    return hi, (a - hi.astype(F32)).astype(BF)


def mm(a, b):
    return jnp.dot(a, b, preferred_element_type=F32)


def mm0(a, b):
    return lax.dot_general(
        a, b, (((0,), (0,)), ((), ())), precision=lax.Precision.HIGHEST,
        preferred_element_type=F32,
    )


def mm0_split(a, b):
    ah, al = split(a)
    bh, bl = split(b)
    return lax.dot_general(
        jnp.concatenate([ah, al, ah], axis=0), jnp.concatenate([bh, bh, bl], axis=0),
        (((0,), (0,)), ((), ())), preferred_element_type=F32,
    )


def column(row, n):
    full = jnp.broadcast_to(row, (n, row.shape[1]))
    same = lax.broadcasted_iota(jnp.int32, full.shape, 0) == lax.broadcasted_iota(
        jnp.int32, full.shape, 1
    )
    return jnp.sum(jnp.where(same, full, 0.0), axis=1, keepdims=True)


def run_row(ids):
    flat = ids.astype(F32).T
    parts = [flat[c : c + 1, :] for c in range(SEG // RUN)]
    return jnp.concatenate(parts, axis=1).astype(jnp.int32)


def analysis_kernel(
    x_hbm, t_hbm, v_hbm, ti_hbm, ro_hbm, cs_hbm, basis_hbm, synth_hbm, tw_hbm,
    out_ref, x_ref, synth_ref, tw_ref, line_ref,
    t_ref, v_ref, ti_ref, ro_ref, cs_ref, basis_ref, sems,
):
    copies = [
        pltpu.make_async_copy(src, dst, sems.at[n])
        for n, (src, dst) in enumerate(
            [
                (t_hbm, t_ref), (v_hbm, v_ref), (basis_hbm, basis_ref), (x_hbm, x_ref),
                (ti_hbm, ti_ref), (ro_hbm, ro_ref), (cs_hbm, cs_ref),
                (tw_hbm, tw_ref), (synth_hbm, synth_ref),
            ]
        )
    ]
    for copy in copies:
        copy.start()
    copies[0].wait()
    copies[1].wait()
    w = column(v_ref[...].astype(F32), DETS)
    t = t_ref[...]
    wt = t * w
    gram = mm0(wt, t)
    out_ref[2 * NMODE : PART, :] = jnp.concatenate(
        [gram[8 * i : 8 * i + 8, :] for i in range(NMODE // 8)], axis=1
    )
    for copy in copies[-5:-2]:
        copy.wait()
    line = ti_ref[...] * TROWS + ro_ref[...]
    line_ref[...] = run_row(line)
    out_ref[PART:, :] = jnp.concatenate(
        [t, line.astype(F32), cs_ref[...].astype(F32), jnp.broadcast_to(w, (DETS, 32))], axis=1
    )
    copies[2].wait()
    eh = basis_ref[:CHUNK, :]
    el = basis_ref[CHUNK:, :]
    copies[3].wait()
    wide = jnp.broadcast_to(w, (DETS, CHUNK))
    x = jnp.concatenate(
        [wide * x_ref[:, c * CHUNK : (c + 1) * CHUNK] for c in range(NCHUNK)], axis=0
    )
    hi, lo = split(x)
    y = mm(hi, eh) + mm(lo, eh) + mm(hi, el)
    copies[-2].wait()
    re = jnp.zeros((DETS, FKEEP), F32)
    im = jnp.zeros((DETS, FKEEP), F32)
    for c in range(NCHUNK):
        sl = slice(c * DETS, (c + 1) * DETS)
        yc = y[sl, :FKEEP]
        yi = y[sl, FKEEP:]
        cos = tw_ref[c : c + 1, :FKEEP]
        sin = tw_ref[c : c + 1, FKEEP:]
        re = re + (cos * yc - sin * yi)
        im = im + (sin * yc + cos * yi)
    both = mm0_split(wt, jnp.concatenate([re, im], axis=1))
    out_ref[:NMODE, :] = both[:, :FKEEP]
    out_ref[NMODE : 2 * NMODE, :] = both[:, FKEEP:]
    copies[-1].wait()


def edge_col(lane):
    slot = lane >> 3
    return jnp.where(slot < 3, TCOLS - RADIUS + slot, slot - 3)


def ids_of_blocks(core):
    l = lax.broadcasted_iota(jnp.int32, (NBLK * BROWS, 128), 0)
    i = l & (BROWS - 1)
    b = l >> 4
    row = (b >> 4) * (2 * OWN) + core * OWN - RADIUS + i
    ok = (i < OWN + 2 * RADIUS) & (row >= 0) & (row < TROWS)
    return jnp.where(ok, (b & (NT - 1)) * TROWS + row, -1)


def fill_hot(ref, ids, line):
    for q in range(NRUNS // 128):
        sl = slice(q * 128, (q + 1) * 128)
        ref[:, sl] = jnp.where(ids == line[:, sl], 1.0, 0.0).astype(BF)


def first_index_kernel(core_ref, line_ref, hot_ref):
    fill_hot(hot_ref, ids_of_blocks(core_ref[0]), line_ref[...])


def shifted_tiles(z, by):
    zero = jnp.zeros((z.shape[0], 1, 128), F32)
    if by < 0:
        return jnp.concatenate([zero, z[:, :-1]], axis=1)
    return jnp.concatenate([z[:, 1:], zero], axis=1)


def second_index_kernel(
    core_ref, line_ref, mine_ref, other_ref, hot_ref, idx_ref, hits_ref, rhs_ref, w_ref
):
    core = core_ref[0]
    packs = (mine_ref[PART:, :], other_ref[PART:, :])
    lines = [pack[:, 32:64].astype(jnp.int32) for pack in packs]
    rows = (line_ref[...], run_row(lines[1]))
    fill_hot(hot_ref, ids_of_blocks(core), rows[1])
    line = jnp.concatenate(rows, axis=1)
    zid = (((line & (TROWS - 1)) + RADIUS) >> 3) * NT + (line >> 6)
    zl = lax.broadcasted_iota(jnp.int32, (ZROWS, 2 * NRUNS), 0)
    zhot = jnp.where(zl == zid, 1.0, 0.0).astype(BF)
    lane = lax.broadcasted_iota(jnp.int32, (DETS, 128), 1)
    hparts = []
    for n, pack in enumerate(packs):
        w = jnp.broadcast_to(pack[:, 96:97], (DETS, 128))
        w_ref[n * DETS : (n + 1) * DETS, :] = w
        spot = ((lines[n] + RADIUS) & (OWN - 1)) + 48
        css = pack[:, 64:96].astype(jnp.int32)
        for c in range(SEG // RUN):
            sl = slice(n * NRUNS + c * DETS, n * NRUNS + (c + 1) * DETS)
            cs = jnp.broadcast_to(css[:, c : c + 1], (DETS, 128))
            idx_ref[sl, :] = (lane - cs) & (TCOLS - 1)
            here = jnp.broadcast_to(spot[:, c : c + 1], (DETS, 128)) == lane
            hparts.append(jnp.where(here, w, 0.0).astype(BF))
    z = mm(zhot, jnp.concatenate(hparts, axis=0)).reshape(ZROWS // NT, NT, 128)
    right = shifted_tiles(z, 1)
    right = jnp.concatenate([jnp.zeros(z.shape[:2] + (8,), F32), right[:, :, :-8]], axis=2)
    nd = TROWS // OWN
    for n, v in enumerate((shifted_tiles(z, -1) + right, z)):
        moved = jnp.concatenate([jnp.zeros((nd, NT, 64), F32), v[1:, :, :64]], axis=2)
        v = v[:nd] + moved
        picked = [jnp.where(core == 1, v[2 * y + 1], v[2 * y]) for y in range(NY)]
        hits_ref[n * NBLK : (n + 1) * NBLK, :] = jnp.concatenate(picked, axis=0)
    zero = jnp.zeros((NMODE, 32), F32)
    rhs_ref[...] = jnp.concatenate(
        [zero, packs[0][:, :NMODE].T, packs[1][:, :NMODE].T, zero], axis=1
    )


def lanes_of(v, k):
    return jnp.broadcast_to(v[:, k : k + 1], (8, 128))


def solve(packed, rhs):
    n = NMODE
    groups = range(n // 8)
    full = jnp.concatenate(
        [packed] + [pltpu.roll(packed, 128 - n * i, 1) for i in groups[1:]], axis=0
    )
    row = lax.broadcasted_iota(jnp.int32, (n, 128), 0)
    lane = lax.broadcasted_iota(jnp.int32, (n, 128), 1)
    full = jnp.where(lane < n, full, rhs) + jnp.where(lane == row, 0.05, 0.0)
    diag = jnp.where(lane == row, full, 0.0)
    down = lax.rsqrt(jnp.sum(diag, axis=1, keepdims=True))
    along = jnp.sum(jnp.where(lane < n, diag, 1.0 / n), axis=0, keepdims=True)
    full = full * down * lax.rsqrt(along)
    a = [full[8 * i : 8 * i + 8, :] for i in groups]
    sub = lax.broadcasted_iota(jnp.int32, (8, 128), 0)
    for q in range(8):
        c = [[lanes_of(v, 8 * j + q) for v in a] for j in groups]
        p = [[c[j][i] for j in groups] for i in groups]
        i1 = 1.0 / (p[0][0] * p[1][1] - p[0][1] * p[0][1])
        e00, e01, e11 = p[1][1] * i1, -p[0][1] * i1, p[0][0] * i1
        w00 = e00 * p[0][2] + e01 * p[1][2]
        w01 = e00 * p[0][3] + e01 * p[1][3]
        w10 = e01 * p[0][2] + e11 * p[1][2]
        w11 = e01 * p[0][3] + e11 * p[1][3]
        s00 = p[2][2] - (p[0][2] * w00 + p[1][2] * w10)
        s01 = p[2][3] - (p[0][2] * w01 + p[1][2] * w11)
        s11 = p[3][3] - (p[0][3] * w01 + p[1][3] * w11)
        i2 = 1.0 / (s00 * s11 - s01 * s01)
        y0 = e00 * a[0] + e01 * a[1]
        y1 = e01 * a[0] + e11 * a[1]
        q2 = a[2] - (p[0][2] * y0 + p[1][2] * y1)
        q3 = a[3] - (p[0][3] * y0 + p[1][3] * y1)
        n2 = (s11 * q2 - s01 * q3) * i2
        n3 = (s00 * q3 - s01 * q2) * i2
        n0 = y0 - (w00 * n2 + w01 * n3)
        n1 = y1 - (w10 * n2 + w11 * n3)
        new = [jnp.broadcast_to(v[q : q + 1, :], (8, 128)) for v in (n0, n1, n2, n3)]
        a = [
            jnp.where(
                sub == q,
                new[i],
                a[i] - ((c[0][i] * new[0] + c[1][i] * new[1]) + (c[2][i] * new[2] + c[3][i] * new[3])),
            )
            for i in groups
        ]
    return jnp.concatenate(a, axis=0)[:, n : 3 * n] * down


def edge_rows(s):
    lane = lax.broadcasted_iota(jnp.int32, s.shape, 1)
    moved = jnp.take_along_axis(s, edge_col(lane & 63), axis=1, mode="promise_in_bounds")
    moved = moved.reshape(NBLK, 2, 8, 128)
    sub = lax.broadcasted_iota(jnp.int32, (NBLK, 8, 128), 1)
    lane = lax.broadcasted_iota(jnp.int32, (NBLK, 8, 128), 2)
    moved = jnp.where(lane < 64, moved[:, 0], moved[:, 1])
    here = ((lane & 7) == sub) & ((lane & 63) < 48)
    return jnp.sum(jnp.where(here, moved, 0.0), axis=1)


def clean_kernel(
    p_ref, q_ref, r_ref, s_ref, rhs_ref, w_ref, x_ref, other_ref, synth_ref, tw_ref,
    idx_ref, hits_ref, hot_ref, other_hot_ref,
    blocks_ref, out_hbm, clean_ref, sem,
):
    p = (p_ref[...] + q_ref[...]) + (r_ref[...] + s_ref[...])
    coef = solve(p[2 * NMODE :, :], rhs_ref[...])
    ab = mm0_split(coef, jnp.concatenate([p[:NMODE, :], p[NMODE : 2 * NMODE, :]], axis=1))
    a = ab[:, :FKEEP]
    b = ab[:, FKEEP:]
    parts = []
    for c in range(SEG // WIDE):
        at = c * WIDE // CHUNK
        cos = tw_ref[at : at + 1, :FKEEP]
        sin = tw_ref[at : at + 1, FKEEP:]
        parts.append(jnp.concatenate([a * cos + b * sin, b * cos - a * sin], axis=1))
    hi, lo = split(jnp.concatenate(parts, axis=0))
    sh = synth_ref[: 2 * FKEEP, :]
    low = mm(hi, sh) + mm(lo, sh) + mm(hi, synth_ref[2 * FKEEP :, :])
    runs = []
    for n, source in enumerate((x_ref, other_ref)):
        w = w_ref[n * DETS : (n + 1) * DETS, :]
        for r in range(SEG // RUN):
            at = 2 * DETS * (r * RUN // WIDE) + DETS * n
            col = r * RUN % WIDE
            part = w * (source[:, r * RUN : (r + 1) * RUN] - low[at : at + DETS, col : col + RUN])
            if n == 0:
                clean_ref[:, r * RUN : (r + 1) * RUN] = part
            runs.append(part)
    copy = pltpu.make_async_copy(clean_ref, out_hbm, sem)
    copy.start()
    run = jnp.concatenate(runs, axis=0)
    vals = jnp.concatenate(
        split(jnp.take_along_axis(run, idx_ref[...], axis=1, mode="promise_in_bounds")), axis=1
    )
    s = mm(hot_ref[...], vals[:NRUNS]) + mm(other_hot_ref[...], vals[NRUNS:])
    s = s[:, :128] + s[:, 128:]
    blocks_ref[...] = s
    edges = edge_rows(s)
    tile = lax.broadcasted_iota(jnp.int32, edges.shape, 0) & (NT - 1)
    slot = (lax.broadcasted_iota(jnp.int32, edges.shape, 1) & 63) >> 3
    zero = jnp.zeros((1, 128), F32)
    left = jnp.where(tile == 0, 0.0, jnp.concatenate([zero, edges[:-1]], axis=0))
    right = jnp.where(tile == NT - 1, 0.0, jnp.concatenate([edges[1:], zero], axis=0))
    near = jnp.where(slot < RADIUS, left, right) + hits_ref[:NBLK, :]
    blocks_ref[pl.ds(14, NBLK, stride=BROWS), :] = near
    blocks_ref[pl.ds(15, NBLK, stride=BROWS), :] = hits_ref[NBLK:, :]
    copy.wait()


def beam_kernel(blocks_ref, out_ref):
    sums = [blocks_ref[b * BROWS : (b + 1) * BROWS, :] for b in range(4)]
    for b in range(4, NBLK):
        sums[b % 4] = sums[b % 4] + blocks_ref[b * BROWS : (b + 1) * BROWS, :]
    total = (sums[0] + sums[1]) + (sums[2] + sums[3])
    near = jnp.broadcast_to(total[14:15, :], (BROWS, 128))
    mine = jnp.broadcast_to(total[15:16, :], (BROWS, 128))
    i = lax.broadcasted_iota(jnp.int32, (BROWS, 128), 0)
    lane = lax.broadcasted_iota(jnp.int32, (BROWS, 128), 1)
    spot = jnp.where(i < OWN, i, 64 + i - OWN)

    def take(src, slot):
        return jnp.sum(jnp.where(lane == spot + 8 * slot, src, 0.0), axis=1, keepdims=True)

    left_hits = take(near, 6) + 1.0
    right_hits = take(near, 7) + 1.0
    hits = take(mine, 6) + 1.0
    valid = i < OWN + 2 * RADIUS
    binned = jnp.where(valid, total / hits, 0.0)
    left = [take(near, m) / left_hits for m in range(RADIUS)]
    right = [take(near, RADIUS + m) / right_hits for m in range(RADIUS)]
    taps = beam_taps()
    smooth = taps[RADIUS] * binned
    for m in range(1, RADIUS + 1):
        moved = pltpu.roll(binned, m, 1)
        for q in range(m):
            moved = jnp.where(lane == q, left[RADIUS - m + q], moved)
        smooth = smooth + taps[RADIUS - m] * moved
        moved = pltpu.roll(binned, TCOLS - m, 1)
        for q in range(m):
            moved = jnp.where(lane == TCOLS - m + q, right[q], moved)
        smooth = smooth + taps[RADIUS + m] * moved
    out = taps[0] * smooth[0:OWN, :]
    for m in range(1, 2 * RADIUS + 1):
        out = out + taps[m] * smooth[m : m + OWN, :]
    out_ref[...] = out


VMEM = pl.BlockSpec(memory_space=pltpu.VMEM)
SMEM = pl.BlockSpec(memory_space=pltpu.SMEM)
HBM = pl.BlockSpec(memory_space=pltpu.HBM)


def call(kernel, outs, specs, name, flops, *args, out_specs=None, scratch=()):
    args = [
        pltpu.with_memory_space_constraint(a, pltpu.HBM) if spec is HBM else a
        for a, spec in zip(args, specs)
    ]
    nbytes = sum(math.prod(s.shape) * 4 for s in outs) + sum(a.size * 4 for a in args)
    return pl.pallas_call(
        kernel,
        out_shape=outs,
        in_specs=specs,
        out_specs=out_specs or [VMEM] * len(outs),
        scratch_shapes=list(scratch),
        name=name,
        compiler_params=pltpu.CompilerParams(vmem_limit_bytes=40 << 20),
        cost_estimate=pl.CostEstimate(flops=flops, bytes_accessed=nbytes, transcendentals=0),
    )(*args)


def sds(shape, dtype=F32):
    return jax.ShapeDtypeStruct(shape, dtype)


def body(timestreams, templates, validity, tile_index, row_offset, col_start):
    basis, synth, tw = tables()
    core = lax.axis_index("core").reshape(1)
    small = (DETS, SEG // RUN)
    big = (NBLK * BROWS, NRUNS)
    swap = [(0, 1), (1, 0)]
    mate_x = lax.ppermute(timestreams, "core", swap)
    part, x, synth, tw, line = call(
        analysis_kernel,
        [
            sds((PART + DETS, FKEEP)), sds((DETS, SEG)), sds((4 * FKEEP, WIDE), BF),
            sds((NCHUNK, 2 * FKEEP)), sds((1, NRUNS), I32),
        ],
        [HBM] * 9, "analysis", 400_000_000,
        timestreams, templates, validity.reshape(1, DETS), tile_index, row_offset, col_start,
        jnp.asarray(basis), jnp.asarray(synth), jnp.asarray(tw),
        scratch=[
            pltpu.VMEM((DETS, NMODE), F32), pltpu.VMEM((1, DETS), I32), pltpu.VMEM(small, I32),
            pltpu.VMEM(small, I32), pltpu.VMEM(small, I32),
            pltpu.VMEM((2 * CHUNK, 2 * FKEEP), BF), pltpu.SemaphoreType.DMA((9,)),
        ],
    )
    mate = lax.ppermute(part, "core", swap)
    (hot,) = call(
        first_index_kernel, [sds(big, BF)], [SMEM, VMEM], "index1", 100_000_000, core, line
    )
    sums, hot, line = lax.optimization_barrier((part[:PART] + mate[:PART], hot, line))
    others = [lax.ppermute(sums, "y", [(k, k ^ m) for k in range(NY)]) for m in (2, 3, 1)]
    mate_hot, idx, hits, rhs, w = call(
        second_index_kernel,
        [
            sds(big, BF), sds((2 * NRUNS, 128), I32), sds((2 * NBLK, 128)),
            sds((NMODE, 128)), sds((2 * DETS, 128)),
        ],
        [SMEM] + [VMEM] * 3, "index2", 100_000_000,
        core, line, part, mate,
    )
    blocks, cleaned = call(
        clean_kernel,
        [sds((NBLK * BROWS, 128)), sds((DETS, SEG))],
        [VMEM] * 14, "clean", 2_000_000_000,
        sums, *others, rhs, w, x, mate_x, synth, tw, idx, hits, hot, mate_hot,
        out_specs=[VMEM, HBM],
        scratch=[pltpu.VMEM((DETS, SEG), F32), pltpu.SemaphoreType.DMA],
    )
    blocks = lax.all_to_all(blocks, ("y", "z", "x"), 0, 0, tiled=True)
    (beamed,) = call(
        beam_kernel, [sds((OWN, TCOLS))], [VMEM], "beam", 1_000_000, blocks
    )
    return (cleaned, beamed)


def solution(mesh):
    fine = Mesh(mesh.devices.reshape(NY, 2, 4, 4), ("y", "core", "z", "x"))
    det, tm = ("y", "core"), ("z", "x")
    in_specs = (P(det, tm), P(det, None), P(det), P(det, tm), P(det, tm), P(det, tm))
    out_specs = (P(det, tm), P(det, tm))
    return jax.shard_map(body, mesh=fine, in_specs=in_specs, out_specs=out_specs, check_vma=False)
```

```python
import math

import jax
import jax.numpy as jnp
import numpy as np
from jax import lax
from jax.experimental import pallas as pl
from jax.experimental.pallas import tpu as pltpu
from jax.sharding import Mesh
from jax.sharding import PartitionSpec as P
import ml_dtypes

SEG = 4096
NMODE = 32
FKEEP = 128
RUN = 128
TROWS = 64
TCOLS = 128
RADIUS = 3
DETS = 32
CHUNK = 256
NCHUNK = SEG // CHUNK
WIDE = 1024
NRUNS = DETS * SEG // RUN
NT = 16
NY = 4
OWN = 8
BROWS = 16
NBLK = NY * NT
ZROWS = (TROWS // OWN + 1) * NT
BF = jnp.bfloat16
F32 = jnp.float32
I32 = jnp.int32
FIRST = 512
PART = 2 * NMODE + 8


def split_np(a):
    hi = a.astype(np.float32).astype(ml_dtypes.bfloat16)
    lo = (a - hi.astype(np.float64)).astype(np.float32).astype(ml_dtypes.bfloat16)
    return hi, lo


def tables():
    j = np.arange(CHUNK)[:, None]
    k = np.arange(FKEEP)[None, :]
    phi = 2.0 * np.pi * (j * k % SEG) / SEG
    basis = np.concatenate([np.cos(phi), np.sin(phi)], axis=1)
    c = np.arange(NCHUNK)[:, None]
    theta = 2.0 * np.pi * (c * CHUNK * k % SEG) / SEG
    twiddle = np.concatenate([np.cos(theta), np.sin(theta)], axis=1).astype(np.float32)
    scale = np.where(np.arange(FKEEP) == 0, 1.0 / SEG, 2.0 / SEG)
    phi = 2.0 * np.pi * (np.arange(WIDE)[:, None] * k % SEG) / SEG
    synth = np.concatenate([np.cos(phi), np.sin(phi)], axis=1).T
    synth = synth * np.concatenate([scale, scale])[:, None]
    return np.concatenate(split_np(basis)), np.concatenate(split_np(synth)), twiddle


def beam_taps():
    values = [math.exp(-(m * m) / 4.5) for m in range(-RADIUS, RADIUS + 1)]
    total = sum(values)
    return [v / total for v in values]


def split(a):
    hi = a.astype(BF)
    return hi, (a - hi.astype(F32)).astype(BF)


def mm(a, b):
    return jnp.dot(a, b, preferred_element_type=F32)


def mm0(a, b):
    return lax.dot_general(
        a, b, (((0,), (0,)), ((), ())), precision=lax.Precision.HIGHEST,
        preferred_element_type=F32,
    )


def mm0_split(a, b):
    ah, al = split(a)
    bh, bl = split(b)
    return lax.dot_general(
        jnp.concatenate([ah, al, ah], axis=0), jnp.concatenate([bh, bh, bl], axis=0),
        (((0,), (0,)), ((), ())), preferred_element_type=F32,
    )


def column(row, n):
    full = jnp.broadcast_to(row, (n, row.shape[1]))
    same = lax.broadcasted_iota(jnp.int32, full.shape, 0) == lax.broadcasted_iota(
        jnp.int32, full.shape, 1
    )
    return jnp.sum(jnp.where(same, full, 0.0), axis=1, keepdims=True)


def run_row(ids):
    flat = ids.astype(F32).T
    parts = [flat[c : c + 1, :] for c in range(SEG // RUN)]
    return jnp.concatenate(parts, axis=1).astype(jnp.int32)


def analysis_kernel(
    x_hbm, t_hbm, v_hbm, ti_hbm, ro_hbm, cs_hbm, basis_hbm, synth_hbm, tw_hbm,
    out_ref, x_ref, synth_ref, tw_ref, line_ref,
    t_ref, v_ref, ti_ref, ro_ref, cs_ref, basis_ref, sems,
):
    copies = [
        pltpu.make_async_copy(src, dst, sems.at[n])
        for n, (src, dst) in enumerate(
            [
                (t_hbm, t_ref), (v_hbm, v_ref), (basis_hbm, basis_ref), (x_hbm, x_ref),
                (ti_hbm, ti_ref), (ro_hbm, ro_ref), (cs_hbm, cs_ref),
                (tw_hbm, tw_ref), (synth_hbm, synth_ref),
            ]
        )
    ]
    for copy in copies:
        copy.start()
    copies[0].wait()
    copies[1].wait()
    copies[2].wait()
    copies[3].wait()
    copies[4].wait()
    copies[5].wait()
    copies[6].wait()
    copies[7].wait()
    w = column(v_ref[...].astype(F32), DETS)
    t = t_ref[...]
    wt = t * w
    eh = basis_ref[:CHUNK, :]
    el = basis_ref[CHUNK:, :]
    wide = jnp.broadcast_to(w, (DETS, CHUNK))
    x = jnp.concatenate(
        [wide * x_ref[:, c * CHUNK : (c + 1) * CHUNK] for c in range(NCHUNK)], axis=0
    )
    hi, lo = split(x)
    y = mm(hi, eh) + mm(lo, eh) + mm(hi, el)
    gram = mm0(wt, t)
    out_ref[2 * NMODE : PART, :] = jnp.concatenate(
        [gram[8 * i : 8 * i + 8, :] for i in range(NMODE // 8)], axis=1
    )
    line = ti_ref[...] * TROWS + ro_ref[...]
    line_ref[...] = run_row(line)
    out_ref[PART:, :] = jnp.concatenate(
        [t, line.astype(F32), cs_ref[...].astype(F32), jnp.broadcast_to(w, (DETS, 32))], axis=1
    )
    re = jnp.zeros((DETS, FKEEP), F32)
    im = jnp.zeros((DETS, FKEEP), F32)
    for c in range(NCHUNK):
        sl = slice(c * DETS, (c + 1) * DETS)
        yc = y[sl, :FKEEP]
        yi = y[sl, FKEEP:]
        cos = tw_ref[c : c + 1, :FKEEP]
        sin = tw_ref[c : c + 1, FKEEP:]
        re = re + (cos * yc - sin * yi)
        im = im + (sin * yc + cos * yi)
    both = mm0_split(wt, jnp.concatenate([re, im], axis=1))
    out_ref[:NMODE, :] = both[:, :FKEEP]
    out_ref[NMODE : 2 * NMODE, :] = both[:, FKEEP:]
    copies[8].wait()


def edge_col(lane):
    slot = lane >> 3
    return jnp.where(slot < 3, TCOLS - RADIUS + slot, slot - 3)


def ids_of_blocks(core):
    l = lax.broadcasted_iota(jnp.int32, (NBLK * BROWS, 128), 0)
    i = l & (BROWS - 1)
    b = l >> 4
    row = (b >> 4) * (2 * OWN) + core * OWN - RADIUS + i
    ok = (i < OWN + 2 * RADIUS) & (row >= 0) & (row < TROWS)
    return jnp.where(ok, (b & (NT - 1)) * TROWS + row, -1)


def fill_hot(ref, ids, line):
    for q in range(line.shape[1] // 128):
        sl = slice(q * 128, (q + 1) * 128)
        ref[:, sl] = jnp.where(ids == line[:, sl], 1.0, 0.0).astype(BF)


def first_index_kernel(core_ref, line_ref, hot_ref):
    fill_hot(hot_ref, ids_of_blocks(core_ref[0]), line_ref[:, :FIRST])


def shifted_tiles(z, by):
    zero = jnp.zeros((z.shape[0], 1, 128), F32)
    if by < 0:
        return jnp.concatenate([zero, z[:, :-1]], axis=1)
    return jnp.concatenate([z[:, 1:], zero], axis=1)


def second_index_kernel(
    core_ref, line_ref, mine_ref, other_ref, hot_ref, idx_ref, hits_ref, rhs_ref, w_ref
):
    core = core_ref[0]
    packs = (mine_ref[PART:, :], other_ref[PART:, :])
    lines = [pack[:, 32:64].astype(jnp.int32) for pack in packs]
    rows = (line_ref[...], run_row(lines[1]))
    line = jnp.concatenate(rows, axis=1)
    fill_hot(hot_ref, ids_of_blocks(core), line[:, FIRST:])
    zid = (((line & (TROWS - 1)) + RADIUS) >> 3) * NT + (line >> 6)
    zl = lax.broadcasted_iota(jnp.int32, (ZROWS, 2 * NRUNS), 0)
    zhot = jnp.where(zl == zid, 1.0, 0.0).astype(BF)
    lane = lax.broadcasted_iota(jnp.int32, (DETS, 128), 1)
    hparts = []
    for n, pack in enumerate(packs):
        w = jnp.broadcast_to(pack[:, 96:97], (DETS, 128))
        w_ref[n * DETS : (n + 1) * DETS, :] = w
        spot = ((lines[n] + RADIUS) & (OWN - 1)) + 48
        css = pack[:, 64:96].astype(jnp.int32)
        for c in range(SEG // RUN):
            sl = slice(n * NRUNS + c * DETS, n * NRUNS + (c + 1) * DETS)
            cs = jnp.broadcast_to(css[:, c : c + 1], (DETS, 128))
            idx_ref[sl, :] = (lane - cs) & (TCOLS - 1)
            here = jnp.broadcast_to(spot[:, c : c + 1], (DETS, 128)) == lane
            hparts.append(jnp.where(here, w, 0.0).astype(BF))
    z = mm(zhot, jnp.concatenate(hparts, axis=0)).reshape(ZROWS // NT, NT, 128)
    right = shifted_tiles(z, 1)
    right = jnp.concatenate([jnp.zeros(z.shape[:2] + (8,), F32), right[:, :, :-8]], axis=2)
    nd = TROWS // OWN
    for n, v in enumerate((shifted_tiles(z, -1) + right, z)):
        moved = jnp.concatenate([jnp.zeros((nd, NT, 64), F32), v[1:, :, :64]], axis=2)
        v = v[:nd] + moved
        picked = [jnp.where(core == 1, v[2 * y + 1], v[2 * y]) for y in range(NY)]
        hits_ref[n * NBLK : (n + 1) * NBLK, :] = jnp.concatenate(picked, axis=0)
    zero = jnp.zeros((NMODE, 32), F32)
    rhs_ref[...] = jnp.concatenate(
        [zero, packs[0][:, :NMODE].T, packs[1][:, :NMODE].T, zero], axis=1
    )


def lanes_of(v, k):
    return jnp.broadcast_to(v[:, k : k + 1], (8, 128))


def solve(packed, rhs):
    n = NMODE
    groups = range(n // 8)
    full = jnp.concatenate(
        [packed] + [pltpu.roll(packed, 128 - n * i, 1) for i in groups[1:]], axis=0
    )
    row = lax.broadcasted_iota(jnp.int32, (n, 128), 0)
    lane = lax.broadcasted_iota(jnp.int32, (n, 128), 1)
    full = jnp.where(lane < n, full, rhs) + jnp.where(lane == row, 0.05, 0.0)
    diag = jnp.where(lane == row, full, 0.0)
    down = lax.rsqrt(jnp.sum(diag, axis=1, keepdims=True))
    along = jnp.sum(jnp.where(lane < n, diag, 1.0 / n), axis=0, keepdims=True)
    full = full * down * lax.rsqrt(along)
    a = [full[8 * i : 8 * i + 8, :] for i in groups]
    sub = lax.broadcasted_iota(jnp.int32, (8, 128), 0)
    for q in range(8):
        c = [[lanes_of(v, 8 * j + q) for v in a] for j in groups]
        p = [[c[j][i] for j in groups] for i in groups]
        i1 = 1.0 / (p[0][0] * p[1][1] - p[0][1] * p[0][1])
        e00, e01, e11 = p[1][1] * i1, -p[0][1] * i1, p[0][0] * i1
        w00 = e00 * p[0][2] + e01 * p[1][2]
        w01 = e00 * p[0][3] + e01 * p[1][3]
        w10 = e01 * p[0][2] + e11 * p[1][2]
        w11 = e01 * p[0][3] + e11 * p[1][3]
        s00 = p[2][2] - (p[0][2] * w00 + p[1][2] * w10)
        s01 = p[2][3] - (p[0][2] * w01 + p[1][2] * w11)
        s11 = p[3][3] - (p[0][3] * w01 + p[1][3] * w11)
        i2 = 1.0 / (s00 * s11 - s01 * s01)
        y0 = e00 * a[0] + e01 * a[1]
        y1 = e01 * a[0] + e11 * a[1]
        q2 = a[2] - (p[0][2] * y0 + p[1][2] * y1)
        q3 = a[3] - (p[0][3] * y0 + p[1][3] * y1)
        n2 = (s11 * q2 - s01 * q3) * i2
        n3 = (s00 * q3 - s01 * q2) * i2
        n0 = y0 - (w00 * n2 + w01 * n3)
        n1 = y1 - (w10 * n2 + w11 * n3)
        new = [jnp.broadcast_to(v[q : q + 1, :], (8, 128)) for v in (n0, n1, n2, n3)]
        a = [
            jnp.where(
                sub == q,
                new[i],
                a[i] - ((c[0][i] * new[0] + c[1][i] * new[1]) + (c[2][i] * new[2] + c[3][i] * new[3])),
            )
            for i in groups
        ]
    return jnp.concatenate(a, axis=0)[:, n : 3 * n] * down


def edge_rows(s):
    lane = lax.broadcasted_iota(jnp.int32, s.shape, 1)
    moved = jnp.take_along_axis(s, edge_col(lane & 63), axis=1, mode="promise_in_bounds")
    moved = moved.reshape(NBLK, 2, 8, 128)
    sub = lax.broadcasted_iota(jnp.int32, (NBLK, 8, 128), 1)
    lane = lax.broadcasted_iota(jnp.int32, (NBLK, 8, 128), 2)
    moved = jnp.where(lane < 64, moved[:, 0], moved[:, 1])
    here = ((lane & 7) == sub) & ((lane & 63) < 48)
    return jnp.sum(jnp.where(here, moved, 0.0), axis=1)


def clean_kernel(
    p_ref, q_ref, r_ref, s_ref, rhs_ref, w_ref, x_ref, other_ref, synth_ref, tw_ref,
    idx_ref, hits_ref, hot_ref, more_hot_ref,
    blocks_ref, out_hbm, clean_ref, sem,
):
    p = (p_ref[...] + q_ref[...]) + (r_ref[...] + s_ref[...])
    coef = solve(p[2 * NMODE :, :], rhs_ref[...])
    ab = mm0_split(coef, jnp.concatenate([p[:NMODE, :], p[NMODE : 2 * NMODE, :]], axis=1))
    a = ab[:, :FKEEP]
    b = ab[:, FKEEP:]
    parts = []
    for c in range(SEG // WIDE):
        at = c * WIDE // CHUNK
        cos = tw_ref[at : at + 1, :FKEEP]
        sin = tw_ref[at : at + 1, FKEEP:]
        parts.append(jnp.concatenate([a * cos + b * sin, b * cos - a * sin], axis=1))
    hi, lo = split(jnp.concatenate(parts, axis=0))
    sh = synth_ref[: 2 * FKEEP, :]
    low = mm(hi, sh) + mm(lo, sh) + mm(hi, synth_ref[2 * FKEEP :, :])
    runs = []
    for n, source in enumerate((x_ref, other_ref)):
        w = w_ref[n * DETS : (n + 1) * DETS, :]
        for r in range(SEG // RUN):
            at = 2 * DETS * (r * RUN // WIDE) + DETS * n
            col = r * RUN % WIDE
            part = w * (source[:, r * RUN : (r + 1) * RUN] - low[at : at + DETS, col : col + RUN])
            if n == 0:
                clean_ref[:, r * RUN : (r + 1) * RUN] = part
            runs.append(part)
    copy = pltpu.make_async_copy(clean_ref, out_hbm, sem)
    copy.start()
    run = jnp.concatenate(runs, axis=0)
    vals = jnp.concatenate(
        split(jnp.take_along_axis(run, idx_ref[...], axis=1, mode="promise_in_bounds")), axis=1
    )
    s = mm(hot_ref[...], vals[:FIRST]) + mm(more_hot_ref[...], vals[FIRST:])
    s = s[:, :128] + s[:, 128:]
    blocks_ref[...] = s
    edges = edge_rows(s)
    tile = lax.broadcasted_iota(jnp.int32, edges.shape, 0) & (NT - 1)
    slot = (lax.broadcasted_iota(jnp.int32, edges.shape, 1) & 63) >> 3
    zero = jnp.zeros((1, 128), F32)
    left = jnp.where(tile == 0, 0.0, jnp.concatenate([zero, edges[:-1]], axis=0))
    right = jnp.where(tile == NT - 1, 0.0, jnp.concatenate([edges[1:], zero], axis=0))
    near = jnp.where(slot < RADIUS, left, right) + hits_ref[:NBLK, :]
    blocks_ref[pl.ds(14, NBLK, stride=BROWS), :] = near
    blocks_ref[pl.ds(15, NBLK, stride=BROWS), :] = hits_ref[NBLK:, :]
    copy.wait()


def beam_kernel(blocks_ref, out_ref):
    sums = [blocks_ref[b * BROWS : (b + 1) * BROWS, :] for b in range(4)]
    for b in range(4, NBLK):
        sums[b % 4] = sums[b % 4] + blocks_ref[b * BROWS : (b + 1) * BROWS, :]
    total = (sums[0] + sums[1]) + (sums[2] + sums[3])
    near = jnp.broadcast_to(total[14:15, :], (BROWS, 128))
    mine = jnp.broadcast_to(total[15:16, :], (BROWS, 128))
    i = lax.broadcasted_iota(jnp.int32, (BROWS, 128), 0)
    lane = lax.broadcasted_iota(jnp.int32, (BROWS, 128), 1)
    spot = jnp.where(i < OWN, i, 64 + i - OWN)

    def take(src, slot):
        return jnp.sum(jnp.where(lane == spot + 8 * slot, src, 0.0), axis=1, keepdims=True)

    left_hits = take(near, 6) + 1.0
    right_hits = take(near, 7) + 1.0
    hits = take(mine, 6) + 1.0
    valid = i < OWN + 2 * RADIUS
    binned = jnp.where(valid, total / hits, 0.0)
    left = [take(near, m) / left_hits for m in range(RADIUS)]
    right = [take(near, RADIUS + m) / right_hits for m in range(RADIUS)]
    taps = beam_taps()
    smooth = taps[RADIUS] * binned
    for m in range(1, RADIUS + 1):
        moved = pltpu.roll(binned, m, 1)
        for q in range(m):
            moved = jnp.where(lane == q, left[RADIUS - m + q], moved)
        smooth = smooth + taps[RADIUS - m] * moved
        moved = pltpu.roll(binned, TCOLS - m, 1)
        for q in range(m):
            moved = jnp.where(lane == TCOLS - m + q, right[q], moved)
        smooth = smooth + taps[RADIUS + m] * moved
    out = taps[0] * smooth[0:OWN, :]
    for m in range(1, 2 * RADIUS + 1):
        out = out + taps[m] * smooth[m : m + OWN, :]
    out_ref[...] = out


VMEM = pl.BlockSpec(memory_space=pltpu.VMEM)
SMEM = pl.BlockSpec(memory_space=pltpu.SMEM)
HBM = pl.BlockSpec(memory_space=pltpu.HBM)


def call(kernel, outs, specs, name, flops, *args, out_specs=None, scratch=()):
    args = [
        pltpu.with_memory_space_constraint(a, pltpu.HBM) if spec is HBM else a
        for a, spec in zip(args, specs)
    ]
    nbytes = sum(math.prod(s.shape) * 4 for s in outs) + sum(a.size * 4 for a in args)
    return pl.pallas_call(
        kernel,
        out_shape=outs,
        in_specs=specs,
        out_specs=out_specs or [VMEM] * len(outs),
        scratch_shapes=list(scratch),
        name=name,
        compiler_params=pltpu.CompilerParams(vmem_limit_bytes=40 << 20),
        cost_estimate=pl.CostEstimate(flops=flops, bytes_accessed=nbytes, transcendentals=0),
    )(*args)


def sds(shape, dtype=F32):
    return jax.ShapeDtypeStruct(shape, dtype)


def body(timestreams, templates, validity, tile_index, row_offset, col_start):
    basis, synth, tw = tables()
    core = lax.axis_index("core").reshape(1)
    small = (DETS, SEG // RUN)
    swap = [(0, 1), (1, 0)]
    mate_x = lax.ppermute(timestreams, "core", swap)
    part, x, synth, tw, line = call(
        analysis_kernel,
        [
            sds((PART + DETS, FKEEP)), sds((DETS, SEG)), sds((4 * FKEEP, WIDE), BF),
            sds((NCHUNK, 2 * FKEEP)), sds((1, NRUNS), I32),
        ],
        [HBM] * 9, "analysis", 400_000_000,
        timestreams, templates, validity.reshape(1, DETS), tile_index, row_offset, col_start,
        jnp.asarray(basis), jnp.asarray(synth), jnp.asarray(tw),
        scratch=[
            pltpu.VMEM((DETS, NMODE), F32), pltpu.VMEM((1, DETS), I32), pltpu.VMEM(small, I32),
            pltpu.VMEM(small, I32), pltpu.VMEM(small, I32),
            pltpu.VMEM((2 * CHUNK, 2 * FKEEP), BF), pltpu.SemaphoreType.DMA((9,)),
        ],
    )
    mate = lax.ppermute(part, "core", swap)
    (hot,) = call(
        first_index_kernel, [sds((NBLK * BROWS, FIRST), BF)], [SMEM, VMEM], "index1", 100_000_000, core, line
    )
    sums, hot, line = lax.optimization_barrier((part[:PART] + mate[:PART], hot, line))
    others = [lax.ppermute(sums, "y", [(k, k ^ m) for k in range(NY)]) for m in (2, 3, 1)]
    more_hot, idx, hits, rhs, w = call(
        second_index_kernel,
        [
            sds((NBLK * BROWS, 2 * NRUNS - FIRST), BF), sds((2 * NRUNS, 128), I32),
            sds((2 * NBLK, 128)),
            sds((NMODE, 128)), sds((2 * DETS, 128)),
        ],
        [SMEM] + [VMEM] * 3, "index2", 3_000_000_000,
        core, line, part, mate,
    )
    blocks, cleaned = call(
        clean_kernel,
        [sds((NBLK * BROWS, 128)), sds((DETS, SEG))],
        [VMEM] * 14, "clean", 2_000_000_000,
        sums, *others, rhs, w, x, mate_x, synth, tw, idx, hits, hot, more_hot,
        out_specs=[VMEM, HBM],
        scratch=[pltpu.VMEM((DETS, SEG), F32), pltpu.SemaphoreType.DMA],
    )
    blocks = lax.all_to_all(blocks, ("y", "z", "x"), 0, 0, tiled=True)
    (beamed,) = call(
        beam_kernel, [sds((OWN, TCOLS))], [VMEM], "beam", 1_000_000, blocks
    )
    return (cleaned, beamed)


def solution(mesh):
    fine = Mesh(mesh.devices.reshape(NY, 2, 4, 4), ("y", "core", "z", "x"))
    det, tm = ("y", "core"), ("z", "x")
    in_specs = (P(det, tm), P(det, None), P(det), P(det, tm), P(det, tm), P(det, tm))
    out_specs = (P(det, tm), P(det, tm))
    return jax.shard_map(body, mesh=fine, in_specs=in_specs, out_specs=out_specs, check_vma=False)
```

```python
import math

import jax
import jax.numpy as jnp
import numpy as np
from jax import lax
from jax.experimental import pallas as pl
from jax.experimental.pallas import tpu as pltpu
from jax.sharding import Mesh
from jax.sharding import PartitionSpec as P
import ml_dtypes

SEG = 4096
NMODE = 32
FKEEP = 128
RUN = 128
TROWS = 64
TCOLS = 128
RADIUS = 3
DETS = 32
CHUNK = 256
NCHUNK = SEG // CHUNK
WIDE = 1024
NRUNS = DETS * SEG // RUN
NT = 16
NY = 4
OWN = 8
BROWS = 16
NBLK = NY * NT
ZROWS = (TROWS // OWN + 1) * NT
BF = jnp.bfloat16
F32 = jnp.float32
I32 = jnp.int32
FIRST = 512
PART = 2 * NMODE + 8


def split_np(a):
    hi = a.astype(np.float32).astype(ml_dtypes.bfloat16)
    lo = (a - hi.astype(np.float64)).astype(np.float32).astype(ml_dtypes.bfloat16)
    return hi, lo


def tables():
    j = np.arange(CHUNK)[:, None]
    k = np.arange(FKEEP)[None, :]
    phi = 2.0 * np.pi * (j * k % SEG) / SEG
    basis = np.concatenate([np.cos(phi), np.sin(phi)], axis=1)
    c = np.arange(NCHUNK)[:, None]
    theta = 2.0 * np.pi * (c * CHUNK * k % SEG) / SEG
    twiddle = np.concatenate([np.cos(theta), np.sin(theta)], axis=1).astype(np.float32)
    scale = np.where(np.arange(FKEEP) == 0, 1.0 / SEG, 2.0 / SEG)
    phi = 2.0 * np.pi * (np.arange(WIDE)[:, None] * k % SEG) / SEG
    synth = np.concatenate([np.cos(phi), np.sin(phi)], axis=1).T
    synth = synth * np.concatenate([scale, scale])[:, None]
    return np.concatenate(split_np(basis)), np.concatenate(split_np(synth)), twiddle


def beam_taps():
    values = [math.exp(-(m * m) / 4.5) for m in range(-RADIUS, RADIUS + 1)]
    total = sum(values)
    return [v / total for v in values]


def split(a):
    hi = a.astype(BF)
    return hi, (a - hi.astype(F32)).astype(BF)


def mm(a, b):
    return jnp.dot(a, b, preferred_element_type=F32)


def mm0(a, b):
    return lax.dot_general(
        a, b, (((0,), (0,)), ((), ())), precision=lax.Precision.HIGHEST,
        preferred_element_type=F32,
    )


def mm0_split(a, b):
    ah, al = split(a)
    bh, bl = split(b)
    return lax.dot_general(
        jnp.concatenate([ah, al, ah], axis=0), jnp.concatenate([bh, bh, bl], axis=0),
        (((0,), (0,)), ((), ())), preferred_element_type=F32,
    )


def column(row, n):
    full = jnp.broadcast_to(row, (n, row.shape[1]))
    same = lax.broadcasted_iota(jnp.int32, full.shape, 0) == lax.broadcasted_iota(
        jnp.int32, full.shape, 1
    )
    return jnp.sum(jnp.where(same, full, 0.0), axis=1, keepdims=True)


def run_row(ids):
    flat = ids.astype(F32).T
    parts = [flat[c : c + 1, :] for c in range(SEG // RUN)]
    return jnp.concatenate(parts, axis=1).astype(jnp.int32)


def analysis_kernel(
    x_hbm, t_hbm, v_hbm, ti_hbm, ro_hbm, cs_hbm, basis_hbm, synth_hbm, tw_hbm,
    out_ref, x_ref, synth_ref, tw_ref, line_ref,
    t_ref, v_ref, ti_ref, ro_ref, cs_ref, basis_ref, sems,
):
    copies = [
        pltpu.make_async_copy(src, dst, sems.at[n])
        for n, (src, dst) in enumerate(
            [
                (t_hbm, t_ref), (v_hbm, v_ref), (basis_hbm, basis_ref), (x_hbm, x_ref),
                (ti_hbm, ti_ref), (ro_hbm, ro_ref), (cs_hbm, cs_ref),
                (tw_hbm, tw_ref), (synth_hbm, synth_ref),
            ]
        )
    ]
    for copy in copies:
        copy.start()
    copies[0].wait()
    copies[1].wait()
    copies[2].wait()
    copies[3].wait()
    copies[4].wait()
    copies[5].wait()
    copies[6].wait()
    copies[7].wait()
    w = column(v_ref[...].astype(F32), DETS)
    t = t_ref[...]
    wt = t * w
    eh = basis_ref[:CHUNK, :]
    el = basis_ref[CHUNK:, :]
    wide = jnp.broadcast_to(w, (DETS, CHUNK))
    x = jnp.concatenate(
        [wide * x_ref[:, c * CHUNK : (c + 1) * CHUNK] for c in range(NCHUNK)], axis=0
    )
    hi, lo = split(x)
    y = mm(hi, eh) + mm(lo, eh) + mm(hi, el)
    gram = mm0(wt, t)
    out_ref[2 * NMODE : PART, :] = jnp.concatenate(
        [gram[8 * i : 8 * i + 8, :] for i in range(NMODE // 8)], axis=1
    )
    line = ti_ref[...] * TROWS + ro_ref[...]
    line_ref[...] = run_row(line)
    out_ref[PART:, :] = jnp.concatenate(
        [t, line.astype(F32), cs_ref[...].astype(F32), jnp.broadcast_to(w, (DETS, 32))], axis=1
    )
    re = jnp.zeros((DETS, FKEEP), F32)
    im = jnp.zeros((DETS, FKEEP), F32)
    for c in range(NCHUNK):
        sl = slice(c * DETS, (c + 1) * DETS)
        yc = y[sl, :FKEEP]
        yi = y[sl, FKEEP:]
        cos = tw_ref[c : c + 1, :FKEEP]
        sin = tw_ref[c : c + 1, FKEEP:]
        re = re + (cos * yc - sin * yi)
        im = im + (sin * yc + cos * yi)
    both = mm0_split(wt, jnp.concatenate([re, im], axis=1))
    out_ref[:NMODE, :] = both[:, :FKEEP]
    out_ref[NMODE : 2 * NMODE, :] = both[:, FKEEP:]
    copies[8].wait()


def edge_col(lane):
    slot = lane >> 3
    return jnp.where(slot < 3, TCOLS - RADIUS + slot, slot - 3)


def ids_of_blocks(core):
    l = lax.broadcasted_iota(jnp.int32, (NBLK * BROWS, 128), 0)
    i = l & (BROWS - 1)
    b = l >> 4
    row = (b >> 4) * (2 * OWN) + core * OWN - RADIUS + i
    ok = (i < OWN + 2 * RADIUS) & (row >= 0) & (row < TROWS)
    return jnp.where(ok, (b & (NT - 1)) * TROWS + row, -1)


def fill_hot(ref, ids, line):
    for q in range(line.shape[1] // 128):
        sl = slice(q * 128, (q + 1) * 128)
        ref[:, sl] = jnp.where(ids == line[:, sl], 1.0, 0.0).astype(BF)


def first_index_kernel(core_ref, line_ref, hot_ref):
    fill_hot(hot_ref, ids_of_blocks(core_ref[0]), line_ref[:, :FIRST])


def shifted_tiles(z, by):
    zero = jnp.zeros((z.shape[0], 1, 128), F32)
    if by < 0:
        return jnp.concatenate([zero, z[:, :-1]], axis=1)
    return jnp.concatenate([z[:, 1:], zero], axis=1)


def second_index_kernel(
    core_ref, line_ref, mine_ref, other_ref, hot_ref, idx_ref, hits_ref, rhs_ref, w_ref
):
    core = core_ref[0]
    packs = (mine_ref[PART:, :], other_ref[PART:, :])
    lines = [pack[:, 32:64].astype(jnp.int32) for pack in packs]
    rows = (line_ref[...], run_row(lines[1]))
    line = jnp.concatenate(rows, axis=1)
    fill_hot(hot_ref, ids_of_blocks(core), line[:, FIRST:])
    zid = (((line & (TROWS - 1)) + RADIUS) >> 3) * NT + (line >> 6)
    zl = lax.broadcasted_iota(jnp.int32, (ZROWS, 2 * NRUNS), 0)
    zhot = jnp.where(zl == zid, 1.0, 0.0).astype(BF)
    lane = lax.broadcasted_iota(jnp.int32, (DETS, 128), 1)
    hparts = []
    for n, pack in enumerate(packs):
        w = jnp.broadcast_to(pack[:, 96:97], (DETS, 128))
        w_ref[n * DETS : (n + 1) * DETS, :] = w
        spot = ((lines[n] + RADIUS) & (OWN - 1)) + 48
        css = pack[:, 64:96].astype(jnp.int32)
        for c in range(SEG // RUN):
            sl = slice(n * NRUNS + c * DETS, n * NRUNS + (c + 1) * DETS)
            cs = jnp.broadcast_to(css[:, c : c + 1], (DETS, 128))
            idx_ref[sl, :] = (lane - cs) & (TCOLS - 1)
            here = jnp.broadcast_to(spot[:, c : c + 1], (DETS, 128)) == lane
            hparts.append(jnp.where(here, w, 0.0).astype(BF))
    z = mm(zhot, jnp.concatenate(hparts, axis=0)).reshape(ZROWS // NT, NT, 128)
    right = shifted_tiles(z, 1)
    right = jnp.concatenate([jnp.zeros(z.shape[:2] + (8,), F32), right[:, :, :-8]], axis=2)
    nd = TROWS // OWN
    for n, v in enumerate((shifted_tiles(z, -1) + right, z)):
        moved = jnp.concatenate([jnp.zeros((nd, NT, 64), F32), v[1:, :, :64]], axis=2)
        v = v[:nd] + moved
        picked = [jnp.where(core == 1, v[2 * y + 1], v[2 * y]) for y in range(NY)]
        hits_ref[n * NBLK : (n + 1) * NBLK, :] = jnp.concatenate(picked, axis=0)
    zero = jnp.zeros((NMODE, 32), F32)
    rhs_ref[...] = jnp.concatenate(
        [zero, packs[0][:, :NMODE].T, packs[1][:, :NMODE].T, zero], axis=1
    )


def lanes_of(v, k):
    return jnp.broadcast_to(v[:, k : k + 1], (8, 128))


def solve(packed, rhs):
    n = NMODE
    groups = range(n // 8)
    full = jnp.concatenate(
        [packed] + [pltpu.roll(packed, 128 - n * i, 1) for i in groups[1:]], axis=0
    )
    row = lax.broadcasted_iota(jnp.int32, (n, 128), 0)
    lane = lax.broadcasted_iota(jnp.int32, (n, 128), 1)
    full = jnp.where(lane < n, full, rhs) + jnp.where(lane == row, 0.05, 0.0)
    diag = jnp.where(lane == row, full, 0.0)
    down = lax.rsqrt(jnp.sum(diag, axis=1, keepdims=True))
    along = jnp.sum(jnp.where(lane < n, diag, 1.0 / n), axis=0, keepdims=True)
    full = full * down * lax.rsqrt(along)
    a = [full[8 * i : 8 * i + 8, :] for i in groups]
    sub = lax.broadcasted_iota(jnp.int32, (8, 128), 0)
    for q in range(8):
        c = [[lanes_of(v, 8 * j + q) for v in a] for j in groups]
        p = [[c[j][i] for j in groups] for i in groups]
        i1 = 1.0 / (p[0][0] * p[1][1] - p[0][1] * p[0][1])
        e00, e01, e11 = p[1][1] * i1, -p[0][1] * i1, p[0][0] * i1
        w00 = e00 * p[0][2] + e01 * p[1][2]
        w01 = e00 * p[0][3] + e01 * p[1][3]
        w10 = e01 * p[0][2] + e11 * p[1][2]
        w11 = e01 * p[0][3] + e11 * p[1][3]
        s00 = p[2][2] - (p[0][2] * w00 + p[1][2] * w10)
        s01 = p[2][3] - (p[0][2] * w01 + p[1][2] * w11)
        s11 = p[3][3] - (p[0][3] * w01 + p[1][3] * w11)
        i2 = 1.0 / (s00 * s11 - s01 * s01)
        y0 = e00 * a[0] + e01 * a[1]
        y1 = e01 * a[0] + e11 * a[1]
        q2 = a[2] - (p[0][2] * y0 + p[1][2] * y1)
        q3 = a[3] - (p[0][3] * y0 + p[1][3] * y1)
        n2 = (s11 * q2 - s01 * q3) * i2
        n3 = (s00 * q3 - s01 * q2) * i2
        n0 = y0 - (w00 * n2 + w01 * n3)
        n1 = y1 - (w10 * n2 + w11 * n3)
        new = [jnp.broadcast_to(v[q : q + 1, :], (8, 128)) for v in (n0, n1, n2, n3)]
        a = [
            jnp.where(
                sub == q,
                new[i],
                a[i] - ((c[0][i] * new[0] + c[1][i] * new[1]) + (c[2][i] * new[2] + c[3][i] * new[3])),
            )
            for i in groups
        ]
    return jnp.concatenate(a, axis=0)[:, n : 3 * n] * down


def edge_rows(s):
    lane = lax.broadcasted_iota(jnp.int32, s.shape, 1)
    moved = jnp.take_along_axis(s, edge_col(lane & 63), axis=1, mode="promise_in_bounds")
    moved = moved.reshape(NBLK, 2, 8, 128)
    sub = lax.broadcasted_iota(jnp.int32, (NBLK, 8, 128), 1)
    lane = lax.broadcasted_iota(jnp.int32, (NBLK, 8, 128), 2)
    moved = jnp.where(lane < 64, moved[:, 0], moved[:, 1])
    here = ((lane & 7) == sub) & ((lane & 63) < 48)
    return jnp.sum(jnp.where(here, moved, 0.0), axis=1)


def clean_kernel(
    p_ref, q_ref, r_ref, s_ref, rhs_ref, w_ref, x_ref, other_ref, synth_ref, tw_ref,
    idx_ref, hits_ref, hot_ref, more_hot_ref,
    blocks_ref, out_hbm, clean_ref, sem,
):
    p = (p_ref[...] + q_ref[...]) + (r_ref[...] + s_ref[...])
    coef = solve(p[2 * NMODE :, :], rhs_ref[...])
    ab = mm0_split(coef, jnp.concatenate([p[:NMODE, :], p[NMODE : 2 * NMODE, :]], axis=1))
    a = ab[:, :FKEEP]
    b = ab[:, FKEEP:]
    parts = []
    for c in range(SEG // WIDE):
        at = c * WIDE // CHUNK
        cos = tw_ref[at : at + 1, :FKEEP]
        sin = tw_ref[at : at + 1, FKEEP:]
        parts.append(jnp.concatenate([a * cos + b * sin, b * cos - a * sin], axis=1))
    hi, lo = split(jnp.concatenate(parts, axis=0))
    sh = synth_ref[: 2 * FKEEP, :]
    low = mm(hi, sh) + mm(lo, sh) + mm(hi, synth_ref[2 * FKEEP :, :])
    runs = []
    for n, source in enumerate((x_ref, other_ref)):
        w = w_ref[n * DETS : (n + 1) * DETS, :]
        for r in range(SEG // RUN):
            at = 2 * DETS * (r * RUN // WIDE) + DETS * n
            col = r * RUN % WIDE
            part = w * (source[:, r * RUN : (r + 1) * RUN] - low[at : at + DETS, col : col + RUN])
            if n == 0:
                clean_ref[:, r * RUN : (r + 1) * RUN] = part
            runs.append(part)
    copy = pltpu.make_async_copy(clean_ref, out_hbm, sem)
    copy.start()
    run = jnp.concatenate(runs, axis=0)
    vals = jnp.concatenate(
        split(jnp.take_along_axis(run, idx_ref[...], axis=1, mode="promise_in_bounds")), axis=1
    )
    s = mm(hot_ref[...], vals[:FIRST]) + mm(more_hot_ref[...], vals[FIRST:])
    s = s[:, :128] + s[:, 128:]
    blocks_ref[...] = s
    edges = edge_rows(s)
    tile = lax.broadcasted_iota(jnp.int32, edges.shape, 0) & (NT - 1)
    slot = (lax.broadcasted_iota(jnp.int32, edges.shape, 1) & 63) >> 3
    zero = jnp.zeros((1, 128), F32)
    left = jnp.where(tile == 0, 0.0, jnp.concatenate([zero, edges[:-1]], axis=0))
    right = jnp.where(tile == NT - 1, 0.0, jnp.concatenate([edges[1:], zero], axis=0))
    near = jnp.where(slot < RADIUS, left, right) + hits_ref[:NBLK, :]
    blocks_ref[pl.ds(14, NBLK, stride=BROWS), :] = near
    blocks_ref[pl.ds(15, NBLK, stride=BROWS), :] = hits_ref[NBLK:, :]
    copy.wait()


def beam_kernel(blocks_ref, out_ref):
    sums = [blocks_ref[b * BROWS : (b + 1) * BROWS, :] for b in range(4)]
    for b in range(4, NBLK):
        sums[b % 4] = sums[b % 4] + blocks_ref[b * BROWS : (b + 1) * BROWS, :]
    total = (sums[0] + sums[1]) + (sums[2] + sums[3])
    near = jnp.broadcast_to(total[14:15, :], (BROWS, 128))
    mine = jnp.broadcast_to(total[15:16, :], (BROWS, 128))
    i = lax.broadcasted_iota(jnp.int32, (BROWS, 128), 0)
    lane = lax.broadcasted_iota(jnp.int32, (BROWS, 128), 1)
    spot = jnp.where(i < OWN, i, 64 + i - OWN)

    def take(src, slot):
        return jnp.sum(jnp.where(lane == spot + 8 * slot, src, 0.0), axis=1, keepdims=True)

    left_hits = take(near, 6) + 1.0
    right_hits = take(near, 7) + 1.0
    hits = take(mine, 6) + 1.0
    valid = i < OWN + 2 * RADIUS
    binned = jnp.where(valid, total / hits, 0.0)
    left = [take(near, m) / left_hits for m in range(RADIUS)]
    right = [take(near, RADIUS + m) / right_hits for m in range(RADIUS)]
    taps = beam_taps()
    smooth = taps[RADIUS] * binned
    for m in range(1, RADIUS + 1):
        moved = pltpu.roll(binned, m, 1)
        for q in range(m):
            moved = jnp.where(lane == q, left[RADIUS - m + q], moved)
        smooth = smooth + taps[RADIUS - m] * moved
        moved = pltpu.roll(binned, TCOLS - m, 1)
        for q in range(m):
            moved = jnp.where(lane == TCOLS - m + q, right[q], moved)
        smooth = smooth + taps[RADIUS + m] * moved
    out = taps[0] * smooth[0:OWN, :]
    for m in range(1, 2 * RADIUS + 1):
        out = out + taps[m] * smooth[m : m + OWN, :]
    out_ref[...] = out


VMEM = pl.BlockSpec(memory_space=pltpu.VMEM)
SMEM = pl.BlockSpec(memory_space=pltpu.SMEM)
HBM = pl.BlockSpec(memory_space=pltpu.HBM)


def call(kernel, outs, specs, name, flops, *args, out_specs=None, scratch=()):
    args = [
        pltpu.with_memory_space_constraint(a, pltpu.HBM) if spec is HBM else a
        for a, spec in zip(args, specs)
    ]
    nbytes = sum(math.prod(s.shape) * 4 for s in outs) + sum(a.size * 4 for a in args)
    return pl.pallas_call(
        kernel,
        out_shape=outs,
        in_specs=specs,
        out_specs=out_specs or [VMEM] * len(outs),
        scratch_shapes=list(scratch),
        name=name,
        compiler_params=pltpu.CompilerParams(vmem_limit_bytes=40 << 20),
        cost_estimate=pl.CostEstimate(flops=flops, bytes_accessed=nbytes, transcendentals=0),
    )(*args)


def sds(shape, dtype=F32):
    return jax.ShapeDtypeStruct(shape, dtype)


def body(timestreams, templates, validity, tile_index, row_offset, col_start):
    basis, synth, tw = tables()
    core = lax.axis_index("core").reshape(1)
    small = (DETS, SEG // RUN)
    swap = [(0, 1), (1, 0)]
    mate_x = lax.ppermute(timestreams, "core", swap)
    part, x, synth, tw, line = call(
        analysis_kernel,
        [
            sds((PART + DETS, FKEEP)), sds((DETS, SEG)), sds((4 * FKEEP, WIDE), BF),
            sds((NCHUNK, 2 * FKEEP)), sds((1, NRUNS), I32),
        ],
        [HBM] * 9, "analysis", 400_000_000,
        timestreams, templates, validity.reshape(1, DETS), tile_index, row_offset, col_start,
        jnp.asarray(basis), jnp.asarray(synth), jnp.asarray(tw),
        scratch=[
            pltpu.VMEM((DETS, NMODE), F32), pltpu.VMEM((1, DETS), I32), pltpu.VMEM(small, I32),
            pltpu.VMEM(small, I32), pltpu.VMEM(small, I32),
            pltpu.VMEM((2 * CHUNK, 2 * FKEEP), BF), pltpu.SemaphoreType.DMA((9,)),
        ],
    )
    mate = lax.ppermute(part, "core", swap)
    (hot,) = call(
        first_index_kernel, [sds((NBLK * BROWS, FIRST), BF)], [SMEM, VMEM], "index1", 100_000_000, core, line
    )
    sums, hot, line = lax.optimization_barrier((part[:PART] + mate[:PART], hot, line))
    others = [lax.ppermute(sums, "y", [(k, (k + m) % NY) for k in range(NY)]) for m in (1, 3, 2)]
    more_hot, idx, hits, rhs, w = call(
        second_index_kernel,
        [
            sds((NBLK * BROWS, 2 * NRUNS - FIRST), BF), sds((2 * NRUNS, 128), I32),
            sds((2 * NBLK, 128)),
            sds((NMODE, 128)), sds((2 * DETS, 128)),
        ],
        [SMEM] + [VMEM] * 3, "index2", 3_000_000_000,
        core, line, part, mate,
    )
    blocks, cleaned = call(
        clean_kernel,
        [sds((NBLK * BROWS, 128)), sds((DETS, SEG))],
        [VMEM] * 14, "clean", 2_000_000_000,
        sums, *others, rhs, w, x, mate_x, synth, tw, idx, hits, hot, more_hot,
        out_specs=[VMEM, HBM],
        scratch=[pltpu.VMEM((DETS, SEG), F32), pltpu.SemaphoreType.DMA],
    )
    blocks = lax.all_to_all(blocks, ("y", "z", "x"), 0, 0, tiled=True)
    (beamed,) = call(
        beam_kernel, [sds((OWN, TCOLS))], [VMEM], "beam", 1_000_000, blocks
    )
    return (cleaned, beamed)


def solution(mesh):
    fine = Mesh(mesh.devices.reshape(NY, 2, 4, 4), ("y", "core", "z", "x"))
    det, tm = ("y", "core"), ("z", "x")
    in_specs = (P(det, tm), P(det, None), P(det), P(det, tm), P(det, tm), P(det, tm))
    out_specs = (P(det, tm), P(det, tm))
    return jax.shard_map(body, mesh=fine, in_specs=in_specs, out_specs=out_specs, check_vma=False)
```

```python
import math

import jax
import jax.numpy as jnp
import numpy as np
from jax import lax
from jax.experimental import pallas as pl
from jax.experimental.pallas import tpu as pltpu
from jax.sharding import Mesh
from jax.sharding import PartitionSpec as P
import ml_dtypes

SEG = 4096
NMODE = 32
FKEEP = 128
RUN = 128
TROWS = 64
TCOLS = 128
RADIUS = 3
DETS = 32
CHUNK = 256
NCHUNK = SEG // CHUNK
WIDE = 1024
NRUNS = DETS * SEG // RUN
NT = 16
NY = 4
OWN = 8
BROWS = 16
NBLK = NY * NT
ZROWS = (TROWS // OWN + 1) * NT
BF = jnp.bfloat16
F32 = jnp.float32
I32 = jnp.int32
FIRST = 512
PART = 2 * NMODE + 8


def split_np(a):
    hi = a.astype(np.float32).astype(ml_dtypes.bfloat16)
    lo = (a - hi.astype(np.float64)).astype(np.float32).astype(ml_dtypes.bfloat16)
    return hi, lo


def tables():
    j = np.arange(CHUNK)[:, None]
    k = np.arange(FKEEP)[None, :]
    phi = 2.0 * np.pi * (j * k % SEG) / SEG
    basis = np.concatenate([np.cos(phi), np.sin(phi)], axis=1)
    c = np.arange(NCHUNK)[:, None]
    theta = 2.0 * np.pi * (c * CHUNK * k % SEG) / SEG
    twiddle = np.concatenate([np.cos(theta), np.sin(theta)], axis=1).astype(np.float32)
    scale = np.where(np.arange(FKEEP) == 0, 1.0 / SEG, 2.0 / SEG)
    phi = 2.0 * np.pi * (np.arange(WIDE)[:, None] * k % SEG) / SEG
    synth = np.concatenate([np.cos(phi), np.sin(phi)], axis=1).T
    synth = synth * np.concatenate([scale, scale])[:, None]
    return np.concatenate(split_np(basis)), np.concatenate(split_np(synth)), twiddle


def beam_taps():
    values = [math.exp(-(m * m) / 4.5) for m in range(-RADIUS, RADIUS + 1)]
    total = sum(values)
    return [v / total for v in values]


def split(a):
    hi = a.astype(BF)
    return hi, (a - hi.astype(F32)).astype(BF)


def mm(a, b):
    return jnp.dot(a, b, preferred_element_type=F32)


def mm0(a, b):
    return lax.dot_general(
        a, b, (((0,), (0,)), ((), ())), precision=lax.Precision.HIGHEST,
        preferred_element_type=F32,
    )


def mm0_split(a, b):
    ah, al = split(a)
    bh, bl = split(b)
    return lax.dot_general(
        jnp.concatenate([ah, al, ah], axis=0), jnp.concatenate([bh, bh, bl], axis=0),
        (((0,), (0,)), ((), ())), preferred_element_type=F32,
    )


def column(row, n):
    full = jnp.broadcast_to(row, (n, row.shape[1]))
    same = lax.broadcasted_iota(jnp.int32, full.shape, 0) == lax.broadcasted_iota(
        jnp.int32, full.shape, 1
    )
    return jnp.sum(jnp.where(same, full, 0.0), axis=1, keepdims=True)


def run_row(ids):
    flat = ids.astype(F32).T
    parts = [flat[c : c + 1, :] for c in range(SEG // RUN)]
    return jnp.concatenate(parts, axis=1).astype(jnp.int32)


def analysis_kernel(
    x_hbm, t_hbm, v_hbm, ti_hbm, ro_hbm, cs_hbm, basis_hbm, synth_hbm, tw_hbm,
    out_ref, x_ref, synth_ref, tw_ref, line_ref,
    t_ref, v_ref, ti_ref, ro_ref, cs_ref, basis_ref, sems,
):
    copies = [
        pltpu.make_async_copy(src, dst, sems.at[n])
        for n, (src, dst) in enumerate(
            [
                (t_hbm, t_ref), (v_hbm, v_ref), (basis_hbm, basis_ref), (x_hbm, x_ref),
                (ti_hbm, ti_ref), (ro_hbm, ro_ref), (cs_hbm, cs_ref),
                (tw_hbm, tw_ref), (synth_hbm, synth_ref),
            ]
        )
    ]
    for copy in copies:
        copy.start()
    copies[0].wait()
    copies[1].wait()
    copies[2].wait()
    copies[3].wait()
    copies[4].wait()
    copies[5].wait()
    copies[6].wait()
    copies[7].wait()
    w = column(v_ref[...].astype(F32), DETS)
    t = t_ref[...]
    wt = t * w
    eh = basis_ref[:CHUNK, :]
    el = basis_ref[CHUNK:, :]
    wide = jnp.broadcast_to(w, (DETS, CHUNK))
    x = jnp.concatenate(
        [wide * x_ref[:, c * CHUNK : (c + 1) * CHUNK] for c in range(NCHUNK)], axis=0
    )
    hi, lo = split(x)
    y = mm(hi, eh) + mm(lo, eh) + mm(hi, el)
    gram = mm0(wt, t)
    out_ref[2 * NMODE : PART, :] = jnp.concatenate(
        [gram[8 * i : 8 * i + 8, :] for i in range(NMODE // 8)], axis=1
    )
    line = ti_ref[...] * TROWS + ro_ref[...]
    line_ref[...] = run_row(line)
    out_ref[PART:, :] = jnp.concatenate(
        [t, line.astype(F32), cs_ref[...].astype(F32), jnp.broadcast_to(w, (DETS, 32))], axis=1
    )
    re = jnp.zeros((DETS, FKEEP), F32)
    im = jnp.zeros((DETS, FKEEP), F32)
    for c in range(NCHUNK):
        sl = slice(c * DETS, (c + 1) * DETS)
        yc = y[sl, :FKEEP]
        yi = y[sl, FKEEP:]
        cos = tw_ref[c : c + 1, :FKEEP]
        sin = tw_ref[c : c + 1, FKEEP:]
        re = re + (cos * yc - sin * yi)
        im = im + (sin * yc + cos * yi)
    both = mm0_split(wt, jnp.concatenate([re, im], axis=1))
    out_ref[:NMODE, :] = both[:, :FKEEP]
    out_ref[NMODE : 2 * NMODE, :] = both[:, FKEEP:]
    copies[8].wait()


def edge_col(lane):
    slot = lane >> 3
    return jnp.where(slot < 3, TCOLS - RADIUS + slot, slot - 3)


def ids_of_blocks(core):
    l = lax.broadcasted_iota(jnp.int32, (NBLK * BROWS, 128), 0)
    i = l & (BROWS - 1)
    b = l >> 4
    row = (b & (NY - 1)) * (2 * OWN) + core * OWN - RADIUS + i
    ok = (i < OWN + 2 * RADIUS) & (row >= 0) & (row < TROWS)
    return jnp.where(ok, (b >> 2) * TROWS + row, -1)


def fill_hot(ref, ids, line):
    for q in range(line.shape[1] // 128):
        sl = slice(q * 128, (q + 1) * 128)
        ref[:, sl] = jnp.where(ids == line[:, sl], 1.0, 0.0).astype(BF)


def first_index_kernel(core_ref, line_ref, hot_ref):
    fill_hot(hot_ref, ids_of_blocks(core_ref[0]), line_ref[:, :FIRST])


def shifted_tiles(z, by):
    zero = jnp.zeros((z.shape[0], 1, 128), F32)
    if by < 0:
        return jnp.concatenate([zero, z[:, :-1]], axis=1)
    return jnp.concatenate([z[:, 1:], zero], axis=1)


def second_index_kernel(
    core_ref, line_ref, mine_ref, other_ref, hot_ref, idx_ref, hits_ref, rhs_ref, w_ref
):
    core = core_ref[0]
    packs = (mine_ref[PART:, :], other_ref[PART:, :])
    lines = [pack[:, 32:64].astype(jnp.int32) for pack in packs]
    rows = (line_ref[...], run_row(lines[1]))
    line = jnp.concatenate(rows, axis=1)
    fill_hot(hot_ref, ids_of_blocks(core), line[:, FIRST:])
    zid = (((line & (TROWS - 1)) + RADIUS) >> 3) * NT + (line >> 6)
    zl = lax.broadcasted_iota(jnp.int32, (ZROWS, 2 * NRUNS), 0)
    zhot = jnp.where(zl == zid, 1.0, 0.0).astype(BF)
    lane = lax.broadcasted_iota(jnp.int32, (DETS, 128), 1)
    hparts = []
    for n, pack in enumerate(packs):
        w = jnp.broadcast_to(pack[:, 96:97], (DETS, 128))
        w_ref[n * DETS : (n + 1) * DETS, :] = w
        spot = ((lines[n] + RADIUS) & (OWN - 1)) + 48
        css = pack[:, 64:96].astype(jnp.int32)
        for c in range(SEG // RUN):
            sl = slice(n * NRUNS + c * DETS, n * NRUNS + (c + 1) * DETS)
            cs = jnp.broadcast_to(css[:, c : c + 1], (DETS, 128))
            idx_ref[sl, :] = (lane - cs) & (TCOLS - 1)
            here = jnp.broadcast_to(spot[:, c : c + 1], (DETS, 128)) == lane
            hparts.append(jnp.where(here, w, 0.0).astype(BF))
    z = mm(zhot, jnp.concatenate(hparts, axis=0)).reshape(ZROWS // NT, NT, 128)
    right = shifted_tiles(z, 1)
    right = jnp.concatenate([jnp.zeros(z.shape[:2] + (8,), F32), right[:, :, :-8]], axis=2)
    nd = TROWS // OWN
    for n, v in enumerate((shifted_tiles(z, -1) + right, z)):
        moved = jnp.concatenate([jnp.zeros((nd, NT, 64), F32), v[1:, :, :64]], axis=2)
        v = v[:nd] + moved
        for y in range(NY):
            hits_ref[pl.ds(n * NBLK + y, NT, stride=NY), :] = jnp.where(
                core == 1, v[2 * y + 1], v[2 * y]
            )
    zero = jnp.zeros((NMODE, 32), F32)
    rhs_ref[...] = jnp.concatenate(
        [zero, packs[0][:, :NMODE].T, packs[1][:, :NMODE].T, zero], axis=1
    )


def lanes_of(v, k):
    return jnp.broadcast_to(v[:, k : k + 1], (8, 128))


def solve(packed, rhs):
    n = NMODE
    groups = range(n // 8)
    full = jnp.concatenate(
        [packed] + [pltpu.roll(packed, 128 - n * i, 1) for i in groups[1:]], axis=0
    )
    row = lax.broadcasted_iota(jnp.int32, (n, 128), 0)
    lane = lax.broadcasted_iota(jnp.int32, (n, 128), 1)
    full = jnp.where(lane < n, full, rhs) + jnp.where(lane == row, 0.05, 0.0)
    diag = jnp.where(lane == row, full, 0.0)
    down = lax.rsqrt(jnp.sum(diag, axis=1, keepdims=True))
    along = jnp.sum(jnp.where(lane < n, diag, 1.0 / n), axis=0, keepdims=True)
    full = full * down * lax.rsqrt(along)
    a = [full[8 * i : 8 * i + 8, :] for i in groups]
    sub = lax.broadcasted_iota(jnp.int32, (8, 128), 0)
    for q in range(8):
        c = [[lanes_of(v, 8 * j + q) for v in a] for j in groups]
        p = [[c[j][i] for j in groups] for i in groups]
        i1 = 1.0 / (p[0][0] * p[1][1] - p[0][1] * p[0][1])
        e00, e01, e11 = p[1][1] * i1, -p[0][1] * i1, p[0][0] * i1
        w00 = e00 * p[0][2] + e01 * p[1][2]
        w01 = e00 * p[0][3] + e01 * p[1][3]
        w10 = e01 * p[0][2] + e11 * p[1][2]
        w11 = e01 * p[0][3] + e11 * p[1][3]
        s00 = p[2][2] - (p[0][2] * w00 + p[1][2] * w10)
        s01 = p[2][3] - (p[0][2] * w01 + p[1][2] * w11)
        s11 = p[3][3] - (p[0][3] * w01 + p[1][3] * w11)
        i2 = 1.0 / (s00 * s11 - s01 * s01)
        y0 = e00 * a[0] + e01 * a[1]
        y1 = e01 * a[0] + e11 * a[1]
        q2 = a[2] - (p[0][2] * y0 + p[1][2] * y1)
        q3 = a[3] - (p[0][3] * y0 + p[1][3] * y1)
        n2 = (s11 * q2 - s01 * q3) * i2
        n3 = (s00 * q3 - s01 * q2) * i2
        n0 = y0 - (w00 * n2 + w01 * n3)
        n1 = y1 - (w10 * n2 + w11 * n3)
        new = [jnp.broadcast_to(v[q : q + 1, :], (8, 128)) for v in (n0, n1, n2, n3)]
        a = [
            jnp.where(
                sub == q,
                new[i],
                a[i] - ((c[0][i] * new[0] + c[1][i] * new[1]) + (c[2][i] * new[2] + c[3][i] * new[3])),
            )
            for i in groups
        ]
    return jnp.concatenate(a, axis=0)[:, n : 3 * n] * down


def edge_rows(s):
    lane = lax.broadcasted_iota(jnp.int32, s.shape, 1)
    moved = jnp.take_along_axis(s, edge_col(lane & 63), axis=1, mode="promise_in_bounds")
    moved = moved.reshape(NBLK, 2, 8, 128)
    sub = lax.broadcasted_iota(jnp.int32, (NBLK, 8, 128), 1)
    lane = lax.broadcasted_iota(jnp.int32, (NBLK, 8, 128), 2)
    moved = jnp.where(lane < 64, moved[:, 0], moved[:, 1])
    here = ((lane & 7) == sub) & ((lane & 63) < 48)
    return jnp.sum(jnp.where(here, moved, 0.0), axis=1)


def clean_kernel(
    p_ref, q_ref, r_ref, s_ref, rhs_ref, w_ref, x_ref, other_ref, synth_ref, tw_ref,
    idx_ref, hits_ref, hot_ref, more_hot_ref,
    blocks_ref, out_hbm, clean_ref, sem,
):
    p = (p_ref[...] + q_ref[...]) + (r_ref[...] + s_ref[...])
    coef = solve(p[2 * NMODE :, :], rhs_ref[...])
    ab = mm0_split(coef, jnp.concatenate([p[:NMODE, :], p[NMODE : 2 * NMODE, :]], axis=1))
    a = ab[:, :FKEEP]
    b = ab[:, FKEEP:]
    parts = []
    for c in range(SEG // WIDE):
        at = c * WIDE // CHUNK
        cos = tw_ref[at : at + 1, :FKEEP]
        sin = tw_ref[at : at + 1, FKEEP:]
        parts.append(jnp.concatenate([a * cos + b * sin, b * cos - a * sin], axis=1))
    hi, lo = split(jnp.concatenate(parts, axis=0))
    sh = synth_ref[: 2 * FKEEP, :]
    low = mm(hi, sh) + mm(lo, sh) + mm(hi, synth_ref[2 * FKEEP :, :])
    runs = []
    for n, source in enumerate((x_ref, other_ref)):
        w = w_ref[n * DETS : (n + 1) * DETS, :]
        for r in range(SEG // RUN):
            at = 2 * DETS * (r * RUN // WIDE) + DETS * n
            col = r * RUN % WIDE
            part = w * (source[:, r * RUN : (r + 1) * RUN] - low[at : at + DETS, col : col + RUN])
            if n == 0:
                clean_ref[:, r * RUN : (r + 1) * RUN] = part
            runs.append(part)
    copy = pltpu.make_async_copy(clean_ref, out_hbm, sem)
    copy.start()
    run = jnp.concatenate(runs, axis=0)
    vals = jnp.concatenate(
        split(jnp.take_along_axis(run, idx_ref[...], axis=1, mode="promise_in_bounds")), axis=1
    )
    s = mm(hot_ref[...], vals[:FIRST]) + mm(more_hot_ref[...], vals[FIRST:])
    s = s[:, :128] + s[:, 128:]
    blocks_ref[...] = s
    edges = edge_rows(s)
    tile = lax.broadcasted_iota(jnp.int32, edges.shape, 0) >> 2
    slot = (lax.broadcasted_iota(jnp.int32, edges.shape, 1) & 63) >> 3
    zero = jnp.zeros((NY, 128), F32)
    left = jnp.where(tile == 0, 0.0, jnp.concatenate([zero, edges[:-NY]], axis=0))
    right = jnp.where(tile == NT - 1, 0.0, jnp.concatenate([edges[NY:], zero], axis=0))
    near = jnp.where(slot < RADIUS, left, right) + hits_ref[:NBLK, :]
    blocks_ref[pl.ds(14, NBLK, stride=BROWS), :] = near
    blocks_ref[pl.ds(15, NBLK, stride=BROWS), :] = hits_ref[NBLK:, :]
    copy.wait()


def beam_kernel(blocks_ref, out_ref):
    sums = [blocks_ref[b * BROWS : (b + 1) * BROWS, :] for b in range(4)]
    for b in range(4, NBLK):
        sums[b % 4] = sums[b % 4] + blocks_ref[b * BROWS : (b + 1) * BROWS, :]
    total = (sums[0] + sums[1]) + (sums[2] + sums[3])
    near = jnp.broadcast_to(total[14:15, :], (BROWS, 128))
    mine = jnp.broadcast_to(total[15:16, :], (BROWS, 128))
    i = lax.broadcasted_iota(jnp.int32, (BROWS, 128), 0)
    lane = lax.broadcasted_iota(jnp.int32, (BROWS, 128), 1)
    spot = jnp.where(i < OWN, i, 64 + i - OWN)

    def take(src, slot):
        return jnp.sum(jnp.where(lane == spot + 8 * slot, src, 0.0), axis=1, keepdims=True)

    left_hits = take(near, 6) + 1.0
    right_hits = take(near, 7) + 1.0
    hits = take(mine, 6) + 1.0
    valid = i < OWN + 2 * RADIUS
    binned = jnp.where(valid, total / hits, 0.0)
    left = [take(near, m) / left_hits for m in range(RADIUS)]
    right = [take(near, RADIUS + m) / right_hits for m in range(RADIUS)]
    taps = beam_taps()
    smooth = taps[RADIUS] * binned
    for m in range(1, RADIUS + 1):
        moved = pltpu.roll(binned, m, 1)
        for q in range(m):
            moved = jnp.where(lane == q, left[RADIUS - m + q], moved)
        smooth = smooth + taps[RADIUS - m] * moved
        moved = pltpu.roll(binned, TCOLS - m, 1)
        for q in range(m):
            moved = jnp.where(lane == TCOLS - m + q, right[q], moved)
        smooth = smooth + taps[RADIUS + m] * moved
    out = taps[0] * smooth[0:OWN, :]
    for m in range(1, 2 * RADIUS + 1):
        out = out + taps[m] * smooth[m : m + OWN, :]
    out_ref[...] = out


VMEM = pl.BlockSpec(memory_space=pltpu.VMEM)
SMEM = pl.BlockSpec(memory_space=pltpu.SMEM)
HBM = pl.BlockSpec(memory_space=pltpu.HBM)


def call(kernel, outs, specs, name, flops, *args, out_specs=None, scratch=()):
    args = [
        pltpu.with_memory_space_constraint(a, pltpu.HBM) if spec is HBM else a
        for a, spec in zip(args, specs)
    ]
    nbytes = sum(math.prod(s.shape) * 4 for s in outs) + sum(a.size * 4 for a in args)
    return pl.pallas_call(
        kernel,
        out_shape=outs,
        in_specs=specs,
        out_specs=out_specs or [VMEM] * len(outs),
        scratch_shapes=list(scratch),
        name=name,
        compiler_params=pltpu.CompilerParams(vmem_limit_bytes=40 << 20),
        cost_estimate=pl.CostEstimate(flops=flops, bytes_accessed=nbytes, transcendentals=0),
    )(*args)


def sds(shape, dtype=F32):
    return jax.ShapeDtypeStruct(shape, dtype)


def body(timestreams, templates, validity, tile_index, row_offset, col_start):
    basis, synth, tw = tables()
    core = lax.axis_index("core").reshape(1)
    small = (DETS, SEG // RUN)
    swap = [(0, 1), (1, 0)]
    mate_x = lax.ppermute(timestreams, "core", swap)
    part, x, synth, tw, line = call(
        analysis_kernel,
        [
            sds((PART + DETS, FKEEP)), sds((DETS, SEG)), sds((4 * FKEEP, WIDE), BF),
            sds((NCHUNK, 2 * FKEEP)), sds((1, NRUNS), I32),
        ],
        [HBM] * 9, "analysis", 400_000_000,
        timestreams, templates, validity.reshape(1, DETS), tile_index, row_offset, col_start,
        jnp.asarray(basis), jnp.asarray(synth), jnp.asarray(tw),
        scratch=[
            pltpu.VMEM((DETS, NMODE), F32), pltpu.VMEM((1, DETS), I32), pltpu.VMEM(small, I32),
            pltpu.VMEM(small, I32), pltpu.VMEM(small, I32),
            pltpu.VMEM((2 * CHUNK, 2 * FKEEP), BF), pltpu.SemaphoreType.DMA((9,)),
        ],
    )
    mate = lax.ppermute(part, "core", swap)
    (hot,) = call(
        first_index_kernel, [sds((NBLK * BROWS, FIRST), BF)], [SMEM, VMEM], "index1", 100_000_000, core, line
    )
    sums, hot, line = lax.optimization_barrier((part[:PART] + mate[:PART], hot, line))
    others = [lax.ppermute(sums, "y", [(k, (k + m) % NY) for k in range(NY)]) for m in (1, 3, 2)]
    more_hot, idx, hits, rhs, w = call(
        second_index_kernel,
        [
            sds((NBLK * BROWS, 2 * NRUNS - FIRST), BF), sds((2 * NRUNS, 128), I32),
            sds((2 * NBLK, 128)),
            sds((NMODE, 128)), sds((2 * DETS, 128)),
        ],
        [SMEM] + [VMEM] * 3, "index2", 3_000_000_000,
        core, line, part, mate,
    )
    blocks, cleaned = call(
        clean_kernel,
        [sds((NBLK * BROWS, 128)), sds((DETS, SEG))],
        [VMEM] * 14, "clean", 2_000_000_000,
        sums, *others, rhs, w, x, mate_x, synth, tw, idx, hits, hot, more_hot,
        out_specs=[VMEM, HBM],
        scratch=[pltpu.VMEM((DETS, SEG), F32), pltpu.SemaphoreType.DMA],
    )
    blocks = lax.all_to_all(blocks, ("z", "x", "y"), 0, 0, tiled=True)
    (beamed,) = call(
        beam_kernel, [sds((OWN, TCOLS))], [VMEM], "beam", 1_000_000, blocks
    )
    return (cleaned, beamed)


def solution(mesh):
    fine = Mesh(mesh.devices.reshape(NY, 2, 4, 4), ("y", "core", "z", "x"))
    det, tm = ("y", "core"), ("z", "x")
    in_specs = (P(det, tm), P(det, None), P(det), P(det, tm), P(det, tm), P(det, tm))
    out_specs = (P(det, tm), P(det, tm))
    return jax.shard_map(body, mesh=fine, in_specs=in_specs, out_specs=out_specs, check_vma=False)
```

```python
import math

import jax
import jax.numpy as jnp
import numpy as np
from jax import lax
from jax.experimental import pallas as pl
from jax.experimental.pallas import tpu as pltpu
from jax.sharding import Mesh
from jax.sharding import PartitionSpec as P
import ml_dtypes

SEG = 4096
NMODE = 32
FKEEP = 128
RUN = 128
TROWS = 64
TCOLS = 128
RADIUS = 3
DETS = 32
CHUNK = 256
NCHUNK = SEG // CHUNK
WIDE = 1024
NRUNS = DETS * SEG // RUN
NT = 16
NY = 4
OWN = 8
BROWS = 16
NBLK = NY * NT
ZROWS = (TROWS // OWN + 1) * NT
BF = jnp.bfloat16
F32 = jnp.float32
I32 = jnp.int32
FIRST = 512
PART = 2 * NMODE + 8


def split_np(a):
    hi = a.astype(np.float32).astype(ml_dtypes.bfloat16)
    lo = (a - hi.astype(np.float64)).astype(np.float32).astype(ml_dtypes.bfloat16)
    return hi, lo


def tables():
    j = np.arange(CHUNK)[:, None]
    k = np.arange(FKEEP)[None, :]
    phi = 2.0 * np.pi * (j * k % SEG) / SEG
    basis = np.concatenate([np.cos(phi), np.sin(phi)], axis=1)
    c = np.arange(NCHUNK)[:, None]
    theta = 2.0 * np.pi * (c * CHUNK * k % SEG) / SEG
    twiddle = np.concatenate([np.cos(theta), np.sin(theta)], axis=1).astype(np.float32)
    scale = np.where(np.arange(FKEEP) == 0, 1.0 / SEG, 2.0 / SEG)
    phi = 2.0 * np.pi * (np.arange(WIDE)[:, None] * k % SEG) / SEG
    synth = np.concatenate([np.cos(phi), np.sin(phi)], axis=1).T
    synth = synth * np.concatenate([scale, scale])[:, None]
    return np.concatenate(split_np(basis)), np.concatenate(split_np(synth)), twiddle


def beam_taps():
    values = [math.exp(-(m * m) / 4.5) for m in range(-RADIUS, RADIUS + 1)]
    total = sum(values)
    return [v / total for v in values]


def split(a):
    hi = a.astype(BF)
    return hi, (a - hi.astype(F32)).astype(BF)


def mm(a, b):
    return jnp.dot(a, b, preferred_element_type=F32)


def mm0(a, b):
    return lax.dot_general(
        a, b, (((0,), (0,)), ((), ())), precision=lax.Precision.HIGHEST,
        preferred_element_type=F32,
    )


def mm0_split(a, b):
    ah, al = split(a)
    bh, bl = split(b)
    return lax.dot_general(
        jnp.concatenate([ah, al, ah], axis=0), jnp.concatenate([bh, bh, bl], axis=0),
        (((0,), (0,)), ((), ())), preferred_element_type=F32,
    )


def column(row, n):
    full = jnp.broadcast_to(row, (n, row.shape[1]))
    same = lax.broadcasted_iota(jnp.int32, full.shape, 0) == lax.broadcasted_iota(
        jnp.int32, full.shape, 1
    )
    return jnp.sum(jnp.where(same, full, 0.0), axis=1, keepdims=True)


def run_row(ids):
    flat = ids.astype(F32).T
    parts = [flat[c : c + 1, :] for c in range(SEG // RUN)]
    return jnp.concatenate(parts, axis=1).astype(jnp.int32)


def analysis_kernel(
    x_hbm, t_hbm, v_hbm, ti_hbm, ro_hbm, cs_hbm, basis_hbm, synth_hbm, tw_hbm,
    out_ref, x_ref, synth_ref, tw_ref, line_ref,
    t_ref, v_ref, ti_ref, ro_ref, cs_ref, basis_ref, sems,
):
    copies = [
        pltpu.make_async_copy(src, dst, sems.at[n])
        for n, (src, dst) in enumerate(
            [
                (v_hbm, v_ref), (t_hbm, t_ref), (x_hbm, x_ref), (basis_hbm, basis_ref),
                (ti_hbm, ti_ref), (ro_hbm, ro_ref), (cs_hbm, cs_ref),
                (tw_hbm, tw_ref), (synth_hbm, synth_ref),
            ]
        )
    ]
    for copy in copies:
        copy.start()
    copies[0].wait()
    copies[1].wait()
    copies[2].wait()
    copies[3].wait()
    copies[4].wait()
    copies[5].wait()
    copies[6].wait()
    copies[7].wait()
    w = column(v_ref[...].astype(F32), DETS)
    t = t_ref[...]
    wt = t * w
    eh = basis_ref[:CHUNK, :]
    el = basis_ref[CHUNK:, :]
    wide = jnp.broadcast_to(w, (DETS, CHUNK))
    x = jnp.concatenate(
        [wide * x_ref[:, c * CHUNK : (c + 1) * CHUNK] for c in range(NCHUNK)], axis=0
    )
    hi, lo = split(x)
    y = mm(hi, eh) + mm(lo, eh) + mm(hi, el)
    gram = mm0(wt, t)
    out_ref[2 * NMODE : PART, :] = jnp.concatenate(
        [gram[8 * i : 8 * i + 8, :] for i in range(NMODE // 8)], axis=1
    )
    line = ti_ref[...] * TROWS + ro_ref[...]
    line_ref[...] = run_row(line)
    out_ref[PART:, :] = jnp.concatenate(
        [t, line.astype(F32), cs_ref[...].astype(F32), jnp.broadcast_to(w, (DETS, 32))], axis=1
    )
    re = jnp.zeros((DETS, FKEEP), F32)
    im = jnp.zeros((DETS, FKEEP), F32)
    for c in range(NCHUNK):
        sl = slice(c * DETS, (c + 1) * DETS)
        yc = y[sl, :FKEEP]
        yi = y[sl, FKEEP:]
        cos = tw_ref[c : c + 1, :FKEEP]
        sin = tw_ref[c : c + 1, FKEEP:]
        re = re + (cos * yc - sin * yi)
        im = im + (sin * yc + cos * yi)
    both = mm0_split(wt, jnp.concatenate([re, im], axis=1))
    out_ref[:NMODE, :] = both[:, :FKEEP]
    out_ref[NMODE : 2 * NMODE, :] = both[:, FKEEP:]
    copies[8].wait()


def edge_col(lane):
    slot = lane >> 3
    return jnp.where(slot < 3, TCOLS - RADIUS + slot, slot - 3)


def ids_of_blocks(core):
    l = lax.broadcasted_iota(jnp.int32, (NBLK * BROWS, 128), 0)
    i = l & (BROWS - 1)
    b = l >> 4
    row = (b & (NY - 1)) * (2 * OWN) + core * OWN - RADIUS + i
    ok = (i < OWN + 2 * RADIUS) & (row >= 0) & (row < TROWS)
    return jnp.where(ok, (b >> 2) * TROWS + row, -1)


def fill_hot(ref, ids, line):
    for q in range(line.shape[1] // 128):
        sl = slice(q * 128, (q + 1) * 128)
        ref[:, sl] = jnp.where(ids == line[:, sl], 1.0, 0.0).astype(BF)


def first_index_kernel(core_ref, line_ref, hot_ref):
    fill_hot(hot_ref, ids_of_blocks(core_ref[0]), line_ref[:, :FIRST])


def shifted_tiles(z, by):
    zero = jnp.zeros((z.shape[0], 1, 128), F32)
    if by < 0:
        return jnp.concatenate([zero, z[:, :-1]], axis=1)
    return jnp.concatenate([z[:, 1:], zero], axis=1)


def second_index_kernel(
    core_ref, line_ref, mine_ref, other_ref, hot_ref, idx_ref, hits_ref, rhs_ref, w_ref
):
    core = core_ref[0]
    packs = (mine_ref[PART:, :], other_ref[PART:, :])
    lines = [pack[:, 32:64].astype(jnp.int32) for pack in packs]
    rows = (line_ref[...], run_row(lines[1]))
    line = jnp.concatenate(rows, axis=1)
    fill_hot(hot_ref, ids_of_blocks(core), line[:, FIRST:])
    zid = (((line & (TROWS - 1)) + RADIUS) >> 3) * NT + (line >> 6)
    zl = lax.broadcasted_iota(jnp.int32, (ZROWS, 2 * NRUNS), 0)
    zhot = jnp.where(zl == zid, 1.0, 0.0).astype(BF)
    lane = lax.broadcasted_iota(jnp.int32, (DETS, 128), 1)
    hparts = []
    for n, pack in enumerate(packs):
        w = jnp.broadcast_to(pack[:, 96:97], (DETS, 128))
        w_ref[n * DETS : (n + 1) * DETS, :] = w
        spot = ((lines[n] + RADIUS) & (OWN - 1)) + 48
        css = pack[:, 64:96].astype(jnp.int32)
        for c in range(SEG // RUN):
            sl = slice(n * NRUNS + c * DETS, n * NRUNS + (c + 1) * DETS)
            cs = jnp.broadcast_to(css[:, c : c + 1], (DETS, 128))
            idx_ref[sl, :] = (lane - cs) & (TCOLS - 1)
            here = jnp.broadcast_to(spot[:, c : c + 1], (DETS, 128)) == lane
            hparts.append(jnp.where(here, w, 0.0).astype(BF))
    z = mm(zhot, jnp.concatenate(hparts, axis=0)).reshape(ZROWS // NT, NT, 128)
    right = shifted_tiles(z, 1)
    right = jnp.concatenate([jnp.zeros(z.shape[:2] + (8,), F32), right[:, :, :-8]], axis=2)
    nd = TROWS // OWN
    for n, v in enumerate((shifted_tiles(z, -1) + right, z)):
        moved = jnp.concatenate([jnp.zeros((nd, NT, 64), F32), v[1:, :, :64]], axis=2)
        v = v[:nd] + moved
        for y in range(NY):
            hits_ref[pl.ds(n * NBLK + y, NT, stride=NY), :] = jnp.where(
                core == 1, v[2 * y + 1], v[2 * y]
            )
    zero = jnp.zeros((NMODE, 32), F32)
    rhs_ref[...] = jnp.concatenate(
        [zero, packs[0][:, :NMODE].T, packs[1][:, :NMODE].T, zero], axis=1
    )


def lanes_of(v, k):
    return jnp.broadcast_to(v[:, k : k + 1], (8, 128))


def solve(packed, rhs):
    n = NMODE
    groups = range(n // 8)
    full = jnp.concatenate(
        [packed] + [pltpu.roll(packed, 128 - n * i, 1) for i in groups[1:]], axis=0
    )
    row = lax.broadcasted_iota(jnp.int32, (n, 128), 0)
    lane = lax.broadcasted_iota(jnp.int32, (n, 128), 1)
    full = jnp.where(lane < n, full, rhs) + jnp.where(lane == row, 0.05, 0.0)
    diag = jnp.where(lane == row, full, 0.0)
    down = lax.rsqrt(jnp.sum(diag, axis=1, keepdims=True))
    along = jnp.sum(jnp.where(lane < n, diag, 1.0 / n), axis=0, keepdims=True)
    full = full * down * lax.rsqrt(along)
    a = [full[8 * i : 8 * i + 8, :] for i in groups]
    sub = lax.broadcasted_iota(jnp.int32, (8, 128), 0)
    for q in range(8):
        c = [[lanes_of(v, 8 * j + q) for v in a] for j in groups]
        p = [[c[j][i] for j in groups] for i in groups]
        i1 = 1.0 / (p[0][0] * p[1][1] - p[0][1] * p[0][1])
        e00, e01, e11 = p[1][1] * i1, -p[0][1] * i1, p[0][0] * i1
        w00 = e00 * p[0][2] + e01 * p[1][2]
        w01 = e00 * p[0][3] + e01 * p[1][3]
        w10 = e01 * p[0][2] + e11 * p[1][2]
        w11 = e01 * p[0][3] + e11 * p[1][3]
        s00 = p[2][2] - (p[0][2] * w00 + p[1][2] * w10)
        s01 = p[2][3] - (p[0][2] * w01 + p[1][2] * w11)
        s11 = p[3][3] - (p[0][3] * w01 + p[1][3] * w11)
        i2 = 1.0 / (s00 * s11 - s01 * s01)
        y0 = e00 * a[0] + e01 * a[1]
        y1 = e01 * a[0] + e11 * a[1]
        q2 = a[2] - (p[0][2] * y0 + p[1][2] * y1)
        q3 = a[3] - (p[0][3] * y0 + p[1][3] * y1)
        n2 = (s11 * q2 - s01 * q3) * i2
        n3 = (s00 * q3 - s01 * q2) * i2
        n0 = y0 - (w00 * n2 + w01 * n3)
        n1 = y1 - (w10 * n2 + w11 * n3)
        new = [jnp.broadcast_to(v[q : q + 1, :], (8, 128)) for v in (n0, n1, n2, n3)]
        a = [
            jnp.where(
                sub == q,
                new[i],
                a[i] - ((c[0][i] * new[0] + c[1][i] * new[1]) + (c[2][i] * new[2] + c[3][i] * new[3])),
            )
            for i in groups
        ]
    return jnp.concatenate(a, axis=0)[:, n : 3 * n] * down


def edge_rows(s):
    lane = lax.broadcasted_iota(jnp.int32, s.shape, 1)
    moved = jnp.take_along_axis(s, edge_col(lane & 63), axis=1, mode="promise_in_bounds")
    moved = moved.reshape(NBLK, 2, 8, 128)
    sub = lax.broadcasted_iota(jnp.int32, (NBLK, 8, 128), 1)
    lane = lax.broadcasted_iota(jnp.int32, (NBLK, 8, 128), 2)
    moved = jnp.where(lane < 64, moved[:, 0], moved[:, 1])
    here = ((lane & 7) == sub) & ((lane & 63) < 48)
    return jnp.sum(jnp.where(here, moved, 0.0), axis=1)


def clean_kernel(
    p_ref, q_ref, r_ref, s_ref, rhs_ref, w_ref, x_ref, other_ref, synth_ref, tw_ref,
    idx_ref, hits_ref, hot_ref, more_hot_ref,
    blocks_ref, out_hbm, clean_ref, sem,
):
    p = (p_ref[...] + q_ref[...]) + (r_ref[...] + s_ref[...])
    coef = solve(p[2 * NMODE :, :], rhs_ref[...])
    ab = mm0_split(coef, jnp.concatenate([p[:NMODE, :], p[NMODE : 2 * NMODE, :]], axis=1))
    a = ab[:, :FKEEP]
    b = ab[:, FKEEP:]
    parts = []
    for c in range(SEG // WIDE):
        at = c * WIDE // CHUNK
        cos = tw_ref[at : at + 1, :FKEEP]
        sin = tw_ref[at : at + 1, FKEEP:]
        parts.append(jnp.concatenate([a * cos + b * sin, b * cos - a * sin], axis=1))
    hi, lo = split(jnp.concatenate(parts, axis=0))
    sh = synth_ref[: 2 * FKEEP, :]
    low = mm(hi, sh) + mm(lo, sh) + mm(hi, synth_ref[2 * FKEEP :, :])
    runs = []
    for n, source in enumerate((x_ref, other_ref)):
        w = w_ref[n * DETS : (n + 1) * DETS, :]
        for r in range(SEG // RUN):
            at = 2 * DETS * (r * RUN // WIDE) + DETS * n
            col = r * RUN % WIDE
            part = w * (source[:, r * RUN : (r + 1) * RUN] - low[at : at + DETS, col : col + RUN])
            if n == 0:
                clean_ref[:, r * RUN : (r + 1) * RUN] = part
            runs.append(part)
    copy = pltpu.make_async_copy(clean_ref, out_hbm, sem)
    copy.start()
    run = jnp.concatenate(runs, axis=0)
    vals = jnp.concatenate(
        split(jnp.take_along_axis(run, idx_ref[...], axis=1, mode="promise_in_bounds")), axis=1
    )
    s = mm(hot_ref[...], vals[:FIRST]) + mm(more_hot_ref[...], vals[FIRST:])
    s = s[:, :128] + s[:, 128:]
    blocks_ref[...] = s
    edges = edge_rows(s)
    tile = lax.broadcasted_iota(jnp.int32, edges.shape, 0) >> 2
    slot = (lax.broadcasted_iota(jnp.int32, edges.shape, 1) & 63) >> 3
    zero = jnp.zeros((NY, 128), F32)
    left = jnp.where(tile == 0, 0.0, jnp.concatenate([zero, edges[:-NY]], axis=0))
    right = jnp.where(tile == NT - 1, 0.0, jnp.concatenate([edges[NY:], zero], axis=0))
    near = jnp.where(slot < RADIUS, left, right) + hits_ref[:NBLK, :]
    blocks_ref[pl.ds(14, NBLK, stride=BROWS), :] = near
    blocks_ref[pl.ds(15, NBLK, stride=BROWS), :] = hits_ref[NBLK:, :]
    copy.wait()


def beam_kernel(blocks_ref, out_ref):
    sums = [blocks_ref[b * BROWS : (b + 1) * BROWS, :] for b in range(4)]
    for b in range(4, NBLK):
        sums[b % 4] = sums[b % 4] + blocks_ref[b * BROWS : (b + 1) * BROWS, :]
    total = (sums[0] + sums[1]) + (sums[2] + sums[3])
    near = jnp.broadcast_to(total[14:15, :], (BROWS, 128))
    mine = jnp.broadcast_to(total[15:16, :], (BROWS, 128))
    i = lax.broadcasted_iota(jnp.int32, (BROWS, 128), 0)
    lane = lax.broadcasted_iota(jnp.int32, (BROWS, 128), 1)
    spot = jnp.where(i < OWN, i, 64 + i - OWN)

    def take(src, slot):
        return jnp.sum(jnp.where(lane == spot + 8 * slot, src, 0.0), axis=1, keepdims=True)

    left_hits = take(near, 6) + 1.0
    right_hits = take(near, 7) + 1.0
    hits = take(mine, 6) + 1.0
    valid = i < OWN + 2 * RADIUS
    binned = jnp.where(valid, total / hits, 0.0)
    left = [take(near, m) / left_hits for m in range(RADIUS)]
    right = [take(near, RADIUS + m) / right_hits for m in range(RADIUS)]
    taps = beam_taps()
    smooth = taps[RADIUS] * binned
    for m in range(1, RADIUS + 1):
        moved = pltpu.roll(binned, m, 1)
        for q in range(m):
            moved = jnp.where(lane == q, left[RADIUS - m + q], moved)
        smooth = smooth + taps[RADIUS - m] * moved
        moved = pltpu.roll(binned, TCOLS - m, 1)
        for q in range(m):
            moved = jnp.where(lane == TCOLS - m + q, right[q], moved)
        smooth = smooth + taps[RADIUS + m] * moved
    out = taps[0] * smooth[0:OWN, :]
    for m in range(1, 2 * RADIUS + 1):
        out = out + taps[m] * smooth[m : m + OWN, :]
    out_ref[...] = out


VMEM = pl.BlockSpec(memory_space=pltpu.VMEM)
SMEM = pl.BlockSpec(memory_space=pltpu.SMEM)
HBM = pl.BlockSpec(memory_space=pltpu.HBM)


def call(kernel, outs, specs, name, flops, *args, out_specs=None, scratch=()):
    args = [
        pltpu.with_memory_space_constraint(a, pltpu.HBM) if spec is HBM else a
        for a, spec in zip(args, specs)
    ]
    nbytes = sum(math.prod(s.shape) * 4 for s in outs) + sum(a.size * 4 for a in args)
    return pl.pallas_call(
        kernel,
        out_shape=outs,
        in_specs=specs,
        out_specs=out_specs or [VMEM] * len(outs),
        scratch_shapes=list(scratch),
        name=name,
        compiler_params=pltpu.CompilerParams(vmem_limit_bytes=40 << 20),
        cost_estimate=pl.CostEstimate(flops=flops, bytes_accessed=nbytes, transcendentals=0),
    )(*args)


def sds(shape, dtype=F32):
    return jax.ShapeDtypeStruct(shape, dtype)


def body(timestreams, templates, validity, tile_index, row_offset, col_start):
    basis, synth, tw = tables()
    core = lax.axis_index("core").reshape(1)
    small = (DETS, SEG // RUN)
    swap = [(0, 1), (1, 0)]
    mate_x = lax.ppermute(timestreams, "core", swap)
    part, x, synth, tw, line = call(
        analysis_kernel,
        [
            sds((PART + DETS, FKEEP)), sds((DETS, SEG)), sds((4 * FKEEP, WIDE), BF),
            sds((NCHUNK, 2 * FKEEP)), sds((1, NRUNS), I32),
        ],
        [HBM] * 9, "analysis", 400_000_000,
        timestreams, templates, validity.reshape(1, DETS), tile_index, row_offset, col_start,
        jnp.asarray(basis), jnp.asarray(synth), jnp.asarray(tw),
        scratch=[
            pltpu.VMEM((DETS, NMODE), F32), pltpu.VMEM((1, DETS), I32), pltpu.VMEM(small, I32),
            pltpu.VMEM(small, I32), pltpu.VMEM(small, I32),
            pltpu.VMEM((2 * CHUNK, 2 * FKEEP), BF), pltpu.SemaphoreType.DMA((9,)),
        ],
    )
    mate = lax.ppermute(part, "core", swap)
    (hot,) = call(
        first_index_kernel, [sds((NBLK * BROWS, FIRST), BF)], [SMEM, VMEM], "index1", 100_000_000, core, line
    )
    sums, hot, line = lax.optimization_barrier((part[:PART] + mate[:PART], hot, line))
    others = [lax.ppermute(sums, "y", [(k, k ^ m) for k in range(NY)]) for m in (3, 1, 2)]
    more_hot, idx, hits, rhs, w = call(
        second_index_kernel,
        [
            sds((NBLK * BROWS, 2 * NRUNS - FIRST), BF), sds((2 * NRUNS, 128), I32),
            sds((2 * NBLK, 128)),
            sds((NMODE, 128)), sds((2 * DETS, 128)),
        ],
        [SMEM] + [VMEM] * 3, "index2", 3_000_000_000,
        core, line, part, mate,
    )
    blocks, cleaned = call(
        clean_kernel,
        [sds((NBLK * BROWS, 128)), sds((DETS, SEG))],
        [VMEM] * 14, "clean", 2_000_000_000,
        sums, *others, rhs, w, x, mate_x, synth, tw, idx, hits, hot, more_hot,
        out_specs=[VMEM, HBM],
        scratch=[pltpu.VMEM((DETS, SEG), F32), pltpu.SemaphoreType.DMA],
    )
    blocks = lax.all_to_all(blocks, ("z", "x", "y"), 0, 0, tiled=True)
    (beamed,) = call(
        beam_kernel, [sds((OWN, TCOLS))], [VMEM], "beam", 1_000_000, blocks
    )
    return (cleaned, beamed)


def solution(mesh):
    fine = Mesh(mesh.devices.reshape(NY, 2, 4, 4), ("y", "core", "z", "x"))
    det, tm = ("y", "core"), ("z", "x")
    in_specs = (P(det, tm), P(det, None), P(det), P(det, tm), P(det, tm), P(det, tm))
    out_specs = (P(det, tm), P(det, tm))
    return jax.shard_map(body, mesh=fine, in_specs=in_specs, out_specs=out_specs, check_vma=False)
```

```python
import math

import jax
import jax.numpy as jnp
import numpy as np
from jax import lax
from jax.experimental import pallas as pl
from jax.experimental.pallas import tpu as pltpu
from jax.sharding import Mesh
from jax.sharding import PartitionSpec as P
import ml_dtypes

SEG = 4096
NMODE = 32
FKEEP = 128
RUN = 128
TROWS = 64
TCOLS = 128
RADIUS = 3
DETS = 32
CHUNK = 256
NCHUNK = SEG // CHUNK
WIDE = 1024
NRUNS = DETS * SEG // RUN
NT = 16
NY = 4
OWN = 8
BROWS = 16
NBLK = NY * NT
ZROWS = (TROWS // OWN + 1) * NT
BF = jnp.bfloat16
F32 = jnp.float32
I32 = jnp.int32
FIRST = 512
PART = 2 * NMODE + 8


def split_np(a):
    hi = a.astype(np.float32).astype(ml_dtypes.bfloat16)
    lo = (a - hi.astype(np.float64)).astype(np.float32).astype(ml_dtypes.bfloat16)
    return hi, lo


def tables():
    j = np.arange(CHUNK)[:, None]
    k = np.arange(FKEEP)[None, :]
    phi = 2.0 * np.pi * (j * k % SEG) / SEG
    basis = np.concatenate([np.cos(phi), np.sin(phi)], axis=1)
    c = np.arange(NCHUNK)[:, None]
    theta = 2.0 * np.pi * (c * CHUNK * k % SEG) / SEG
    twiddle = np.concatenate([np.cos(theta), np.sin(theta)], axis=1).astype(np.float32)
    scale = np.where(np.arange(FKEEP) == 0, 1.0 / SEG, 2.0 / SEG)
    phi = 2.0 * np.pi * (np.arange(WIDE)[:, None] * k % SEG) / SEG
    synth = np.concatenate([np.cos(phi), np.sin(phi)], axis=1).T
    synth = synth * np.concatenate([scale, scale])[:, None]
    return np.concatenate(split_np(basis)), np.concatenate(split_np(synth)), twiddle


def beam_taps():
    values = [math.exp(-(m * m) / 4.5) for m in range(-RADIUS, RADIUS + 1)]
    total = sum(values)
    return [v / total for v in values]


def split(a):
    hi = a.astype(BF)
    return hi, (a - hi.astype(F32)).astype(BF)


def mm(a, b):
    return jnp.dot(a, b, preferred_element_type=F32)


def mm0(a, b):
    return lax.dot_general(
        a, b, (((0,), (0,)), ((), ())), precision=lax.Precision.HIGHEST,
        preferred_element_type=F32,
    )


def mm0_split(a, b):
    ah, al = split(a)
    bh, bl = split(b)
    return lax.dot_general(
        jnp.concatenate([ah, al, ah], axis=0), jnp.concatenate([bh, bh, bl], axis=0),
        (((0,), (0,)), ((), ())), preferred_element_type=F32,
    )


def column(row, n):
    full = jnp.broadcast_to(row, (n, row.shape[1]))
    same = lax.broadcasted_iota(jnp.int32, full.shape, 0) == lax.broadcasted_iota(
        jnp.int32, full.shape, 1
    )
    return jnp.sum(jnp.where(same, full, 0.0), axis=1, keepdims=True)


def run_row(ids):
    flat = ids.astype(F32).T
    parts = [flat[c : c + 1, :] for c in range(SEG // RUN)]
    return jnp.concatenate(parts, axis=1).astype(jnp.int32)


def analysis_kernel(
    x_hbm, t_hbm, v_hbm, ti_hbm, ro_hbm, cs_hbm, basis_hbm, synth_hbm, tw_hbm,
    out_ref, x_ref, synth_ref, tw_ref, line_ref,
    t_ref, v_ref, ti_ref, ro_ref, cs_ref, basis_ref, sems,
):
    copies = [
        pltpu.make_async_copy(src, dst, sems.at[n])
        for n, (src, dst) in enumerate(
            [
                (v_hbm, v_ref), (t_hbm, t_ref), (x_hbm, x_ref), (basis_hbm, basis_ref),
                (ti_hbm, ti_ref), (ro_hbm, ro_ref), (cs_hbm, cs_ref),
                (tw_hbm, tw_ref), (synth_hbm, synth_ref),
            ]
        )
    ]
    for copy in copies:
        copy.start()
    copies[0].wait()
    copies[1].wait()
    copies[2].wait()
    copies[3].wait()
    copies[4].wait()
    copies[5].wait()
    copies[6].wait()
    copies[7].wait()
    w = column(v_ref[...].astype(F32), DETS)
    t = t_ref[...]
    wt = t * w
    eh = basis_ref[:CHUNK, :]
    el = basis_ref[CHUNK:, :]
    wide = jnp.broadcast_to(w, (DETS, CHUNK))
    x = jnp.concatenate(
        [wide * x_ref[:, c * CHUNK : (c + 1) * CHUNK] for c in range(NCHUNK)], axis=0
    )
    hi, lo = split(x)
    y = mm(hi, eh) + mm(lo, eh) + mm(hi, el)
    gram = mm0(wt, t)
    out_ref[2 * NMODE : PART, :] = jnp.concatenate(
        [gram[8 * i : 8 * i + 8, :] for i in range(NMODE // 8)], axis=1
    )
    line = ti_ref[...] * TROWS + ro_ref[...]
    line_ref[...] = run_row(line)
    out_ref[PART:, :] = jnp.concatenate(
        [t, line.astype(F32), cs_ref[...].astype(F32), jnp.broadcast_to(w, (DETS, 32))], axis=1
    )
    re = jnp.zeros((DETS, FKEEP), F32)
    im = jnp.zeros((DETS, FKEEP), F32)
    for c in range(NCHUNK):
        sl = slice(c * DETS, (c + 1) * DETS)
        yc = y[sl, :FKEEP]
        yi = y[sl, FKEEP:]
        cos = tw_ref[c : c + 1, :FKEEP]
        sin = tw_ref[c : c + 1, FKEEP:]
        re = re + (cos * yc - sin * yi)
        im = im + (sin * yc + cos * yi)
    both = mm0_split(wt, jnp.concatenate([re, im], axis=1))
    out_ref[:NMODE, :] = both[:, :FKEEP]
    out_ref[NMODE : 2 * NMODE, :] = both[:, FKEEP:]
    copies[8].wait()


def edge_col(lane):
    slot = lane >> 3
    return jnp.where(slot < 3, TCOLS - RADIUS + slot, slot - 3)


def ids_of_blocks(core):
    l = lax.broadcasted_iota(jnp.int32, (NBLK * BROWS, 128), 0)
    i = l & (BROWS - 1)
    b = l >> 4
    row = (b & (NY - 1)) * (2 * OWN) + core * OWN - RADIUS + i
    ok = (i < OWN + 2 * RADIUS) & (row >= 0) & (row < TROWS)
    return jnp.where(ok, (b >> 2) * TROWS + row, -1)


def fill_hot(ref, ids, line):
    for q in range(line.shape[1] // 128):
        sl = slice(q * 128, (q + 1) * 128)
        ref[:, sl] = jnp.where(ids == line[:, sl], 1.0, 0.0).astype(BF)


def first_index_kernel(core_ref, line_ref, hot_ref):
    fill_hot(hot_ref, ids_of_blocks(core_ref[0]), line_ref[:, :FIRST])


def shifted_tiles(z, by):
    zero = jnp.zeros((z.shape[0], 1, 128), F32)
    if by < 0:
        return jnp.concatenate([zero, z[:, :-1]], axis=1)
    return jnp.concatenate([z[:, 1:], zero], axis=1)


def second_index_kernel(
    core_ref, line_ref, mine_ref, other_ref, hot_ref, idx_ref, hits_ref, rhs_ref, w_ref
):
    core = core_ref[0]
    packs = (mine_ref[PART:, :], other_ref[PART:, :])
    lines = [pack[:, 32:64].astype(jnp.int32) for pack in packs]
    rows = (line_ref[...], run_row(lines[1]))
    line = jnp.concatenate(rows, axis=1)
    fill_hot(hot_ref, ids_of_blocks(core), line[:, FIRST:])
    zid = (((line & (TROWS - 1)) + RADIUS) >> 3) * NT + (line >> 6)
    zl = lax.broadcasted_iota(jnp.int32, (ZROWS, 2 * NRUNS), 0)
    zhot = jnp.where(zl == zid, 1.0, 0.0).astype(BF)
    lane = lax.broadcasted_iota(jnp.int32, (DETS, 128), 1)
    hparts = []
    for n, pack in enumerate(packs):
        w = jnp.broadcast_to(pack[:, 96:97], (DETS, 128))
        w_ref[n * DETS : (n + 1) * DETS, :] = w
        spot = ((lines[n] + RADIUS) & (OWN - 1)) + 48
        css = pack[:, 64:96].astype(jnp.int32)
        for c in range(SEG // RUN):
            sl = slice(n * NRUNS + c * DETS, n * NRUNS + (c + 1) * DETS)
            cs = jnp.broadcast_to(css[:, c : c + 1], (DETS, 128))
            idx_ref[sl, :] = (lane - cs) & (TCOLS - 1)
            here = jnp.broadcast_to(spot[:, c : c + 1], (DETS, 128)) == lane
            hparts.append(jnp.where(here, w, 0.0).astype(BF))
    z = mm(zhot, jnp.concatenate(hparts, axis=0)).reshape(ZROWS // NT, NT, 128)
    right = shifted_tiles(z, 1)
    right = jnp.concatenate([jnp.zeros(z.shape[:2] + (8,), F32), right[:, :, :-8]], axis=2)
    nd = TROWS // OWN
    for n, v in enumerate((shifted_tiles(z, -1) + right, z)):
        moved = jnp.concatenate([jnp.zeros((nd, NT, 64), F32), v[1:, :, :64]], axis=2)
        v = v[:nd] + moved
        for y in range(NY):
            hits_ref[pl.ds(n * NBLK + y, NT, stride=NY), :] = jnp.where(
                core == 1, v[2 * y + 1], v[2 * y]
            )
    zero = jnp.zeros((NMODE, 32), F32)
    rhs_ref[...] = jnp.concatenate(
        [zero, packs[0][:, :NMODE].T, packs[1][:, :NMODE].T, zero], axis=1
    )


def lanes_of(v, k):
    return jnp.broadcast_to(v[:, k : k + 1], (8, 128))


def solve(packed, rhs):
    n = NMODE
    groups = range(n // 8)
    full = jnp.concatenate(
        [packed] + [pltpu.roll(packed, 128 - n * i, 1) for i in groups[1:]], axis=0
    )
    row = lax.broadcasted_iota(jnp.int32, (n, 128), 0)
    lane = lax.broadcasted_iota(jnp.int32, (n, 128), 1)
    full = jnp.where(lane < n, full, rhs) + jnp.where(lane == row, 0.05, 0.0)
    diag = jnp.where(lane == row, full, 0.0)
    down = lax.rsqrt(jnp.sum(diag, axis=1, keepdims=True))
    along = jnp.sum(jnp.where(lane < n, diag, 1.0 / n), axis=0, keepdims=True)
    full = full * down * lax.rsqrt(along)
    a = [full[8 * i : 8 * i + 8, :] for i in groups]
    sub = lax.broadcasted_iota(jnp.int32, (8, 128), 0)
    for q in range(8):
        c = [[lanes_of(v, 8 * j + q) for v in a] for j in groups]
        p = [[c[j][i] for j in groups] for i in groups]
        i1 = 1.0 / (p[0][0] * p[1][1] - p[0][1] * p[0][1])
        e00, e01, e11 = p[1][1] * i1, -p[0][1] * i1, p[0][0] * i1
        w00 = e00 * p[0][2] + e01 * p[1][2]
        w01 = e00 * p[0][3] + e01 * p[1][3]
        w10 = e01 * p[0][2] + e11 * p[1][2]
        w11 = e01 * p[0][3] + e11 * p[1][3]
        s00 = p[2][2] - (p[0][2] * w00 + p[1][2] * w10)
        s01 = p[2][3] - (p[0][2] * w01 + p[1][2] * w11)
        s11 = p[3][3] - (p[0][3] * w01 + p[1][3] * w11)
        i2 = 1.0 / (s00 * s11 - s01 * s01)
        y0 = e00 * a[0] + e01 * a[1]
        y1 = e01 * a[0] + e11 * a[1]
        q2 = a[2] - (p[0][2] * y0 + p[1][2] * y1)
        q3 = a[3] - (p[0][3] * y0 + p[1][3] * y1)
        n2 = (s11 * q2 - s01 * q3) * i2
        n3 = (s00 * q3 - s01 * q2) * i2
        n0 = y0 - (w00 * n2 + w01 * n3)
        n1 = y1 - (w10 * n2 + w11 * n3)
        new = [jnp.broadcast_to(v[q : q + 1, :], (8, 128)) for v in (n0, n1, n2, n3)]
        a = [
            jnp.where(
                sub == q,
                new[i],
                a[i] - ((c[0][i] * new[0] + c[1][i] * new[1]) + (c[2][i] * new[2] + c[3][i] * new[3])),
            )
            for i in groups
        ]
    return jnp.concatenate(a, axis=0)[:, n : 3 * n] * down


def edge_rows(s):
    lane = lax.broadcasted_iota(jnp.int32, s.shape, 1)
    moved = jnp.take_along_axis(s, edge_col(lane & 63), axis=1, mode="promise_in_bounds")
    moved = moved.reshape(NBLK, 2, 8, 128)
    sub = lax.broadcasted_iota(jnp.int32, (NBLK, 8, 128), 1)
    lane = lax.broadcasted_iota(jnp.int32, (NBLK, 8, 128), 2)
    moved = jnp.where(lane < 64, moved[:, 0], moved[:, 1])
    here = ((lane & 7) == sub) & ((lane & 63) < 48)
    return jnp.sum(jnp.where(here, moved, 0.0), axis=1)


def clean_kernel(
    p_ref, q_ref, r_ref, s_ref, rhs_ref, w_ref, x_ref, other_ref, synth_ref, tw_ref,
    idx_ref, hits_ref, hot_ref, more_hot_ref,
    blocks_ref, out_hbm, clean_ref, sem,
):
    p = (p_ref[...] + q_ref[...]) + (r_ref[...] + s_ref[...])
    coef = solve(p[2 * NMODE :, :], rhs_ref[...])
    ab = mm0_split(coef, jnp.concatenate([p[:NMODE, :], p[NMODE : 2 * NMODE, :]], axis=1))
    a = ab[:, :FKEEP]
    b = ab[:, FKEEP:]
    parts = []
    for c in range(SEG // WIDE):
        at = c * WIDE // CHUNK
        cos = tw_ref[at : at + 1, :FKEEP]
        sin = tw_ref[at : at + 1, FKEEP:]
        parts.append(jnp.concatenate([a * cos + b * sin, b * cos - a * sin], axis=1))
    hi, lo = split(jnp.concatenate(parts, axis=0))
    sh = synth_ref[: 2 * FKEEP, :]
    low = mm(hi, sh) + mm(lo, sh) + mm(hi, synth_ref[2 * FKEEP :, :])
    runs = []
    for n, source in enumerate((x_ref, other_ref)):
        w = w_ref[n * DETS : (n + 1) * DETS, :]
        for r in range(SEG // RUN):
            at = 2 * DETS * (r * RUN // WIDE) + DETS * n
            col = r * RUN % WIDE
            part = w * (source[:, r * RUN : (r + 1) * RUN] - low[at : at + DETS, col : col + RUN])
            if n == 0:
                clean_ref[:, r * RUN : (r + 1) * RUN] = part
            runs.append(part)
    copy = pltpu.make_async_copy(clean_ref, out_hbm, sem)
    copy.start()
    run = jnp.concatenate(runs, axis=0)
    vals = jnp.concatenate(
        split(jnp.take_along_axis(run, idx_ref[...], axis=1, mode="promise_in_bounds")), axis=1
    )
    s = mm(hot_ref[...], vals[:FIRST]) + mm(more_hot_ref[...], vals[FIRST:])
    s = s[:, :128] + s[:, 128:]
    blocks_ref[...] = s
    edges = edge_rows(s)
    tile = lax.broadcasted_iota(jnp.int32, edges.shape, 0) >> 2
    slot = (lax.broadcasted_iota(jnp.int32, edges.shape, 1) & 63) >> 3
    zero = jnp.zeros((NY, 128), F32)
    left = jnp.where(tile == 0, 0.0, jnp.concatenate([zero, edges[:-NY]], axis=0))
    right = jnp.where(tile == NT - 1, 0.0, jnp.concatenate([edges[NY:], zero], axis=0))
    near = jnp.where(slot < RADIUS, left, right) + hits_ref[:NBLK, :]
    blocks_ref[pl.ds(14, NBLK, stride=BROWS), :] = near
    blocks_ref[pl.ds(15, NBLK, stride=BROWS), :] = hits_ref[NBLK:, :]
    copy.wait()


def beam_kernel(blocks_ref, out_ref):
    sums = [blocks_ref[b * BROWS : (b + 1) * BROWS, :] for b in range(4)]
    for b in range(4, NBLK):
        sums[b % 4] = sums[b % 4] + blocks_ref[b * BROWS : (b + 1) * BROWS, :]
    total = (sums[0] + sums[1]) + (sums[2] + sums[3])
    near = jnp.broadcast_to(total[14:15, :], (BROWS, 128))
    mine = jnp.broadcast_to(total[15:16, :], (BROWS, 128))
    i = lax.broadcasted_iota(jnp.int32, (BROWS, 128), 0)
    lane = lax.broadcasted_iota(jnp.int32, (BROWS, 128), 1)
    spot = jnp.where(i < OWN, i, 64 + i - OWN)

    def take(src, slot):
        return jnp.sum(jnp.where(lane == spot + 8 * slot, src, 0.0), axis=1, keepdims=True)

    left_hits = take(near, 6) + 1.0
    right_hits = take(near, 7) + 1.0
    hits = take(mine, 6) + 1.0
    valid = i < OWN + 2 * RADIUS
    binned = jnp.where(valid, total / hits, 0.0)
    left = [take(near, m) / left_hits for m in range(RADIUS)]
    right = [take(near, RADIUS + m) / right_hits for m in range(RADIUS)]
    taps = beam_taps()
    smooth = taps[RADIUS] * binned
    for m in range(1, RADIUS + 1):
        moved = pltpu.roll(binned, m, 1)
        for q in range(m):
            moved = jnp.where(lane == q, left[RADIUS - m + q], moved)
        smooth = smooth + taps[RADIUS - m] * moved
        moved = pltpu.roll(binned, TCOLS - m, 1)
        for q in range(m):
            moved = jnp.where(lane == TCOLS - m + q, right[q], moved)
        smooth = smooth + taps[RADIUS + m] * moved
    out = taps[0] * smooth[0:OWN, :]
    for m in range(1, 2 * RADIUS + 1):
        out = out + taps[m] * smooth[m : m + OWN, :]
    out_ref[...] = out


VMEM = pl.BlockSpec(memory_space=pltpu.VMEM)
SMEM = pl.BlockSpec(memory_space=pltpu.SMEM)
HBM = pl.BlockSpec(memory_space=pltpu.HBM)


def call(kernel, outs, specs, name, flops, *args, out_specs=None, scratch=()):
    args = [
        pltpu.with_memory_space_constraint(a, pltpu.HBM) if spec is HBM else a
        for a, spec in zip(args, specs)
    ]
    nbytes = sum(math.prod(s.shape) * 4 for s in outs) + sum(a.size * 4 for a in args)
    return pl.pallas_call(
        kernel,
        out_shape=outs,
        in_specs=specs,
        out_specs=out_specs or [VMEM] * len(outs),
        scratch_shapes=list(scratch),
        name=name,
        compiler_params=pltpu.CompilerParams(vmem_limit_bytes=40 << 20),
        cost_estimate=pl.CostEstimate(flops=flops, bytes_accessed=nbytes, transcendentals=0),
    )(*args)


def sds(shape, dtype=F32):
    return jax.ShapeDtypeStruct(shape, dtype)


def body(timestreams, templates, validity, tile_index, row_offset, col_start):
    basis, synth, tw = tables()
    core = lax.axis_index("core").reshape(1)
    small = (DETS, SEG // RUN)
    swap = [(0, 1), (1, 0)]
    mate_x = lax.ppermute(timestreams, "core", swap)
    part, x, synth, tw, line = call(
        analysis_kernel,
        [
            sds((PART + DETS, FKEEP)), sds((DETS, SEG)), sds((4 * FKEEP, WIDE), BF),
            sds((NCHUNK, 2 * FKEEP)), sds((1, NRUNS), I32),
        ],
        [HBM] * 9, "analysis", 400_000_000,
        timestreams, templates, validity.reshape(1, DETS), tile_index, row_offset, col_start,
        jnp.asarray(basis), jnp.asarray(synth), jnp.asarray(tw),
        scratch=[
            pltpu.VMEM((DETS, NMODE), F32), pltpu.VMEM((1, DETS), I32), pltpu.VMEM(small, I32),
            pltpu.VMEM(small, I32), pltpu.VMEM(small, I32),
            pltpu.VMEM((2 * CHUNK, 2 * FKEEP), BF), pltpu.SemaphoreType.DMA((9,)),
        ],
    )
    mate = lax.ppermute(part, "core", swap)
    (hot,) = call(
        first_index_kernel, [sds((NBLK * BROWS, FIRST), BF)], [SMEM, VMEM], "index1", 100_000_000, core, line
    )
    sums, hot, line = lax.optimization_barrier((part[:PART] + mate[:PART], hot, line))
    others = [lax.ppermute(sums, "y", [(k, k ^ m) for k in range(NY)]) for m in (2, 3, 1)]
    more_hot, idx, hits, rhs, w = call(
        second_index_kernel,
        [
            sds((NBLK * BROWS, 2 * NRUNS - FIRST), BF), sds((2 * NRUNS, 128), I32),
            sds((2 * NBLK, 128)),
            sds((NMODE, 128)), sds((2 * DETS, 128)),
        ],
        [SMEM] + [VMEM] * 3, "index2", 3_000_000_000,
        core, line, part, mate,
    )
    blocks, cleaned = call(
        clean_kernel,
        [sds((NBLK * BROWS, 128)), sds((DETS, SEG))],
        [VMEM] * 14, "clean", 2_000_000_000,
        sums, *others, rhs, w, x, mate_x, synth, tw, idx, hits, hot, more_hot,
        out_specs=[VMEM, HBM],
        scratch=[pltpu.VMEM((DETS, SEG), F32), pltpu.SemaphoreType.DMA],
    )
    blocks = lax.all_to_all(blocks, ("z", "x", "y"), 0, 0, tiled=True)
    (beamed,) = call(
        beam_kernel, [sds((OWN, TCOLS))], [VMEM], "beam", 1_000_000, blocks
    )
    return (cleaned, beamed)


def solution(mesh):
    fine = Mesh(mesh.devices.reshape(NY, 2, 4, 4), ("y", "core", "z", "x"))
    det, tm = ("y", "core"), ("z", "x")
    in_specs = (P(det, tm), P(det, None), P(det), P(det, tm), P(det, tm), P(det, tm))
    out_specs = (P(det, tm), P(det, tm))
    return jax.shard_map(body, mesh=fine, in_specs=in_specs, out_specs=out_specs, check_vma=False)
```
